32 devices in a mesh: member: 2 (over y), tile: 4 (over z), chan: 2 (over x), sub: 2 (over core).
Axes of the slice: x: 2, y: 2, z: 4, core: 2. Of those that a mesh axis runs over, the one named last changes fastest.
Arguments:
- obs_values: bfloat16 [131072, 64], P(('member', 'tile', 'chan', 'sub')), parts along dimension 0, may hold values from -6 to 6
- obs_weight: bfloat16 [131072], P(('member', 'tile', 'chan', 'sub')), parts along dimension 0, may hold values from 0.25 to 4
- obs_tile: int32 [131072], P(('member', 'tile', 'chan', 'sub')), parts along dimension 0, may hold values from 0 to 7, as said below
- obs_cell: int32 [131072], P(('member', 'tile', 'chan', 'sub')), parts along dimension 0, may hold values from 0 to 3071
- conv_one: bfloat16 [3, 3, 256, 64], P(None, None, 'chan'), may hold values from -0.25 to 0.25
- conv_two: bfloat16 [3, 3, 256, 256], P(None, None, 'chan'), may hold values from -0.125 to 0.125
- density_gain: float32 [256], P('chan'), may hold values from -2 to 2
- cotangent: bfloat16 [512, 32, 768], P(('member', 'chan'), 'tile', 'sub'), parts along dimension 0, may hold values from -6 to 6
Outputs:
- encoded: bfloat16 [512, 32, 768], P(('member', 'chan'), 'tile', 'sub'), parts along dimension 0
- grad_conv_one: float32 [6, 3, 256, 64], P('member', None, 'chan'), parts along dimension 0
- grad_conv_two: float32 [6, 3, 256, 256], P('member', None, 'chan'), parts along dimension 0
- grad_gain: float32 [512], P(('member', 'chan')), parts along dimension 0
The draws below stay inside these ranges and needn't reach their ends.
There are 2 independent parts, one for each index of `member`. The reference program is written for one: setup_inputs(seed, part) draws one part's arguments, and reference() takes and returns one part's arrays. A program takes and returns all parts, laid end to end along the dimension named above; an argument that names none is the same for every part. Nothing has to cross between parts.
Inputs may be any that keep to these rules, and one draw needn't show every extreme that they name: `obs_tile`: among the rows of one device no tile is named by more than 1024 rows, and one tile, the same for every device of a member, is named by exactly 1024 of them.
All inputs are finite; a program needn't handle non-finite values.
Results may differ from the reference program's by a relative error of at most 0.0055.
Values may be sent and summed in bfloat16 or wider, within the bound.
No kernel may reach another device: no remote copies, remote signals or barrier semaphores. Data moves between devices by JAX's collectives and lax.ppermute only.
A program may use at most 64 MiB of HBM per device.

```python
import math
import jax
import jax.numpy as jnp
from jax import lax

OC = 64
CH = 256
H_DEV = 8
W_DEV = 384
OBS_DEV = 4096
TILES = 8
SENDERS = 16
OBS = 65536
CAP = 1024
NH = 32
NW = 768
N_TILE = 4
N_SUB = 2


def draw_obs_tile(key, part):
    hot_tile = jax.random.randint(jax.random.fold_in(key, SENDERS + 5), (), 0, TILES).astype(jnp.int32)

    def block_dest(block):
        block_key = jax.random.fold_in(key, block)
        offset = jax.random.randint(jax.random.fold_in(block_key, 1), (), 0, TILES - 1).astype(jnp.int32)
        spread = jnp.arange(OBS_DEV - CAP, dtype=jnp.int32)
        others = (hot_tile + 1 + (spread + offset) % (TILES - 1)) % TILES
        dest_rows = jnp.concatenate([jnp.full((CAP,), 1, jnp.int32) * hot_tile, others])
        order = jax.random.permutation(jax.random.fold_in(block_key, 2), OBS_DEV)
        return dest_rows[order]
    return jax.vmap(block_dest)(jnp.arange(SENDERS, dtype=jnp.int32)).reshape(-1).astype(jnp.int32)


def touch_ends(values, rng, smallest, largest):
    spot = [jax.random.randint(jax.random.fold_in(rng, axis), (), 0, length) for axis, length in enumerate(values.shape)]
    widest = values.shape.index(max(values.shape))
    neighbour = spot[:widest] + [(spot[widest] + 1) % values.shape[widest]] + spot[widest + 1:]
    return values.at[tuple(spot)].set(smallest).at[tuple(neighbour)].set(largest)


def block_scale(stream_key, shape, cuts, smallest, high):
    def one(dim, blocks):
        steps = jax.random.uniform(jax.random.fold_in(jax.random.fold_in(stream_key, 6), dim), (blocks,), jnp.float32, smallest / len(cuts), high / len(cuts))
        return jnp.repeat(jnp.exp(steps), shape[dim] // blocks).reshape((-1,) + (1,) * (len(shape) - dim - 1))

    loudness = one(*cuts[0])
    for cut in cuts[1:]:
        loudness = loudness * one(*cut)
    return loudness


def centred(own_key, extent, deviation, reach, cuts=(), kind=jnp.bfloat16):
    values = jax.random.normal(own_key, extent, jnp.float32) * deviation
    if len(cuts) > 0:
        values = block_scale(own_key, extent, cuts, -0.22, 0.18) * values
    return jnp.clip(values, min=-reach, max=reach).astype(kind)


def setup_inputs(seed: int = 0, part: int = 0) -> dict:
    splits = jax.random.split(jax.random.key(seed), 9)
    own_keys = jax.random.split(jax.random.fold_in(splits[8], part), 9)
    return {
        "obs_values": centred(own_keys[0], (OBS, OC), 1.0, 6.0, ((0, 16),)),
        "obs_weight": jnp.clip(jnp.exp(math.log(4.0) - 2.7725887 * jax.random.uniform(own_keys[1], (OBS,), jnp.float32) ** block_scale(own_keys[1], (OBS,), ((0, 16),), -0.2, 0.2)), 0.25, 4.0).astype(jnp.bfloat16),
        "obs_tile": draw_obs_tile(jax.random.fold_in(jax.random.fold_in(splits[8], part), 71), part),
        "obs_cell": touch_ends(jax.random.randint(own_keys[3], (OBS,), 0, H_DEV * W_DEV), jax.random.fold_in(own_keys[3], 1), 0, (H_DEV * W_DEV) - 1).astype(jnp.int32),
        "conv_one": centred(splits[4], (3, 3, CH, OC), (9 * OC) ** -0.5, 0.25, ((2, 2),)),
        "conv_two": centred(splits[5], (3, 3, CH, CH), (9 * CH) ** -0.5, 0.125, ((2, 2),)),
        "density_gain": centred(splits[6], (CH,), 0.3, 2.0, ((0, 2),), jnp.float32),
        "cotangent": centred(own_keys[7], (CH, NH, NW), 1.0, 6.0, ((0, 2), (1, 4), (2, 2))),
    }


def conv_full(field, kernel):
    return lax.conv_general_dilated(field[None], kernel, (1, 1), ((1, 1), (1, 1)), dimension_numbers=('NCHW', 'HWOI', 'NCHW'), precision=lax.Precision.HIGHEST)[0]

def reference(obs_values, obs_weight, obs_tile, obs_cell, conv_one, conv_two, density_gain, cotangent):
    n_rows = H_DEV * N_TILE
    n_cols = W_DEV * N_SUB
    grid_row = obs_tile // N_SUB * H_DEV + obs_cell // W_DEV
    grid_col = obs_tile % N_SUB * W_DEV + obs_cell % W_DEV
    place = (grid_row * n_cols + grid_col).astype(jnp.int32)
    weight_f = obs_weight.astype(jnp.float32)
    data = jax.ops.segment_sum(obs_values.astype(jnp.float32) * weight_f[:, None], place, num_segments=n_rows * n_cols)
    density = jax.ops.segment_sum(weight_f, place, num_segments=n_rows * n_cols).reshape(n_rows, n_cols)
    features = (data.T.reshape(OC, n_rows, n_cols) / (1.0 + density)[None]).astype(jnp.bfloat16)
    log_density = jnp.log1p(density)
    feats_f = features.astype(jnp.float32)
    one_f = conv_one.astype(jnp.float32)
    two_f = conv_two.astype(jnp.float32)
    pre_one = conv_full(feats_f, one_f) + density_gain[:, None, None] * log_density[None]
    hidden = jax.nn.silu(pre_one).astype(jnp.bfloat16)
    encoded_f, pull_two = jax.vjp(conv_full, hidden.astype(jnp.float32), two_f)
    grad_hidden, grad_two = pull_two(cotangent.astype(jnp.float32))
    sigma = jax.nn.sigmoid(pre_one)
    grad_pre = (grad_hidden * sigma * (1.0 + pre_one * (1.0 - sigma))).astype(jnp.bfloat16)
    grad_pre_f = grad_pre.astype(jnp.float32)
    unused_out, pull_one = jax.vjp(lambda kernel: conv_full(feats_f, kernel), one_f)
    grad_one = pull_one(grad_pre_f)[0]
    grad_gain = lax.optimization_barrier(jnp.sum(grad_pre_f * log_density[None], axis=(1, 2)))
    scale_factor = 1.0 / math.sqrt(n_rows * n_cols)
    return (encoded_f.astype(jnp.bfloat16), grad_one * scale_factor, grad_two * scale_factor, grad_gain * scale_factor)
```

```python
import functools
import math

import jax
import jax.numpy as jnp
from jax import lax
from jax.experimental import pallas as pl
from jax.experimental.pallas import tpu as pltpu
from jax.sharding import PartitionSpec as P

BF16 = jnp.bfloat16
F32 = jnp.float32
LANES = 128
BLOCK = 256
META = 8
VMEM_BYTES = 56 * 1024 * 1024


def dot_nt(a, b):
    return lax.dot_general(a, b, (((1,), (1,)), ((), ())), preferred_element_type=F32)


def dot_nn(a, b):
    return lax.dot_general(a, b, (((1,), (0,)), ((), ())), preferred_element_type=F32)


def iota(shape, dim, dtype=jnp.int32):
    return lax.broadcasted_iota(jnp.int32, shape, dim).astype(dtype)


def vmem_spec():
    return pl.BlockSpec(memory_space=pltpu.VMEM)


def smem_spec():
    return pl.BlockSpec(memory_space=pltpu.SMEM)


def call(kernel, out_shape, in_specs, scratch, flops, moved, name):
    n_out = len(out_shape) if isinstance(out_shape, (tuple, list)) else None
    out_specs = vmem_spec() if n_out is None else [vmem_spec() for _ in range(n_out)]
    return pl.pallas_call(
        kernel,
        out_shape=out_shape,
        in_specs=in_specs,
        out_specs=out_specs,
        scratch_shapes=scratch,
        compiler_params=pltpu.CompilerParams(vmem_limit_bytes=VMEM_BYTES),
        cost_estimate=pl.CostEstimate(flops=flops, bytes_accessed=moved, transcendentals=0),
        name=name,
    )


def route_kernel(
    n_tiles, cap, tile_ref, weight_ref, cell_ref, values_ref, out_ref,
    onehot_ref, slot_ref, info_ref, info_smem, sem,
):
    n_blocks = tile_ref.shape[0]
    n_obs_chans = values_ref.shape[1]
    pairs = n_tiles * n_blocks
    tiles = tile_ref[...]
    for t in range(n_tiles):
        onehot_ref[t * n_blocks : (t + 1) * n_blocks, :] = jnp.where(tiles == t, 1.0, 0.0).astype(BF16)
    onehot = onehot_ref[...]
    upper = jnp.where(
        iota((BLOCK, BLOCK), 0) <= iota((BLOCK, BLOCK), 1), 1.0, 0.0
    ).astype(BF16)
    cum = dot_nn(onehot, upper)
    totals = dot_nn(onehot, jnp.ones((BLOCK, BLOCK), BF16))
    here = iota((pairs, pairs), 0)
    there = iota((pairs, pairs), 1)
    earlier = jnp.where(
        (here // n_blocks == there // n_blocks) & (there < here), 1.0, 0.0
    ).astype(BF16)
    offset = dot_nn(earlier, totals.astype(BF16))
    place = cum + offset - 1.0
    slots = jnp.zeros(tiles.shape, F32)
    for t in range(n_tiles):
        slots = jnp.where(tiles == t, place[t * n_blocks : (t + 1) * n_blocks, :], slots)
    slot_ref[...] = slots
    total_row = dot_nt(jnp.ones((8, BLOCK), BF16), onehot)
    offset_row = dot_nt(total_row.astype(BF16), earlier)
    base_row = jnp.minimum(jnp.floor(offset_row * (1.0 / LANES)) * LANES, float(cap - BLOCK))
    spill = jnp.where(offset_row + total_row > base_row + BLOCK, 1.0, 0.0)
    any_spill = jnp.max(spill, axis=1, keepdims=True)
    info_ref[...] = jnp.where(
        iota((8, pairs), 0) == 0, base_row, any_spill
    ).astype(jnp.int32)
    copy = pltpu.make_async_copy(info_ref, info_smem, sem)
    copy.start()
    out_ref[...] = jnp.zeros(out_ref.shape, BF16)
    eye = jnp.where(
        iota((n_obs_chans, n_obs_chans), 0) == iota((n_obs_chans, n_obs_chans), 1), 1.0, 0.0
    ).astype(BF16)
    meta_row = iota((16, BLOCK), 0)
    window = iota((BLOCK, BLOCK), 0, F32)
    copy.wait()

    def columns(b):
        rows = values_ref[pl.ds(pl.multiple_of(b * BLOCK, BLOCK), BLOCK), :]
        turned = dot_nt(eye, rows).astype(BF16)
        cell = cell_ref[pl.ds(b, 1), :]
        weight = weight_ref[pl.ds(b, 1), :]
        high = (cell // LANES).astype(F32)
        low = (cell % LANES).astype(F32)
        meta = jnp.where(
            meta_row == 0,
            weight,
            jnp.where(meta_row == 1, high, jnp.where(meta_row == 2, low, 0.0)),
        ).astype(BF16)
        return jnp.concatenate([turned, meta], axis=0)

    def add(t, base, wide, key):
        chosen = jnp.where(window == key, 1.0, 0.0).astype(BF16)
        part = dot_nt(wide, chosen)[: n_obs_chans + META].astype(BF16)
        where = pl.ds(pl.multiple_of(base, LANES), BLOCK)
        out_ref[t, :, where] = out_ref[t, :, where] + part

    def first(b, carry):
        wide = columns(b)
        tile = tile_ref[pl.ds(b, 1), :]
        slot = slot_ref[pl.ds(b, 1), :]
        for t in range(n_tiles):
            base = info_smem[0, t * n_blocks + b]
            key = jnp.where(tile == t, slot - base.astype(F32), -1.0)
            add(t, base, wide, key)
        return carry

    lax.fori_loop(0, n_blocks, first, 0)

    if cap > BLOCK:

        @pl.when(info_smem[1, 0] > 0)
        def _():
            def second(b, carry):
                wide = columns(b)
                tile = tile_ref[pl.ds(b, 1), :]
                slot = slot_ref[pl.ds(b, 1), :]
                for t in range(n_tiles):
                    start = info_smem[0, t * n_blocks + b]
                    base = jnp.minimum(start + BLOCK, cap - BLOCK)
                    far = (tile == t) & (slot >= (start + BLOCK).astype(F32))
                    key = jnp.where(far, slot - base.astype(F32), -1.0)
                    add(t, base, wide, key)
                return carry

            lax.fori_loop(0, n_blocks, second, 0)


def route(obs_values, obs_weight, obs_tile, obs_cell, n_tiles, cap):
    n_obs, chans = obs_values.shape
    n_blocks = n_obs // BLOCK
    rows = chans + META
    return call(
        functools.partial(route_kernel, n_tiles, cap),
        jax.ShapeDtypeStruct((n_tiles, rows, cap), BF16),
        [vmem_spec()] * 4,
        [
            pltpu.VMEM((n_tiles * n_blocks, BLOCK), BF16),
            pltpu.VMEM((n_blocks, BLOCK), F32),
            pltpu.VMEM((8, n_tiles * n_blocks), jnp.int32),
            pltpu.SMEM((8, n_tiles * n_blocks), jnp.int32),
            pltpu.SemaphoreType.DMA,
        ],
        2 * n_obs * n_tiles * BLOCK * 80,
        n_tiles * rows * cap * 2,
        "route",
    )(
        obs_tile.reshape(n_blocks, BLOCK),
        obs_weight.astype(F32).reshape(n_blocks, BLOCK),
        obs_cell.reshape(n_blocks, BLOCK),
        obs_values,
    )


def grid_kernel(n_rows, n_cols, got_ref, own_ref, send_ref, left_ref):
    n_send, rows, cap = got_ref.shape
    chans = rows - META
    per_row = n_cols // LANES
    data_rows = n_rows * chans
    own_ref[...] = jnp.zeros(own_ref.shape, F32)
    columns = iota((n_cols, cap), 0, F32)
    row_ids = iota((n_rows, cap), 0, F32)

    def one(s, carry):
        values = got_ref[s, 0:chans, :]
        meta = got_ref[s, chans:rows, :].astype(F32)
        weight = meta[0:1]
        high = meta[1:2]
        row = jnp.floor((high + 0.5) * (1.0 / per_row))
        column = (high - row * per_row) * LANES + meta[2:3]
        placed = jnp.where(columns == column, weight, 0.0).astype(BF16)
        in_row = jnp.where(row_ids == row, 1.0, 0.0)
        for r in range(n_rows):
            left_ref[r * chans : (r + 1) * chans, :] = values * in_row[r : r + 1].astype(BF16)
        left_ref[data_rows : data_rows + n_rows, :] = in_row.astype(BF16)
        own_ref[...] += dot_nt(left_ref[...], placed)
        return carry

    left_ref[data_rows:, :] = jnp.zeros((left_ref.shape[0] - data_rows, cap), BF16)
    lax.fori_loop(0, n_send, one, 0)
    send_ref[0:data_rows, :] = own_ref[0:data_rows, :].astype(BF16)
    density = own_ref[data_rows : data_rows + n_rows, :]
    high = density.astype(BF16)
    low = (density - high.astype(F32)).astype(BF16)
    send_ref[data_rows : data_rows + 2 * n_rows, :] = jnp.concatenate(
        [high.astype(F32), low.astype(F32)], axis=0
    ).astype(BF16)


def grid(got, n_rows, n_cols):
    n_send, rows, cap = got.shape
    chans = rows - META
    total = n_rows * chans + 2 * n_rows
    return call(
        functools.partial(grid_kernel, n_rows, n_cols),
        [
            jax.ShapeDtypeStruct((total, n_cols), F32),
            jax.ShapeDtypeStruct((total, n_cols), BF16),
        ],
        [vmem_spec()],
        [pltpu.VMEM((total, cap), BF16)],
        2 * n_send * cap * total * n_cols,
        n_send * rows * cap * 2,
        "grid",
    )(got)


def lane_mask(shape, n_cols, sub, depth):
    lane = iota(shape, 1)
    width = n_cols + LANES
    keep_right = (lane >= n_cols) & (lane < n_cols + depth) & (sub == 0)
    keep_left = (lane >= width - depth) & (sub == 1)
    return (lane < n_cols) | keep_right | keep_left


def back_kernel(n_cols, index_ref, kernel_ref, own_ref, peer_ref, halo_ref, out_ref, wide_ref, acc_ref):
    n_ext = halo_ref.shape[0]
    n_rows = n_ext - 2
    n_out = out_ref.shape[1]
    own_chans = own_ref.shape[1]
    all_chans = halo_ref.shape[1]
    width = n_cols + LANES
    keep = lane_mask((all_chans, width), n_cols, index_ref[2], 1)
    acc_ref[...] = jnp.zeros(acc_ref.shape, F32)

    def one(h, carry):
        if peer_ref is None:
            mid = own_ref[h]
        else:
            mid = jnp.concatenate([own_ref[h], peer_ref[h]], axis=0)
        ext = jnp.concatenate([mid, halo_ref[h]], axis=1).astype(F32)
        ext = jnp.where(keep, ext, 0.0)
        wide_ref[0:all_chans, :] = pltpu.roll(ext, width - 1, 1)[:, :n_cols].astype(BF16)
        wide_ref[all_chans : 2 * all_chans, :] = mid
        wide_ref[2 * all_chans :, :] = pltpu.roll(ext, 1, 1)[:, :n_cols].astype(BF16)
        part = dot_nn(kernel_ref[...], wide_ref[...])
        for a in range(3):
            acc_ref[h + a] += part[a * n_out : (a + 1) * n_out]
        return carry

    lax.fori_loop(0, n_ext, one, 0)
    out_ref[...] = acc_ref[2 : 2 + n_rows]


def back(index, kernel, own, peer, halo, n_cols):
    n_ext, all_chans = halo.shape[0], halo.shape[1]
    n_out = kernel.shape[0] // 3
    body = functools.partial(back_kernel, n_cols)
    pieces = [own] if peer is None else [own, peer]
    if peer is None:
        body = lambda i, k, o, *rest: back_kernel(n_cols, i, k, o, None, *rest)
    return call(
        body,
        jax.ShapeDtypeStruct((n_ext - 2, n_out, n_cols), F32),
        [smem_spec()] + [vmem_spec()] * (2 + len(pieces)),
        [
            pltpu.VMEM((3 * all_chans, n_cols), BF16),
            pltpu.VMEM((n_ext + 2, n_out, n_cols), F32),
        ],
        2 * n_ext * 9 * all_chans * n_out * n_cols,
        n_ext * all_chans * n_cols * 2,
        "back",
    )(index, kernel, *pieces, halo)


def grads_kernel(
    index_ref, kernel_ref, gain_ref, feats_ref, halo_ref, cot_ref, back_ref,
    hidden_ref, grads_ref,
    taps_ref, logs_ref, pre_ref, wide_ref, out_grad_ref, pre_grad_ref, gain_acc_ref, acc_ref,
):
    n_feat_rows, _, n_cols = feats_ref.shape
    n_rows = n_feat_rows - 4
    n_hidden = kernel_ref.shape[0]
    chans = kernel_ref.shape[1] // 9
    own = cot_ref.shape[1]
    width = n_cols + LANES
    tile, chan, sub, n_tile = index_ref[0], index_ref[1], index_ref[2], index_ref[3]
    keep_two = lane_mask((chans, width), n_cols, sub, 2)

    def taps(i, carry):
        ext = jnp.concatenate([feats_ref[i], halo_ref[i]], axis=1).astype(F32)
        feats = jnp.where(keep_two, ext[0:chans], 0.0)
        logs_ref[i] = jnp.log(1.0 + (ext[chans : chans + 1] + ext[chans + 1 : chans + 2]))
        taps_ref[i, 0:chans, :] = pltpu.roll(feats, 1, 1).astype(BF16)
        taps_ref[i, chans : 2 * chans, :] = feats.astype(BF16)
        taps_ref[i, 2 * chans : 3 * chans, :] = pltpu.roll(feats, width - 1, 1).astype(BF16)
        return carry

    lax.fori_loop(0, n_feat_rows, taps, 0)
    gain = gain_ref[...]
    keep_one = lane_mask((n_hidden, width), n_cols, sub, 1)
    acc_ref[...] = jnp.zeros(acc_ref.shape, F32)
    for e in (0, 1, n_rows + 2, n_rows + 3):
        out_grad_ref[e] = jnp.zeros((own, n_cols), BF16)
        pre_grad_ref[e] = jnp.zeros((own, n_cols), BF16)
    for r in range(n_rows):
        out_grad_ref[r + 2] = cot_ref[r]

    def hide(h, carry):
        columns = taps_ref[pl.ds(h, 3)].reshape(9 * chans, width)
        pre = dot_nn(kernel_ref[...], columns) + gain * logs_ref[h + 1]
        pre_ref[...] = pre[:, :n_cols]
        hidden = pre / (1.0 + jnp.exp(-pre))
        inside = ((h > 0) | (tile > 0)) & ((h < n_rows + 1) | (tile < n_tile - 1))
        hidden = jnp.where(keep_one & inside, hidden, 0.0)
        hidden_ref[h, 0:n_hidden, :] = pltpu.roll(hidden, 1, 1)[:, :n_cols].astype(BF16)
        hidden_ref[h, n_hidden : 2 * n_hidden, :] = hidden[:, :n_cols].astype(BF16)
        hidden_ref[h, 2 * n_hidden :, :] = pltpu.roll(hidden, width - 1, 1)[:, :n_cols].astype(BF16)
        left = out_grad_ref[pl.ds(h, 3)].reshape(3 * own, n_cols)
        acc_ref[:, 0 : 3 * n_hidden] += dot_nt(left, hidden_ref[h])

        @pl.when((h > 0) & (h < n_rows + 1))
        def _():
            mine = pre_ref[pl.ds(pl.multiple_of(chan * own, own), own), :]
            s = 1.0 / (1.0 + jnp.exp(-mine))
            grad = (back_ref[h - 1] * s * (1.0 + mine * (1.0 - s))).astype(BF16)
            pre_grad_ref[h + 1] = grad
            gain_acc_ref[...] += grad.astype(F32) * logs_ref[h + 1][:, :n_cols]

        return carry

    gain_acc_ref[...] = jnp.zeros(gain_acc_ref.shape, F32)
    lax.fori_loop(0, n_rows + 2, hide, 0)
    one_at = 3 * n_hidden

    def first_grad(f, carry):
        left = pre_grad_ref[pl.ds(f, 3)].reshape(3 * own, n_cols)
        acc_ref[:, one_at : one_at + 3 * chans] += dot_nt(left, taps_ref[f + 1][:, :n_cols])
        return carry

    lax.fori_loop(0, n_rows + 2, first_grad, 0)
    gain_at = one_at + 3 * chans
    gain_grad = jnp.sum(gain_acc_ref[...], axis=1, keepdims=True)
    grads_ref[:, 0:gain_at] = acc_ref[:, 0:gain_at].astype(BF16)
    tail = grads_ref.shape[1] - gain_at
    high = gain_grad.astype(BF16).astype(F32)
    low = gain_grad - high
    spread = jnp.where(iota((own, tail), 1) == 0, high, low).astype(BF16)
    grads_ref[0:own, gain_at:] = spread
    grads_ref[own:, gain_at:] = jnp.zeros((2 * own, tail), BF16)


def grads(index, kernel, gain, feats, halo, cot, back_out):
    n_rows, own, n_cols = cot.shape
    n_hidden = kernel.shape[0]
    chans = kernel.shape[1] // 9
    width = n_cols + LANES
    lanes = -(-(3 * n_hidden + 3 * chans + 2) // LANES) * LANES
    return call(
        grads_kernel,
        [
            jax.ShapeDtypeStruct((n_rows + 2, 3 * n_hidden, n_cols), BF16),
            jax.ShapeDtypeStruct((3 * own, lanes), BF16),
        ],
        [smem_spec()] + [vmem_spec()] * 6,
        [
            pltpu.VMEM((n_rows + 4, 3 * chans, width), BF16),
            pltpu.VMEM((n_rows + 4, 1, width), F32),
            pltpu.VMEM((n_hidden, n_cols), F32),
            pltpu.VMEM((8, LANES), BF16),
            pltpu.VMEM((n_rows + 4, own, n_cols), BF16),
            pltpu.VMEM((n_rows + 4, own, n_cols), BF16),
            pltpu.VMEM((own, n_cols), F32),
            pltpu.VMEM((3 * own, lanes), F32),
        ],
        2 * (n_rows + 2) * 9 * n_cols * n_hidden * (own + chans),
        (n_rows + 2) * 3 * n_hidden * n_cols * 2,
        "grads",
    )(index, kernel, gain, feats, halo, cot, back_out)


def encode_kernel(kernel_ref, hidden_ref, out_ref, acc_ref):
    n_ext = hidden_ref.shape[0]
    n_rows = n_ext - 2
    own = out_ref.shape[1]
    acc_ref[...] = jnp.zeros(acc_ref.shape, F32)

    def one(h, carry):
        part = dot_nn(kernel_ref[...], hidden_ref[h])
        for a in range(3):
            acc_ref[h - a + 2] += part[a * own : (a + 1) * own]
        return carry

    lax.fori_loop(0, n_ext, one, 0)
    out_ref[...] = acc_ref[2 : 2 + n_rows].astype(BF16)


def encode(kernel, hidden):
    n_ext, _, n_cols = hidden.shape
    own = kernel.shape[0] // 3
    return call(
        encode_kernel,
        jax.ShapeDtypeStruct((n_ext - 2, own, n_cols), BF16),
        [vmem_spec()] * 2,
        [pltpu.VMEM((n_ext + 2, own, n_cols), F32)],
        2 * n_ext * kernel.shape[0] * kernel.shape[1] * n_cols,
        hidden.size * 2,
        "encode",
    )(kernel, hidden)


def step_perm(count, by):
    return [(i, i + by) for i in range(count) if 0 <= i + by < count]


def swap_sub(x):
    return lax.ppermute(x, "sub", [(0, 1), (1, 0)])


def swap_chan(x):
    return lax.ppermute(x, "chan", [(0, 1), (1, 0)])


def with_rows(block, depth, n_tile):
    low = lax.ppermute(block[-depth:], "tile", step_perm(n_tile, 1))
    high = lax.ppermute(block[:depth], "tile", step_perm(n_tile, -1))
    return jnp.concatenate([low, block, high], axis=0)


def side_halo(block, sub):
    n_cols = block.shape[-1]
    near = jnp.where(sub == 0, block[..., n_cols - LANES :], block[..., :LANES])
    return swap_sub(near)


def body(obs_values, obs_weight, obs_tile, obs_cell, conv_one, conv_two, density_gain, cotangent):
    own, n_rows, n_cols = cotangent.shape
    n_tile = lax.axis_size("tile")
    n_sub = lax.axis_size("sub")
    n_chan = lax.axis_size("chan")
    n_tiles = n_tile * n_sub
    chans = obs_values.shape[1]
    n_hidden = own * n_chan
    cap = 2 * obs_values.shape[0] // n_tiles
    tile, chan, sub = lax.axis_index("tile"), lax.axis_index("chan"), lax.axis_index("sub")
    index = jnp.stack([tile, chan, sub, jnp.int32(n_tile)]).astype(jnp.int32)

    cot = cotangent.transpose(1, 0, 2)
    cot_ext = with_rows(cot, 1, n_tile)
    if n_chan == 2:
        cot_peer = swap_chan(cot_ext)
        cot_pair = jnp.concatenate([cot_ext, cot_peer], axis=1)
    else:
        cot_peer = None
        cot_ext = lax.all_gather(cot_ext, "chan", axis=1, tiled=True)
        cot_pair = cot_ext
    cot_halo = side_halo(cot_pair, sub)

    columns = lax.all_to_all(conv_two, "chan", split_axis=3, concat_axis=2, tiled=True)
    if n_chan == 2:
        columns = jnp.where(chan == 0, columns, jnp.roll(columns, own, axis=2))
    back_weights = columns.transpose(0, 3, 1, 2).reshape(3 * own, 3 * n_hidden)
    code_weights = conv_two.transpose(0, 2, 1, 3).reshape(3 * own, 3 * n_hidden)
    one_full = lax.all_gather(conv_one, "chan", axis=2, tiled=True)
    one_weights = one_full.transpose(2, 0, 1, 3).reshape(n_hidden, 9 * chans)
    gain = lax.all_gather(density_gain, "chan", axis=0, tiled=True)[:, None]

    sent = route(obs_values, obs_weight, obs_tile, obs_cell, n_tiles, cap)
    got = lax.all_to_all(sent, ("tile", "sub"), split_axis=0, concat_axis=0, tiled=True)
    back_out = back(index, back_weights, cot_ext, cot_peer, cot_halo, n_cols)
    part, message = grid(got, n_rows, n_cols)
    data_rows = n_rows * chans
    data = part[:data_rows]
    density = part[data_rows : data_rows + n_rows]
    if n_chan == 2:
        other = swap_chan(message).astype(F32)
        data = data + other[:data_rows]
        density = density + (
            other[data_rows : data_rows + n_rows] + other[data_rows + n_rows :]
        )
    else:
        data, density = lax.psum((data, density), "chan")
    features = data.reshape(n_rows, chans, n_cols) / (1.0 + density)[:, None]
    high = density.astype(BF16)
    low = (density - high.astype(F32)).astype(BF16)
    packed = jnp.concatenate(
        [
            features.astype(BF16),
            high[:, None],
            low[:, None],
            jnp.zeros((n_rows, META - 2, n_cols), BF16),
        ],
        axis=1,
    )
    feats = with_rows(packed, 2, n_tile)
    feats_halo = side_halo(feats, sub)

    hidden, partial = grads(index, one_weights, gain, feats, feats_halo, cot, back_out)

    half = partial.shape[0] // 2
    keep = jnp.where(sub == 0, partial[:half], partial[half:])
    give = jnp.where(sub == 0, partial[half:], partial[:half])
    mine = (keep.astype(F32) + swap_sub(give).astype(F32)).astype(BF16)
    lanes = mine.shape[1]
    spread = lax.all_to_all(
        mine.reshape(n_tile, half // n_tile, lanes), "tile", 0, 0, tiled=True
    )
    mine = jnp.sum(spread.astype(F32), axis=0).astype(BF16)
    mine = lax.all_to_all(
        jnp.broadcast_to(mine[None], (n_tile,) + mine.shape), "tile", 0, 0, tiled=True
    ).reshape(half, lanes)
    other = swap_sub(mine)
    first = jnp.where(sub == 0, mine, other)
    second = jnp.where(sub == 0, other, mine)
    total = jnp.concatenate([first, second], axis=0).astype(F32)

    encoded = encode(code_weights, hidden).transpose(1, 0, 2)

    scale = 1.0 / math.sqrt(n_tiles * n_rows * n_cols)
    total = total * scale
    one_at = 3 * n_hidden
    gain_at = one_at + 3 * chans
    grad_two = total[:, :one_at].reshape(3, own, 3, n_hidden).transpose(0, 2, 1, 3)[::-1]
    grad_one = total[:, one_at:gain_at].reshape(3, own, 3, chans).transpose(0, 2, 1, 3)[::-1]
    grad_gain = total[:own, gain_at] + total[:own, gain_at + 1]
    return encoded, grad_one, grad_two, grad_gain


def solution(mesh):
    placed = (
        P(("member", "tile", "chan", "sub"), None),
        P(("member", "tile", "chan", "sub")),
        P(("member", "tile", "chan", "sub")),
        P(("member", "tile", "chan", "sub")),
        P(None, None, "chan", None),
        P(None, None, "chan", None),
        P("chan"),
        P(("member", "chan"), "tile", "sub"),
    )
    return jax.shard_map(
        body,
        mesh=mesh,
        in_specs=placed,
        out_specs=(
            P(("member", "chan"), "tile", "sub"),
            P("member", None, "chan", None),
            P("member", None, "chan", None),
            P(("member", "chan")),
        ),
        check_vma=False,
    )
```

```python
import functools
import math

import jax
import jax.numpy as jnp
from jax import lax
from jax.experimental import pallas as pl
from jax.experimental.pallas import tpu as pltpu
from jax.sharding import PartitionSpec as P

BF16 = jnp.bfloat16
F32 = jnp.float32
LANES = 128
BLOCK = 256
META = 8
MIB = 1024 * 1024


def dot_nt(a, b):
    return lax.dot_general(a, b, (((1,), (1,)), ((), ())), preferred_element_type=F32)


def dot_nn(a, b):
    return lax.dot_general(a, b, (((1,), (0,)), ((), ())), preferred_element_type=F32)


def iota(shape, dim, dtype=jnp.int32):
    return lax.broadcasted_iota(jnp.int32, shape, dim).astype(dtype)


def vmem_spec():
    return pl.BlockSpec(memory_space=pltpu.VMEM)


def smem_spec():
    return pl.BlockSpec(memory_space=pltpu.SMEM)


def call(kernel, out_shape, in_specs, scratch, flops, moved, name, vmem=48):
    n_out = len(out_shape) if isinstance(out_shape, (tuple, list)) else None
    out_specs = vmem_spec() if n_out is None else [vmem_spec() for _ in range(n_out)]
    return pl.pallas_call(
        kernel,
        out_shape=out_shape,
        in_specs=in_specs,
        out_specs=out_specs,
        scratch_shapes=scratch,
        compiler_params=pltpu.CompilerParams(vmem_limit_bytes=vmem * MIB),
        cost_estimate=pl.CostEstimate(flops=flops, bytes_accessed=moved, transcendentals=0),
        name=name,
    )


def route_kernel(n_tiles, cap, n_parts, tile_ref, weight_ref, cell_ref, values_ref, *rest):
    outs = rest[:n_parts]
    onehot_ref, slot_ref, weight32_ref, all_ref, info_ref, info_smem, sem = rest[n_parts:]
    n_lines = tile_ref.shape[0]
    n_blocks = n_lines // 2
    n_obs_chans = values_ref.shape[0]
    pairs = n_tiles * n_lines
    tiles = tile_ref[...]
    for t in range(n_tiles):
        onehot_ref[t * n_lines : (t + 1) * n_lines, :] = jnp.where(tiles == t, 1.0, 0.0).astype(BF16)
    onehot = onehot_ref[...]
    upper = jnp.where(
        iota((LANES, LANES), 0) <= iota((LANES, LANES), 1), 1.0, 0.0
    ).astype(BF16)
    here = iota((pairs, pairs), 0)
    there = iota((pairs, pairs), 1)
    earlier = jnp.where(
        (here // n_lines == there // n_lines) & (there < here), 1.0, 0.0
    ).astype(BF16)
    total_row = dot_nt(jnp.ones((8, LANES), BF16), onehot)
    offset_row = dot_nt(total_row.astype(BF16), earlier)
    base_row = jnp.minimum(jnp.floor(offset_row * (1.0 / LANES)) * LANES, float(cap - BLOCK))
    even = iota((8, pairs), 1) % 2 == 0
    base_pair = jnp.where(even, base_row, pltpu.roll(base_row, 1, 1))
    spill = jnp.where(offset_row + total_row > base_pair + BLOCK, 1.0, 0.0)
    any_spill = jnp.max(spill, axis=1, keepdims=True)
    info_ref[...] = jnp.where(
        iota((8, pairs), 0) == 0, base_row, any_spill
    ).astype(jnp.int32)
    copy = pltpu.make_async_copy(info_ref, info_smem, sem)
    copy.start()
    cum = dot_nn(onehot, upper)
    totals = dot_nn(onehot, jnp.ones((LANES, LANES), BF16))
    offset = dot_nn(earlier, totals.astype(BF16))
    place = cum + offset - 1.0
    slots = jnp.zeros(tiles.shape, F32)
    for t in range(n_tiles):
        slots = jnp.where(tiles == t, place[t * n_lines : (t + 1) * n_lines, :], slots)
    slot_ref[...] = slots
    weight32_ref[...] = weight_ref[...].astype(F32)
    all_ref[...] = jnp.zeros(all_ref.shape, BF16)
    meta_row = iota((16, BLOCK), 0)
    window = iota((BLOCK, BLOCK), 0, F32)
    copy.wait()

    def line(ref, b):
        return jnp.concatenate([ref[pl.ds(2 * b, 1), :], ref[pl.ds(2 * b + 1, 1), :]], axis=1)

    def columns(b):
        values = values_ref[:, pl.ds(pl.multiple_of(b * BLOCK, BLOCK), BLOCK)]
        cell = line(cell_ref, b)
        weight = line(weight32_ref, b)
        high = (cell // LANES).astype(F32)
        low = (cell % LANES).astype(F32)
        meta = jnp.where(
            meta_row == 0,
            weight,
            jnp.where(meta_row == 1, high, jnp.where(meta_row == 2, low, 0.0)),
        ).astype(BF16)
        return jnp.concatenate([values, meta], axis=0)

    def add(t, base, wide, key):
        chosen = jnp.where(window == key, 1.0, 0.0).astype(BF16)
        part = dot_nt(wide, chosen)[: n_obs_chans + META].astype(BF16)
        where = pl.ds(pl.multiple_of(base, LANES), BLOCK)
        all_ref[t, :, where] = all_ref[t, :, where] + part

    def first(b):
        wide = columns(b)
        tile = line(tile_ref, b)
        slot = line(slot_ref, b)
        for t in range(n_tiles):
            base = info_smem[0, t * n_lines + 2 * b]
            key = jnp.where(tile == t, slot - base.astype(F32), -1.0)
            add(t, base, wide, key)

    def first_two(i, carry):
        first(2 * i)
        first(2 * i + 1)
        return carry

    lax.fori_loop(0, n_blocks // 2, first_two, 0)

    if cap > BLOCK:

        @pl.when(info_smem[1, 0] > 0)
        def _():
            def second(b, carry):
                wide = columns(b)
                tile = line(tile_ref, b)
                slot = line(slot_ref, b)
                for t in range(n_tiles):
                    start = info_smem[0, t * n_lines + 2 * b]
                    base = jnp.minimum(start + BLOCK, cap - BLOCK)
                    far = (tile == t) & (slot >= (start + BLOCK).astype(F32))
                    key = jnp.where(far, slot - base.astype(F32), -1.0)
                    add(t, base, wide, key)
                return carry

            lax.fori_loop(0, n_blocks, second, 0)

    part = cap // n_parts
    for p in range(n_parts):
        outs[p][...] = all_ref[:, :, p * part : (p + 1) * part]


def route(obs_values, obs_weight, obs_tile, obs_cell, n_tiles, cap, n_parts):
    n_obs, chans = obs_values.shape
    n_lines = n_obs // LANES
    rows = chans + META
    return call(
        functools.partial(route_kernel, n_tiles, cap, n_parts),
        [jax.ShapeDtypeStruct((n_tiles, rows, cap // n_parts), BF16)] * n_parts,
        [vmem_spec()] * 4,
        [
            pltpu.VMEM((n_tiles * n_lines, LANES), BF16),
            pltpu.VMEM((n_lines, LANES), F32),
            pltpu.VMEM((n_lines, LANES), F32),
            pltpu.VMEM((n_tiles, rows, cap), BF16),
            pltpu.VMEM((8, n_tiles * n_lines), jnp.int32),
            pltpu.SMEM((8, n_tiles * n_lines), jnp.int32),
            pltpu.SemaphoreType.DMA,
        ],
        2 * n_obs * n_tiles * BLOCK * 80,
        n_tiles * rows * cap * 2,
        "route",
        24,
    )(
        obs_tile.reshape(n_lines, LANES),
        obs_weight.reshape(n_lines, LANES),
        obs_cell.reshape(n_lines, LANES),
        obs_values.T,
    )


def grid_kernel(n_rows, n_cols, group, first, last, got_ref, *rest):
    rest = list(rest)
    before_ref = None if first else rest.pop(0)
    own_ref = rest.pop(0)
    send_ref = rest.pop(0) if last else None
    left_ref, right_ref = rest
    n_send, rows, cap = got_ref.shape
    chans = rows - META
    per_row = n_cols // LANES
    columns = iota((n_cols, cap), 0, F32)
    row_ids = iota((META, cap), 0)
    total = None
    for g in range(n_send // group):
        slot = g % 2
        for i in range(group):
            s = g * group + i
            at = slice(i * cap, (i + 1) * cap)
            values = got_ref[s, 0:chans, :]
            meta = got_ref[s, chans:rows, :].astype(F32)
            weight = meta[0:1]
            high = meta[1:2]
            row = jnp.floor((high + 0.5) * (1.0 / per_row))
            column = (high - row * per_row) * LANES + meta[2:3]
            right_ref[slot, :, at] = jnp.where(columns == column, weight, 0.0).astype(BF16)
            for r in range(n_rows):
                mask = jnp.where(row == r, 1.0, 0.0)
                left_ref[slot, r * rows : r * rows + chans, at] = values * mask.astype(BF16)
                left_ref[slot, r * rows + chans : (r + 1) * rows, at] = jnp.where(
                    row_ids == 0, mask, 0.0
                ).astype(BF16)
        part = dot_nt(left_ref[slot], right_ref[slot])
        total = part if total is None else total + part
    if before_ref is not None:
        total = total + before_ref[...]
    own_ref[...] = total
    if last:
        line = iota((META, n_cols), 0)
        for r in range(n_rows):
            send_ref[r * rows : r * rows + chans, :] = own_ref[r * rows : r * rows + chans, :].astype(BF16)
            extra = own_ref[r * rows + chans : (r + 1) * rows, :]
            density = extra[0:1]
            high = density.astype(BF16).astype(F32)
            send_ref[r * rows + chans : (r + 1) * rows, :] = jnp.where(
                line == 0, high, jnp.where(line == 1, density - high, 0.0)
            ).astype(BF16)


def grid(got, before, last, n_rows, n_cols):
    n_send, rows, cap = got.shape
    group = 4
    total = n_rows * rows
    outs = [jax.ShapeDtypeStruct((total, n_cols), F32)]
    if last:
        outs.append(jax.ShapeDtypeStruct((total, n_cols), BF16))
    ins = [got] if before is None else [got, before]
    return call(
        functools.partial(grid_kernel, n_rows, n_cols, group, before is None, last),
        outs,
        [vmem_spec()] * len(ins),
        [
            pltpu.VMEM((2, total, group * cap), BF16),
            pltpu.VMEM((2, n_cols, group * cap), BF16),
        ],
        2 * n_send * cap * total * n_cols,
        n_send * rows * cap * 2,
        "grid_last" if last else "grid_part",
        32,
    )(*ins)


def lane_mask(shape, n_cols, sub, depth):
    lane = iota(shape, 1)
    width = n_cols + LANES
    keep_right = (lane >= n_cols) & (lane < n_cols + depth) & (sub == 0)
    keep_left = (lane >= width - depth) & (sub == 1)
    return (lane < n_cols) | keep_right | keep_left


def back_kernel(n_cols, n_pieces, index_ref, kernel_ref, *rest):
    pieces = [(rest[2 * i], rest[2 * i + 1]) for i in range(n_pieces)]
    side_ref, out_ref, wide_ref = rest[2 * n_pieces :]
    n_ext, all_chans = side_ref.shape[0], side_ref.shape[1]
    n_rows = n_ext - 2
    width = n_cols + LANES
    keep = lane_mask((1, width), n_cols, index_ref[2], 1)
    for h in range(n_ext):
        if h == 0 or h == n_ext - 1:
            mids = [edge[min(h, 1)] for _, edge in pieces]
        else:
            mids = [middle[h - 1] for middle, _ in pieces]
        mid = mids[0] if n_pieces == 1 else jnp.concatenate(mids, axis=0)
        ext = jnp.concatenate([mid, side_ref[h]], axis=1).astype(F32)
        ext = jnp.where(keep, ext, 0.0)
        at = slice(h * n_cols, (h + 1) * n_cols)
        wide_ref[0:all_chans, at] = pltpu.roll(ext, width - 1, 1)[:, :n_cols].astype(BF16)
        wide_ref[all_chans : 2 * all_chans, at] = mid
        wide_ref[2 * all_chans :, at] = pltpu.roll(ext, 1, 1)[:, :n_cols].astype(BF16)
    total = None
    for a in range(3):
        at = slice((2 - a) * n_cols, (2 - a + n_rows) * n_cols)
        part = dot_nn(kernel_ref[a], wide_ref[:, at])
        total = part if total is None else total + part
    out_ref[...] = total


def back(index, kernel, pieces, side, n_cols):
    n_ext, all_chans = side.shape[0], side.shape[1]
    n_out = kernel.shape[1]
    return call(
        functools.partial(back_kernel, n_cols, len(pieces)),
        jax.ShapeDtypeStruct((n_out, (n_ext - 2) * n_cols), F32),
        [smem_spec()] + [vmem_spec()] * (2 + 2 * len(pieces)),
        [pltpu.VMEM((3 * all_chans, n_ext * n_cols), BF16)],
        2 * n_ext * 9 * all_chans * n_out * n_cols,
        n_ext * all_chans * n_cols * 2,
        "back",
        32,
    )(index, kernel, *[x for piece in pieces for x in piece], side)


def grads_kernel(
    split, chans, index_ref, kernel_ref, gain_ref, own_ref, edge_ref, peer_ref, peer_edge_ref,
    side_ref, cot_ref, back_ref, hidden_ref, *rest,
):
    rest = list(rest)
    if split:
        keep_out, give_out = rest.pop(0), rest.pop(0)
    else:
        all_out = rest.pop(0)
    taps_ref, logs_ref, pre_ref, wide_ref, out_left_ref, pre_left_ref, acc_ref = rest
    n_rows, own, n_cols = cot_ref.shape
    n_hidden = kernel_ref.shape[1]
    rows = chans + META
    taps_rows = 3 * chans
    width = n_cols + LANES
    tile, chan, sub, n_tile = index_ref[0], index_ref[1], index_ref[2], index_ref[3]
    keep_two = lane_mask((1, width), n_cols, sub, 2)

    log_line = iota((16, width), 0)
    for i in range(n_rows + 4):
        if 2 <= i < n_rows + 2:
            mid = own_ref[i - 2]
            if peer_ref is not None:
                mid = mid + peer_ref[i - 2].astype(F32)
        else:
            e = i if i < 2 else i - n_rows
            mid = edge_ref[e].astype(F32)
            if peer_ref is not None:
                mid = mid + peer_edge_ref[e].astype(F32)
        side = side_ref[i, 0:rows].astype(F32)
        if peer_ref is not None:
            side = side + side_ref[i, rows : 2 * rows].astype(F32)
        ext = jnp.concatenate([mid, side], axis=1)
        density = ext[chans : chans + 1] + ext[chans + 1 : chans + 2]
        logs = jnp.log(1.0 + density)
        logs_ref[i] = logs
        shrink = jnp.where(keep_two, 1.0 / (1.0 + density), 0.0)
        feats = ext[0:chans] * shrink
        at = slice(i * width, (i + 1) * width)
        taps_ref[0:chans, at] = pltpu.roll(feats, 1, 1).astype(BF16)
        taps_ref[chans : 2 * chans, at] = feats.astype(BF16)
        taps_ref[2 * chans : taps_rows, at] = pltpu.roll(feats, width - 1, 1).astype(BF16)
        high = logs.astype(BF16).astype(F32)
        middle = (logs - high).astype(BF16).astype(F32)
        taps_ref[taps_rows:, at] = jnp.where(
            log_line == 0,
            high,
            jnp.where(log_line == 1, middle, jnp.where(log_line == 2, logs - high - middle, 0.0)),
        ).astype(BF16)

    nothing = jnp.zeros((own, n_cols), BF16)
    for h in range(n_rows + 2):
        for a in range(3):
            inside = 0 <= h - a < n_rows
            put = slice(a * own, (a + 1) * own)
            out_left_ref[put, h * n_cols : (h + 1) * n_cols] = cot_ref[h - a] if inside else nothing
            if not inside:
                pre_left_ref[put, h * width : h * width + n_cols] = nothing
        pre_left_ref[:, h * width + n_cols : (h + 1) * width] = jnp.zeros((3 * own, LANES), BF16)

    gain = gain_ref[...]
    keep_one = lane_mask((1, width), n_cols, sub, 1)
    group = 2
    for first in range(0, n_rows + 2, group):
        pre_all = None
        for a in range(3):
            at = slice((first + a) * width, (first + a + group) * width)
            part = dot_nn(kernel_ref[a], taps_ref[0:taps_rows, at])
            pre_all = part if pre_all is None else pre_all + part
        for k in range(group):
            h = first + k
            pre = pre_all[:, k * width : (k + 1) * width] + gain * logs_ref[h + 1]
            at = slice(h * n_cols, (h + 1) * n_cols)
            keep = keep_one
            if h == 0:
                keep = keep & (tile > 0)
            elif h == n_rows + 1:
                keep = keep & (tile < n_tile - 1)
            else:
                pre_ref[:, (h - 1) * n_cols : h * n_cols] = pre[:, :n_cols]
            half = 0.5 * pre
            hidden = jnp.where(keep, half + half * jnp.tanh(half), 0.0)
            hidden_ref[h] = hidden.astype(BF16)
            wide_ref[0:n_hidden, at] = pltpu.roll(hidden, 1, 1)[:, :n_cols].astype(BF16)
            wide_ref[n_hidden : 2 * n_hidden, at] = hidden[:, :n_cols].astype(BF16)
            wide_ref[2 * n_hidden :, at] = pltpu.roll(hidden, width - 1, 1)[:, :n_cols].astype(BF16)

    for r in range(n_rows):
        at = slice(r * n_cols, (r + 1) * n_cols)
        mine = pre_ref[pl.ds(pl.multiple_of(chan * own, own), own), at]
        s = 0.5 + 0.5 * jnp.tanh(0.5 * mine)
        grad = (back_ref[:, at] * s * (1.0 + mine * (1.0 - s))).astype(BF16)
        for a in range(3):
            h = r + a
            pre_left_ref[a * own : (a + 1) * own, h * width : h * width + n_cols] = grad

    three = 3 * own
    lanes = 3 * n_hidden
    half_rows = taps_rows // 2
    acc_ref[0:three, :] = dot_nt(out_left_ref[...], wide_ref[...])
    one = dot_nt(taps_ref[:, width : (n_rows + 3) * width], pre_left_ref[...])
    acc_ref[three:, :] = jnp.zeros((acc_ref.shape[0] - three, lanes), F32)
    acc_ref[three : three + half_rows, 0:three] = one[0:half_rows]
    acc_ref[three : three + half_rows, lanes // 2 : lanes // 2 + three] = one[half_rows:taps_rows]
    gains = one[taps_rows : taps_rows + 1] + one[taps_rows + 1 : taps_rows + 2] + one[taps_rows + 2 : taps_rows + 3]
    acc_ref[three + half_rows : three + half_rows + 1, 0:three] = gains
    if split:
        half = acc_ref.shape[0] // 2
        keep_out[...] = acc_ref[pl.ds(pl.multiple_of(sub * half, half), half), :]
        give_out[...] = acc_ref[pl.ds(pl.multiple_of((1 - sub) * half, half), half), :].astype(BF16)
    else:
        all_out[...] = acc_ref[...]


def grads(split, index, kernel, gain, own, edge, peer, peer_edge, side, cot, back_out):
    n_rows, n_own, n_cols = cot.shape
    n_hidden = kernel.shape[1]
    chans = kernel.shape[2] // 3
    width = n_cols + LANES
    lanes = 3 * n_hidden
    acc_rows = 3 * n_own + 3 * chans // 2 + 32
    body = functools.partial(grads_kernel, split, chans)
    ins = [own, edge, peer, peer_edge, side, cot, back_out]
    if peer is None:
        ins = [own, edge, side, cot, back_out]
        body = lambda i, k, g, o, e, *rest: grads_kernel(split, chans, i, k, g, o, e, None, None, *rest)
    outs = [jax.ShapeDtypeStruct((n_rows + 2, n_hidden, width), BF16)]
    if split:
        outs.append(jax.ShapeDtypeStruct((acc_rows // 2, lanes), F32))
        outs.append(jax.ShapeDtypeStruct((acc_rows // 2, lanes), BF16))
    else:
        outs.append(jax.ShapeDtypeStruct((acc_rows, lanes), F32))
    return call(
        body,
        outs,
        [smem_spec()] + [vmem_spec()] * (2 + len(ins)),
        [
            pltpu.VMEM((3 * chans + 16, (n_rows + 4) * width), BF16),
            pltpu.VMEM((n_rows + 4, 1, width), F32),
            pltpu.VMEM((n_hidden, n_rows * n_cols), F32),
            pltpu.VMEM((3 * n_hidden, (n_rows + 2) * n_cols), BF16),
            pltpu.VMEM((3 * n_own, (n_rows + 2) * n_cols), BF16),
            pltpu.VMEM((3 * n_own, (n_rows + 2) * width), BF16),
            pltpu.VMEM((acc_rows, lanes), F32),
        ],
        2 * (n_rows + 2) * 9 * n_cols * n_hidden * (n_own + chans),
        (n_rows + 2) * 3 * n_hidden * n_cols * 2,
        "grads",
        50,
    )(index, kernel, gain, *ins)


def encode_kernel(kernel_ref, hidden_ref, out_ref, wide_ref):
    n_ext, n_hidden, width = hidden_ref.shape
    n_rows = n_ext - 2
    n_cols = width - LANES
    for h in range(n_ext):
        hidden = hidden_ref[h].astype(F32)
        at = slice(h * n_cols, (h + 1) * n_cols)
        wide_ref[0:n_hidden, at] = pltpu.roll(hidden, 1, 1)[:, :n_cols].astype(BF16)
        wide_ref[n_hidden : 2 * n_hidden, at] = hidden_ref[h, :, 0:n_cols]
        wide_ref[2 * n_hidden :, at] = pltpu.roll(hidden, width - 1, 1)[:, :n_cols].astype(BF16)
    total = None
    for a in range(3):
        part = dot_nn(kernel_ref[a], wide_ref[:, a * n_cols : (a + n_rows) * n_cols])
        total = part if total is None else total + part
    for r in range(n_rows):
        out_ref[r] = total[:, r * n_cols : (r + 1) * n_cols].astype(BF16)


def encode(kernel, hidden):
    n_ext, n_hidden, width = hidden.shape
    own = kernel.shape[1]
    n_cols = width - LANES
    return call(
        encode_kernel,
        jax.ShapeDtypeStruct((n_ext - 2, own, n_cols), BF16),
        [vmem_spec()] * 2,
        [pltpu.VMEM((3 * n_hidden, n_ext * n_cols), BF16)],
        2 * n_ext * 9 * own * n_hidden * n_cols,
        hidden.size * 2,
        "encode",
        32,
    )(kernel, hidden)


def quarters_kernel(index_ref, keep_ref, got_ref, *outs):
    n = len(outs)
    rows = keep_ref.shape[0] // n
    for k in range(n):
        other = jnp.bitwise_xor(index_ref[0], k)
        at = pl.ds(pl.multiple_of(other * rows, rows), rows)
        outs[k][...] = (keep_ref[at, :] + got_ref[at, :].astype(F32)).astype(outs[k].dtype)


def quarters(index, keep, got, n):
    rows, lanes = keep.shape
    return call(
        quarters_kernel,
        [jax.ShapeDtypeStruct((rows // n, lanes), F32 if k == 0 else BF16) for k in range(n)],
        [smem_spec(), vmem_spec(), vmem_spec()],
        [],
        rows * lanes,
        rows * lanes * 8,
        "quarters",
        16,
    )(index, keep, got)


def finish_kernel(scale, own, chans, index_ref, mine_ref, other_ref, two_ref, one_ref, gain_ref, all_ref):
    n, rows, lanes = mine_ref.shape
    n_hidden = lanes // 3
    tile, sub = index_ref[0], index_ref[2]
    for k in range(n):
        at = jnp.bitwise_xor(tile, k) * rows
        here = pl.multiple_of(sub * (n * rows) + at, rows)
        there = pl.multiple_of((1 - sub) * (n * rows) + at, rows)
        all_ref[pl.ds(here, rows), :] = mine_ref[k].astype(F32) * scale
        all_ref[pl.ds(there, rows), :] = other_ref[k].astype(F32) * scale
    half_rows = 3 * chans // 2
    for a in range(3):
        for b in range(3):
            two_ref[a, b] = all_ref[a * own : (a + 1) * own, b * n_hidden : (b + 1) * n_hidden]
        lines = jnp.concatenate(
            [
                all_ref[3 * own : 3 * own + half_rows, s + a * own : s + (a + 1) * own]
                for s in (0, lanes // 2)
            ],
            axis=0,
        )
        for b in range(3):
            one_ref[a, b] = lines[b * chans : (b + 1) * chans]
    gain_ref[...] = all_ref[3 * own + half_rows : 3 * own + half_rows + 1, own : 2 * own]


def finish(index, mine, other, scale, own, chans):
    n, rows, lanes = mine.shape
    n_hidden = lanes // 3
    return call(
        functools.partial(finish_kernel, scale, own, chans),
        [
            jax.ShapeDtypeStruct((3, 3, own, n_hidden), F32),
            jax.ShapeDtypeStruct((3, 3, chans, own), F32),
            jax.ShapeDtypeStruct((1, own), F32),
        ],
        [smem_spec(), vmem_spec(), vmem_spec()],
        [pltpu.VMEM((2 * n * rows, lanes), F32)],
        n * rows * lanes,
        n * rows * lanes * 12,
        "finish",
        24,
    )(index, mine, other)


def step_perm(count, by):
    return [(i, i + by) for i in range(count) if 0 <= i + by < count]


def swap_sub(x):
    return lax.ppermute(x, "sub", [(0, 1), (1, 0)])


def swap_chan(x):
    return lax.ppermute(x, "chan", [(0, 1), (1, 0)])


def swap_tile(x, n_tile, k):
    return lax.ppermute(x, "tile", [(i, i ^ k) for i in range(n_tile)])


def edges(block, depth, n_tile):
    low = lax.ppermute(block[-depth:], "tile", step_perm(n_tile, 1))
    high = lax.ppermute(block[:depth], "tile", step_perm(n_tile, -1))
    return low, high


def near(block, sub):
    n_cols = block.shape[-1]
    return jnp.where(sub == 0, block[..., n_cols - LANES :], block[..., :LANES])


def side_rows(parts, sub):
    columns = [
        jnp.concatenate([near(edge[: edge.shape[0] // 2], sub), near(mid, sub), near(edge[edge.shape[0] // 2 :], sub)], axis=0)
        for mid, edge in parts
    ]
    both = columns[0] if len(columns) == 1 else jnp.concatenate(columns, axis=1)
    return swap_sub(both)


def body(obs_values, obs_weight, obs_tile, obs_cell, conv_one, conv_two, density_gain, cotangent):
    own, n_rows, n_cols = cotangent.shape
    n_tile = lax.axis_size("tile")
    n_sub = lax.axis_size("sub")
    n_chan = lax.axis_size("chan")
    pair = n_chan == 2
    n_tiles = n_tile * n_sub
    chans = obs_values.shape[1]
    n_hidden = own * n_chan
    cap = 2 * obs_values.shape[0] // n_tiles
    tile, chan, sub = lax.axis_index("tile"), lax.axis_index("chan"), lax.axis_index("sub")
    index = jnp.stack([tile, chan, sub, jnp.int32(n_tile)]).astype(jnp.int32)

    sent = route(obs_values, obs_weight, obs_tile, obs_cell, n_tiles, cap, 2)
    got = [
        lax.all_to_all(x, ("tile", "sub"), split_axis=0, concat_axis=0, tiled=True) for x in sent
    ]

    cotangent, conv_one, conv_two, density_gain, _ = lax.optimization_barrier(
        (cotangent, conv_one, conv_two, density_gain, sent[0])
    )
    cot = cotangent.transpose(1, 0, 2)
    low, high = edges(cot, 1, n_tile)
    cot_edge = jnp.concatenate([low, high], axis=0)
    if pair:
        pieces = [(cot, cot_edge), (swap_chan(cot), swap_chan(cot_edge))]
    else:
        pieces = [
            (
                lax.all_gather(cot, "chan", axis=1, tiled=True),
                lax.all_gather(cot_edge, "chan", axis=1, tiled=True),
            )
        ]
    cot_side = side_rows(pieces, sub)

    code_weights = conv_two.transpose(0, 2, 1, 3).reshape(3, own, 3 * n_hidden)
    one_own = conv_one.transpose(0, 1, 3, 2)
    if pair:
        split_two = conv_two.reshape(3, 3, own, n_chan, own)
        halves = [split_two[:, :, :, i] for i in range(2)]
        mine = jnp.where(chan == 0, halves[0], halves[1])
        yours = jnp.where(chan == 0, halves[1], halves[0])
        columns = jnp.concatenate([mine, swap_chan(yours)], axis=2)
        one_peer = swap_chan(one_own)
        gain_peer = swap_chan(density_gain)
        one_full = jnp.where(
            chan == 0,
            jnp.concatenate([one_own, one_peer], axis=3),
            jnp.concatenate([one_peer, one_own], axis=3),
        )
        gain = jnp.where(
            chan == 0,
            jnp.concatenate([density_gain, gain_peer]),
            jnp.concatenate([gain_peer, density_gain]),
        )
    else:
        columns = lax.all_to_all(conv_two, "chan", split_axis=3, concat_axis=2, tiled=True)
        one_full = lax.all_gather(one_own, "chan", axis=3, tiled=True)
        gain = lax.all_gather(density_gain, "chan", axis=0, tiled=True)
    back_weights = columns.transpose(0, 3, 1, 2).reshape(3, own, 3 * n_hidden)
    one_weights = one_full.transpose(0, 3, 1, 2).reshape(3, n_hidden, 3 * chans)
    gain = gain[:, None]

    got[0], back_weights, one_weights, code_weights, gain = lax.optimization_barrier(
        (got[0], back_weights, one_weights, code_weights, gain)
    )
    (part,) = grid(got[0], None, False, n_rows, n_cols)
    part, message = grid(got[1], part, True, n_rows, n_cols)
    shape = (n_rows, chans + META, n_cols)
    part = part.reshape(shape)
    message = message.reshape(shape)
    if not pair:
        part = lax.psum(part, "chan")
        density = part[:, chans]
        dense = density.astype(BF16)
        rest = (density - dense.astype(F32)).astype(BF16)
        message = part.astype(BF16).at[:, chans].set(dense).at[:, chans + 1].set(rest)
    low, high = edges(message, 2, n_tile)
    edge = jnp.concatenate([low, high], axis=0)
    if pair:
        peer, peer_edge = swap_chan(message), swap_chan(edge)
        side = side_rows([(message, edge), (peer, peer_edge)], sub)
    else:
        peer, peer_edge = None, None
        side = side_rows([(message, edge)], sub)
    cot_side, _ = lax.optimization_barrier((cot_side, message))
    back_out = back(index, back_weights, pieces, cot_side, n_cols)

    scale = 1.0 / math.sqrt(n_tiles * n_rows * n_cols)
    split = pair and n_tile == 4
    hidden, *partial = grads(
        split, index, one_weights, gain, part, edge, peer, peer_edge, side, cot, back_out
    )
    encoded = encode(code_weights, hidden).transpose(1, 0, 2)

    if split:
        keep, give = partial
        mine, *others = quarters(index, keep, swap_sub(give), n_tile)
        for k, other in enumerate(others, 1):
            mine = mine + swap_tile(other, n_tile, k).astype(F32)
        mine = mine.astype(BF16)
        mine = jnp.stack([mine] + [swap_tile(mine, n_tile, k) for k in range(1, n_tile)])
        grad_two, grad_one, grad_gain = finish(index, mine, swap_sub(mine), scale, own, chans)
        return encoded, grad_one.transpose(0, 1, 3, 2), grad_two, grad_gain[0]

    total = lax.psum(partial[0], ("tile", "sub")) * scale
    three = 3 * own
    half_rows = 3 * chans // 2
    lanes = 3 * n_hidden
    grad_two = total[:three].reshape(3, own, 3, n_hidden).transpose(0, 2, 1, 3)
    lines = total[three : three + half_rows]
    lines = jnp.concatenate([lines[:, :three], lines[:, lanes // 2 : lanes // 2 + three]], axis=0)
    grad_one = lines.reshape(3, chans, 3, own).transpose(2, 0, 3, 1)
    grad_gain = total[three + half_rows, own : 2 * own]
    return encoded, grad_one, grad_two, grad_gain


def solution(mesh):
    placed = (
        P(("member", "tile", "chan", "sub"), None),
        P(("member", "tile", "chan", "sub")),
        P(("member", "tile", "chan", "sub")),
        P(("member", "tile", "chan", "sub")),
        P(None, None, "chan", None),
        P(None, None, "chan", None),
        P("chan"),
        P(("member", "chan"), "tile", "sub"),
    )
    return jax.shard_map(
        body,
        mesh=mesh,
        in_specs=placed,
        out_specs=(
            P(("member", "chan"), "tile", "sub"),
            P("member", None, "chan", None),
            P("member", None, "chan", None),
            P(("member", "chan")),
        ),
        check_vma=False,
    )
```

```python
import functools
import math

import jax
import jax.numpy as jnp
from jax import lax
from jax.experimental import pallas as pl
from jax.experimental.pallas import tpu as pltpu
from jax.sharding import PartitionSpec as P

BF16 = jnp.bfloat16
F32 = jnp.float32
LANES = 128
BLOCK = 256
META = 8
MIB = 1024 * 1024


def dot_nt(a, b):
    return lax.dot_general(a, b, (((1,), (1,)), ((), ())), preferred_element_type=F32)


def dot_nn(a, b):
    return lax.dot_general(a, b, (((1,), (0,)), ((), ())), preferred_element_type=F32)


def iota(shape, dim, dtype=jnp.int32):
    return lax.broadcasted_iota(jnp.int32, shape, dim).astype(dtype)


def vmem_spec():
    return pl.BlockSpec(memory_space=pltpu.VMEM)


def smem_spec():
    return pl.BlockSpec(memory_space=pltpu.SMEM)


def call(kernel, out_shape, in_specs, scratch, flops, moved, name, vmem=48):
    n_out = len(out_shape) if isinstance(out_shape, (tuple, list)) else None
    out_specs = vmem_spec() if n_out is None else [vmem_spec() for _ in range(n_out)]
    return pl.pallas_call(
        kernel,
        out_shape=out_shape,
        in_specs=in_specs,
        out_specs=out_specs,
        scratch_shapes=scratch,
        compiler_params=pltpu.CompilerParams(vmem_limit_bytes=vmem * MIB),
        cost_estimate=pl.CostEstimate(flops=flops, bytes_accessed=moved, transcendentals=0),
        name=name,
    )


def route_kernel(n_tiles, cap, relative, index_ref, tile_hbm, weight_hbm, cell_hbm, values_hbm, *rest):
    n_outs = 5 if relative else 1
    outs = rest[:n_outs]
    (tile_ref, weight_ref, cell_ref, values_ref, onehot_ref, slot_ref, weight32_ref, all_ref,
     info_ref, info_smem, sems) = rest[n_outs:]
    loads = [
        pltpu.make_async_copy(tile_hbm, tile_ref, sems.at[0]),
        pltpu.make_async_copy(weight_hbm, weight_ref, sems.at[1]),
        pltpu.make_async_copy(cell_hbm, cell_ref, sems.at[2]),
        pltpu.make_async_copy(values_hbm, values_ref, sems.at[3]),
    ]
    for load in loads:
        load.start()
    all_ref[...] = jnp.zeros(all_ref.shape, BF16)
    loads[0].wait()
    n_lines = tile_ref.shape[0]
    n_blocks = n_lines // 2
    n_obs_chans = values_ref.shape[0]
    pairs = n_tiles * n_lines
    tiles = tile_ref[...]
    for t in range(n_tiles):
        onehot_ref[t * n_lines : (t + 1) * n_lines, :] = jnp.where(tiles == t, 1.0, 0.0).astype(BF16)
    onehot = onehot_ref[...]
    upper = jnp.where(
        iota((LANES, LANES), 0) <= iota((LANES, LANES), 1), 1.0, 0.0
    ).astype(BF16)
    here = iota((pairs, pairs), 0)
    there = iota((pairs, pairs), 1)
    earlier = jnp.where(
        (here // n_lines == there // n_lines) & (there < here), 1.0, 0.0
    ).astype(BF16)
    total_row = dot_nt(jnp.ones((8, LANES), BF16), onehot)
    offset_row = dot_nt(total_row.astype(BF16), earlier)
    base_row = jnp.minimum(jnp.floor(offset_row * (1.0 / LANES)) * LANES, float(cap - BLOCK))
    even = iota((8, pairs), 1) % 2 == 0
    base_pair = jnp.where(even, base_row, pltpu.roll(base_row, 1, 1))
    spill = jnp.where(offset_row + total_row > base_pair + BLOCK, 1.0, 0.0)
    any_spill = jnp.max(spill, axis=1, keepdims=True)
    info_ref[...] = jnp.where(
        iota((8, pairs), 0) == 0, base_row, any_spill
    ).astype(jnp.int32)
    copy = pltpu.make_async_copy(info_ref, info_smem, sems.at[4])
    copy.start()
    cum = dot_nn(onehot, upper)
    totals = dot_nn(onehot, jnp.ones((LANES, LANES), BF16))
    offset = dot_nn(earlier, totals.astype(BF16))
    place = cum + offset - 1.0
    slots = jnp.zeros(tiles.shape, F32)
    for t in range(n_tiles):
        slots = jnp.where(tiles == t, place[t * n_lines : (t + 1) * n_lines, :], slots)
    slot_ref[...] = slots
    for load in loads[1:]:
        load.wait()
    weight32_ref[...] = weight_ref[...].astype(F32)
    meta_row = iota((16, BLOCK), 0)
    window = iota((BLOCK, BLOCK), 0, F32)
    copy.wait()

    def line(ref, b):
        return jnp.concatenate([ref[pl.ds(2 * b, 1), :], ref[pl.ds(2 * b + 1, 1), :]], axis=1)

    def columns(b):
        values = values_ref[:, pl.ds(pl.multiple_of(b * BLOCK, BLOCK), BLOCK)]
        cell = line(cell_ref, b)
        weight = line(weight32_ref, b)
        high = (cell // LANES).astype(F32)
        low = (cell % LANES).astype(F32)
        meta = jnp.where(
            meta_row == 0,
            weight,
            jnp.where(meta_row == 1, high, jnp.where(meta_row == 2, low, 0.0)),
        ).astype(BF16)
        return jnp.concatenate([values, meta], axis=0)

    def add(t, base, wide, key):
        chosen = jnp.where(window == key, 1.0, 0.0).astype(BF16)
        part = dot_nt(wide, chosen)[: n_obs_chans + META].astype(BF16)
        where = pl.ds(pl.multiple_of(base, LANES), BLOCK)
        all_ref[t, :, where] = all_ref[t, :, where] + part

    def first(b):
        wide = columns(b)
        tile = line(tile_ref, b)
        slot = line(slot_ref, b)
        for t in range(n_tiles):
            base = info_smem[0, t * n_lines + 2 * b]
            key = jnp.where(tile == t, slot - base.astype(F32), -1.0)
            add(t, base, wide, key)

    def first_two(i, carry):
        first(2 * i)
        first(2 * i + 1)
        return carry

    lax.fori_loop(0, n_blocks // 2, first_two, 0)

    if cap > BLOCK:

        @pl.when(info_smem[1, 0] > 0)
        def _():
            def second(b, carry):
                wide = columns(b)
                tile = line(tile_ref, b)
                slot = line(slot_ref, b)
                for t in range(n_tiles):
                    start = info_smem[0, t * n_lines + 2 * b]
                    base = jnp.minimum(start + BLOCK, cap - BLOCK)
                    far = (tile == t) & (slot >= (start + BLOCK).astype(F32))
                    key = jnp.where(far, slot - base.astype(F32), -1.0)
                    add(t, base, wide, key)
                return carry

            lax.fori_loop(0, n_blocks, second, 0)

    if relative:
        me = index_ref[4]
        outs[0][0] = all_ref[me]
        outs[1][0] = all_ref[jnp.bitwise_xor(me, 1)]
        for k in range(1, 4):
            for s in range(2):
                outs[k + 1][s] = all_ref[jnp.bitwise_xor(me, 2 * k + s)]
    else:
        outs[0][...] = all_ref[...]


def route(index, obs_values, obs_weight, obs_tile, obs_cell, n_tiles, cap, relative):
    n_obs, chans = obs_values.shape
    n_lines = n_obs // LANES
    rows = chans + META
    outs = [(n, rows, cap) for n in ((1, 1, 2, 2, 2) if relative else (n_tiles,))]
    hbm_spec = pl.BlockSpec(memory_space=pltpu.HBM)
    return call(
        functools.partial(route_kernel, n_tiles, cap, relative),
        [jax.ShapeDtypeStruct(shape, BF16) for shape in outs],
        [smem_spec()] + [hbm_spec] * 4,
        [
            pltpu.VMEM((n_lines, LANES), jnp.int32),
            pltpu.VMEM((n_lines, LANES), BF16),
            pltpu.VMEM((n_lines, LANES), jnp.int32),
            pltpu.VMEM((chans, n_obs), BF16),
            pltpu.VMEM((n_tiles * n_lines, LANES), BF16),
            pltpu.VMEM((n_lines, LANES), F32),
            pltpu.VMEM((n_lines, LANES), F32),
            pltpu.VMEM((n_tiles, rows, cap), BF16),
            pltpu.VMEM((8, n_tiles * n_lines), jnp.int32),
            pltpu.SMEM((8, n_tiles * n_lines), jnp.int32),
            pltpu.SemaphoreType.DMA((5,)),
        ],
        2 * n_obs * n_tiles * BLOCK * 80,
        n_tiles * rows * cap * 2,
        "route",
        24,
    )(
        index,
        obs_tile.reshape(n_lines, LANES),
        obs_weight.reshape(n_lines, LANES),
        obs_cell.reshape(n_lines, LANES),
        obs_values.T,
    )


def grid_kernel(n_rows, n_cols, group, takes, first, last, *rest):
    rest = list(rest)
    got_refs = [rest.pop(0) for _ in takes]
    senders = [ref.at[i] for ref, n in zip(got_refs, takes) for i in range(n)]
    before_ref = None if first else rest.pop(0)
    own_ref = rest.pop(0)
    send_ref = rest.pop(0) if last else None
    left_ref, right_ref = rest
    n_send = len(senders)
    rows, cap = senders[0].shape
    chans = rows - META
    per_row = n_cols // LANES
    columns = iota((n_cols, cap), 0, F32)
    row_ids = iota((META, cap), 0)
    total = None
    for g in range(n_send // group):
        slot = g % 2
        for i in range(group):
            s = g * group + i
            at = slice(i * cap, (i + 1) * cap)
            values = senders[s][0:chans, :]
            meta = senders[s][chans:rows, :].astype(F32)
            weight = meta[0:1]
            high = meta[1:2]
            row = jnp.floor((high + 0.5) * (1.0 / per_row))
            column = (high - row * per_row) * LANES + meta[2:3]
            right_ref[slot, :, at] = jnp.where(columns == column, weight, 0.0).astype(BF16)
            for r in range(n_rows):
                mask = jnp.where(row == r, 1.0, 0.0)
                left_ref[slot, r * rows : r * rows + chans, at] = values * mask.astype(BF16)
                left_ref[slot, r * rows + chans : (r + 1) * rows, at] = jnp.where(
                    row_ids == 0, mask, 0.0
                ).astype(BF16)
        part = dot_nt(left_ref[slot], right_ref[slot])
        total = part if total is None else total + part
    if before_ref is not None:
        total = total + before_ref[...]
    own_ref[...] = total
    if last:
        line = iota((META, n_cols), 0)
        for r in range(n_rows):
            send_ref[r * rows : r * rows + chans, :] = own_ref[r * rows : r * rows + chans, :].astype(BF16)
            extra = own_ref[r * rows + chans : (r + 1) * rows, :]
            density = extra[0:1]
            high = density.astype(BF16).astype(F32)
            send_ref[r * rows + chans : (r + 1) * rows, :] = jnp.where(
                line == 0, high, jnp.where(line == 1, density - high, 0.0)
            ).astype(BF16)


def grid(got, before, last, n_rows, n_cols):
    takes = [n for _, n in got]
    got = [x for x, _ in got]
    n_send = sum(takes)
    rows, cap = got[0].shape[1:]
    group = max(1, min(2048 // cap, n_send))
    total = n_rows * rows
    outs = [jax.ShapeDtypeStruct((total, n_cols), F32)]
    if last:
        outs.append(jax.ShapeDtypeStruct((total, n_cols), BF16))
    ins = list(got) if before is None else list(got) + [before]
    return call(
        functools.partial(grid_kernel, n_rows, n_cols, group, takes, before is None, last),
        outs,
        [vmem_spec()] * len(ins),
        [
            pltpu.VMEM((2, total, group * cap), BF16),
            pltpu.VMEM((2, n_cols, group * cap), BF16),
        ],
        2 * n_send * cap * total * n_cols,
        n_send * rows * cap * 2,
        "grid_last" if last else "grid_part",
        32,
    )(*ins)


def lane_mask(shape, n_cols, sub, depth):
    lane = iota(shape, 1)
    width = n_cols + LANES
    keep_right = (lane >= n_cols) & (lane < n_cols + depth) & (sub == 0)
    keep_left = (lane >= width - depth) & (sub == 1)
    return (lane < n_cols) | keep_right | keep_left


def back_kernel(n_cols, n_pieces, index_ref, kernel_ref, *rest):
    pieces = [(rest[2 * i], rest[2 * i + 1]) for i in range(n_pieces)]
    side_ref, out_ref, wide_ref = rest[2 * n_pieces :]
    n_ext, all_chans = side_ref.shape[0], side_ref.shape[1]
    n_rows = n_ext - 2
    width = n_cols + LANES
    keep = lane_mask((1, width), n_cols, index_ref[2], 1)
    for h in range(n_ext):
        if h == 0 or h == n_ext - 1:
            mids = [edge[min(h, 1)] for _, edge in pieces]
        else:
            mids = [middle[h - 1] for middle, _ in pieces]
        mid = mids[0] if n_pieces == 1 else jnp.concatenate(mids, axis=0)
        ext = jnp.concatenate([mid, side_ref[h]], axis=1).astype(F32)
        ext = jnp.where(keep, ext, 0.0)
        at = slice(h * n_cols, (h + 1) * n_cols)
        wide_ref[0:all_chans, at] = pltpu.roll(ext, width - 1, 1)[:, :n_cols].astype(BF16)
        wide_ref[all_chans : 2 * all_chans, at] = mid
        wide_ref[2 * all_chans :, at] = pltpu.roll(ext, 1, 1)[:, :n_cols].astype(BF16)
    total = None
    for a in range(3):
        at = slice((2 - a) * n_cols, (2 - a + n_rows) * n_cols)
        part = dot_nn(kernel_ref[a], wide_ref[:, at])
        total = part if total is None else total + part
    out_ref[...] = total


def back(index, kernel, pieces, side, n_cols):
    n_ext, all_chans = side.shape[0], side.shape[1]
    n_out = kernel.shape[1]
    return call(
        functools.partial(back_kernel, n_cols, len(pieces)),
        jax.ShapeDtypeStruct((n_out, (n_ext - 2) * n_cols), F32),
        [smem_spec()] + [vmem_spec()] * (2 + 2 * len(pieces)),
        [pltpu.VMEM((3 * all_chans, n_ext * n_cols), BF16)],
        2 * n_ext * 9 * all_chans * n_out * n_cols,
        n_ext * all_chans * n_cols * 2,
        "back",
        32,
    )(index, kernel, *[x for piece in pieces for x in piece], side)


def grads_kernel(
    split, chans, index_ref, kernel_ref, gain_ref, own_ref, edge_ref, peer_ref, peer_edge_ref,
    side_ref, cot_ref, back_ref, hidden_ref, *rest,
):
    rest = list(rest)
    if split:
        keep_out, give_out = rest.pop(0), rest.pop(0)
    else:
        all_out = rest.pop(0)
    taps_ref, logs_ref, pre_ref, wide_ref, out_left_ref, pre_left_ref, acc_ref = rest
    n_rows, own, n_cols = cot_ref.shape
    n_hidden = kernel_ref.shape[1]
    rows = chans + META
    taps_rows = 3 * chans
    width = n_cols + LANES
    tile, chan, sub, n_tile = index_ref[0], index_ref[1], index_ref[2], index_ref[3]
    keep_two = lane_mask((1, width), n_cols, sub, 2)

    log_line = iota((16, width), 0)
    for i in range(n_rows + 4):
        if 2 <= i < n_rows + 2:
            mid = own_ref[i - 2]
            if peer_ref is not None:
                mid = mid + peer_ref[i - 2].astype(F32)
        else:
            e = i if i < 2 else i - n_rows
            mid = edge_ref[e].astype(F32)
            if peer_ref is not None:
                mid = mid + peer_edge_ref[e].astype(F32)
        side = side_ref[i, 0:rows].astype(F32)
        if peer_ref is not None:
            side = side + side_ref[i, rows : 2 * rows].astype(F32)
        ext = jnp.concatenate([mid, side], axis=1)
        density = ext[chans : chans + 1] + ext[chans + 1 : chans + 2]
        logs = jnp.log(1.0 + density)
        logs_ref[i] = logs
        shrink = jnp.where(keep_two, 1.0 / (1.0 + density), 0.0)
        feats = ext[0:chans] * shrink
        at = slice(i * width, (i + 1) * width)
        taps_ref[0:chans, at] = pltpu.roll(feats, 1, 1).astype(BF16)
        taps_ref[chans : 2 * chans, at] = feats.astype(BF16)
        taps_ref[2 * chans : taps_rows, at] = pltpu.roll(feats, width - 1, 1).astype(BF16)
        high = logs.astype(BF16).astype(F32)
        middle = (logs - high).astype(BF16).astype(F32)
        taps_ref[taps_rows:, at] = jnp.where(
            log_line == 0,
            high,
            jnp.where(log_line == 1, middle, jnp.where(log_line == 2, logs - high - middle, 0.0)),
        ).astype(BF16)

    nothing = jnp.zeros((own, n_cols), BF16)
    for h in range(n_rows + 2):
        for a in range(3):
            inside = 0 <= h - a < n_rows
            put = slice(a * own, (a + 1) * own)
            out_left_ref[put, h * n_cols : (h + 1) * n_cols] = cot_ref[h - a] if inside else nothing
            if not inside:
                pre_left_ref[put, h * width : h * width + n_cols] = nothing
        pre_left_ref[:, h * width + n_cols : (h + 1) * width] = jnp.zeros((3 * own, LANES), BF16)

    gain = gain_ref[...]
    keep_one = lane_mask((1, width), n_cols, sub, 1)
    group = 2
    for first in range(0, n_rows + 2, group):
        pre_all = None
        for a in range(3):
            at = slice((first + a) * width, (first + a + group) * width)
            part = dot_nn(kernel_ref[a], taps_ref[0:taps_rows, at])
            pre_all = part if pre_all is None else pre_all + part
        for k in range(group):
            h = first + k
            pre = pre_all[:, k * width : (k + 1) * width] + gain * logs_ref[h + 1]
            at = slice(h * n_cols, (h + 1) * n_cols)
            keep = keep_one
            if h == 0:
                keep = keep & (tile > 0)
            elif h == n_rows + 1:
                keep = keep & (tile < n_tile - 1)
            else:
                pre_ref[:, (h - 1) * n_cols : h * n_cols] = pre[:, :n_cols]
            half = 0.5 * pre
            hidden = jnp.where(keep, half + half * jnp.tanh(half), 0.0)
            hidden_ref[h] = hidden.astype(BF16)
            wide_ref[0:n_hidden, at] = pltpu.roll(hidden, 1, 1)[:, :n_cols].astype(BF16)
            wide_ref[n_hidden : 2 * n_hidden, at] = hidden[:, :n_cols].astype(BF16)
            wide_ref[2 * n_hidden :, at] = pltpu.roll(hidden, width - 1, 1)[:, :n_cols].astype(BF16)

    for r in range(n_rows):
        at = slice(r * n_cols, (r + 1) * n_cols)
        mine = pre_ref[pl.ds(pl.multiple_of(chan * own, own), own), at]
        s = 0.5 + 0.5 * jnp.tanh(0.5 * mine)
        grad = (back_ref[:, at] * s * (1.0 + mine * (1.0 - s))).astype(BF16)
        for a in range(3):
            h = r + a
            pre_left_ref[a * own : (a + 1) * own, h * width : h * width + n_cols] = grad

    three = 3 * own
    lanes = 3 * n_hidden
    half_rows = taps_rows // 2
    acc_ref[0:three, :] = dot_nt(out_left_ref[...], wide_ref[...])
    one = dot_nt(taps_ref[:, width : (n_rows + 3) * width], pre_left_ref[...])
    acc_ref[three:, :] = jnp.zeros((acc_ref.shape[0] - three, lanes), F32)
    acc_ref[three : three + half_rows, 0:three] = one[0:half_rows]
    acc_ref[three : three + half_rows, lanes // 2 : lanes // 2 + three] = one[half_rows:taps_rows]
    gains = one[taps_rows : taps_rows + 1] + one[taps_rows + 1 : taps_rows + 2] + one[taps_rows + 2 : taps_rows + 3]
    acc_ref[three + half_rows : three + half_rows + 1, 0:three] = gains
    if split:
        half = acc_ref.shape[0] // 2
        keep_out[...] = acc_ref[pl.ds(pl.multiple_of(sub * half, half), half), :]
        give_out[...] = acc_ref[pl.ds(pl.multiple_of((1 - sub) * half, half), half), :].astype(BF16)
    else:
        all_out[...] = acc_ref[...]


def grads(split, index, kernel, gain, own, edge, peer, peer_edge, side, cot, back_out):
    n_rows, n_own, n_cols = cot.shape
    n_hidden = kernel.shape[1]
    chans = kernel.shape[2] // 3
    width = n_cols + LANES
    lanes = 3 * n_hidden
    acc_rows = 3 * n_own + 3 * chans // 2 + 32
    body = functools.partial(grads_kernel, split, chans)
    ins = [own, edge, peer, peer_edge, side, cot, back_out]
    if peer is None:
        ins = [own, edge, side, cot, back_out]
        body = lambda i, k, g, o, e, *rest: grads_kernel(split, chans, i, k, g, o, e, None, None, *rest)
    outs = [jax.ShapeDtypeStruct((n_rows + 2, n_hidden, width), BF16)]
    if split:
        outs.append(jax.ShapeDtypeStruct((acc_rows // 2, lanes), F32))
        outs.append(jax.ShapeDtypeStruct((acc_rows // 2, lanes), BF16))
    else:
        outs.append(jax.ShapeDtypeStruct((acc_rows, lanes), F32))
    return call(
        body,
        outs,
        [smem_spec()] + [vmem_spec()] * (2 + len(ins)),
        [
            pltpu.VMEM((3 * chans + 16, (n_rows + 4) * width), BF16),
            pltpu.VMEM((n_rows + 4, 1, width), F32),
            pltpu.VMEM((n_hidden, n_rows * n_cols), F32),
            pltpu.VMEM((3 * n_hidden, (n_rows + 2) * n_cols), BF16),
            pltpu.VMEM((3 * n_own, (n_rows + 2) * n_cols), BF16),
            pltpu.VMEM((3 * n_own, (n_rows + 2) * width), BF16),
            pltpu.VMEM((acc_rows, lanes), F32),
        ],
        2 * (n_rows + 2) * 9 * n_cols * n_hidden * (n_own + chans),
        (n_rows + 2) * 3 * n_hidden * n_cols * 2,
        "grads",
        50,
    )(index, kernel, gain, *ins)


def encode_kernel(kernel_ref, hidden_ref, out_ref, wide_ref):
    n_ext, n_hidden, width = hidden_ref.shape
    n_rows = n_ext - 2
    n_cols = width - LANES
    for h in range(n_ext):
        hidden = hidden_ref[h].astype(F32)
        at = slice(h * n_cols, (h + 1) * n_cols)
        wide_ref[0:n_hidden, at] = pltpu.roll(hidden, 1, 1)[:, :n_cols].astype(BF16)
        wide_ref[n_hidden : 2 * n_hidden, at] = hidden_ref[h, :, 0:n_cols]
        wide_ref[2 * n_hidden :, at] = pltpu.roll(hidden, width - 1, 1)[:, :n_cols].astype(BF16)
    total = None
    for a in range(3):
        part = dot_nn(kernel_ref[a], wide_ref[:, a * n_cols : (a + n_rows) * n_cols])
        total = part if total is None else total + part
    for r in range(n_rows):
        out_ref[r] = total[:, r * n_cols : (r + 1) * n_cols].astype(BF16)


def encode(kernel, hidden):
    n_ext, n_hidden, width = hidden.shape
    own = kernel.shape[1]
    n_cols = width - LANES
    return call(
        encode_kernel,
        jax.ShapeDtypeStruct((n_ext - 2, own, n_cols), BF16),
        [vmem_spec()] * 2,
        [pltpu.VMEM((3 * n_hidden, n_ext * n_cols), BF16)],
        2 * n_ext * 9 * own * n_hidden * n_cols,
        hidden.size * 2,
        "encode",
        32,
    )(kernel, hidden)


def quarters_kernel(index_ref, keep_ref, got_ref, *outs):
    n = len(outs)
    rows = keep_ref.shape[0] // n
    for k in range(n):
        other = jnp.bitwise_xor(index_ref[0], k)
        at = pl.ds(pl.multiple_of(other * rows, rows), rows)
        outs[k][...] = (keep_ref[at, :] + got_ref[at, :].astype(F32)).astype(outs[k].dtype)


def quarters(index, keep, got, n):
    rows, lanes = keep.shape
    return call(
        quarters_kernel,
        [jax.ShapeDtypeStruct((rows // n, lanes), F32 if k == 0 else BF16) for k in range(n)],
        [smem_spec(), vmem_spec(), vmem_spec()],
        [],
        rows * lanes,
        rows * lanes * 8,
        "quarters",
        16,
    )(index, keep, got)


def finish_kernel(scale, own, chans, index_ref, mine_ref, other_ref, two_ref, one_ref, gain_ref, all_ref):
    n, rows, lanes = mine_ref.shape
    n_hidden = lanes // 3
    tile, sub = index_ref[0], index_ref[2]
    for k in range(n):
        at = jnp.bitwise_xor(tile, k) * rows
        here = pl.multiple_of(sub * (n * rows) + at, rows)
        there = pl.multiple_of((1 - sub) * (n * rows) + at, rows)
        all_ref[pl.ds(here, rows), :] = mine_ref[k].astype(F32) * scale
        all_ref[pl.ds(there, rows), :] = other_ref[k].astype(F32) * scale
    half_rows = 3 * chans // 2
    for a in range(3):
        for b in range(3):
            two_ref[a, b] = all_ref[a * own : (a + 1) * own, b * n_hidden : (b + 1) * n_hidden]
        lines = jnp.concatenate(
            [
                all_ref[3 * own : 3 * own + half_rows, s + a * own : s + (a + 1) * own]
                for s in (0, lanes // 2)
            ],
            axis=0,
        )
        for b in range(3):
            one_ref[a, b] = lines[b * chans : (b + 1) * chans]
    gain_ref[...] = all_ref[3 * own + half_rows : 3 * own + half_rows + 1, own : 2 * own]


def finish(index, mine, other, scale, own, chans):
    n, rows, lanes = mine.shape
    n_hidden = lanes // 3
    return call(
        functools.partial(finish_kernel, scale, own, chans),
        [
            jax.ShapeDtypeStruct((3, 3, own, n_hidden), F32),
            jax.ShapeDtypeStruct((3, 3, chans, own), F32),
            jax.ShapeDtypeStruct((1, own), F32),
        ],
        [smem_spec(), vmem_spec(), vmem_spec()],
        [pltpu.VMEM((2 * n * rows, lanes), F32)],
        n * rows * lanes,
        n * rows * lanes * 12,
        "finish",
        24,
    )(index, mine, other)


def step_perm(count, by):
    return [(i, i + by) for i in range(count) if 0 <= i + by < count]


def swap_sub(x):
    return lax.ppermute(x, "sub", [(0, 1), (1, 0)])


def swap_chan(x):
    return lax.ppermute(x, "chan", [(0, 1), (1, 0)])


def swap_tile(x, n_tile, k):
    return lax.ppermute(x, "tile", [(i, i ^ k) for i in range(n_tile)])


def edges(block, depth, n_tile):
    low = lax.ppermute(block[-depth:], "tile", step_perm(n_tile, 1))
    high = lax.ppermute(block[:depth], "tile", step_perm(n_tile, -1))
    return low, high


def near(block, sub):
    n_cols = block.shape[-1]
    return jnp.where(sub == 0, block[..., n_cols - LANES :], block[..., :LANES])


def side_rows(parts, sub):
    columns = [
        jnp.concatenate([near(edge[: edge.shape[0] // 2], sub), near(mid, sub), near(edge[edge.shape[0] // 2 :], sub)], axis=0)
        for mid, edge in parts
    ]
    both = columns[0] if len(columns) == 1 else jnp.concatenate(columns, axis=1)
    return swap_sub(both)


def body(obs_values, obs_weight, obs_tile, obs_cell, conv_one, conv_two, density_gain, cotangent):
    own, n_rows, n_cols = cotangent.shape
    n_tile = lax.axis_size("tile")
    n_sub = lax.axis_size("sub")
    n_chan = lax.axis_size("chan")
    pair = n_chan == 2
    n_tiles = n_tile * n_sub
    chans = obs_values.shape[1]
    n_hidden = own * n_chan
    cap = 2 * obs_values.shape[0] // n_tiles
    tile, chan, sub = lax.axis_index("tile"), lax.axis_index("chan"), lax.axis_index("sub")
    index = jnp.stack([tile, chan, sub, jnp.int32(n_tile), tile * n_sub + sub]).astype(jnp.int32)

    bottom, top = cotangent[:, -1], cotangent[:, 0]
    obs_tile, bottom, top = lax.optimization_barrier((obs_tile, bottom, top))
    cot_edge = jnp.stack(
        [
            lax.ppermute(bottom, "tile", step_perm(n_tile, 1)),
            lax.ppermute(top, "tile", step_perm(n_tile, -1)),
        ]
    )
    cot = cotangent.transpose(1, 0, 2)
    if pair:
        cot_peer = swap_chan(cotangent).transpose(1, 0, 2)
        pieces = [(cot, cot_edge), (cot_peer, swap_chan(cot_edge))]
    else:
        pieces = [
            (
                lax.all_gather(cot, "chan", axis=1, tiled=True),
                lax.all_gather(cot_edge, "chan", axis=1, tiled=True),
            )
        ]
    cot_side = side_rows(pieces, sub)

    few = n_tiles == 8
    sent = route(index, obs_values, obs_weight, obs_tile, obs_cell, n_tiles, cap, few)
    if few:
        far = [swap_tile(sent[k + 1], n_tile, k) for k in (1, 2, 3)]
        steps = [
            [(sent[0], 1), (swap_sub(sent[1]), 1), (far[0], 1), (swap_sub(far[0][1:]), 1)],
            [(far[1], 1), (far[2], 1)],
            [(swap_sub(far[1][1:]), 1), (swap_sub(far[2][1:]), 1)],
        ]
    else:
        got = lax.all_to_all(sent[0], ("tile", "sub"), split_axis=0, concat_axis=0, tiled=True)
        steps = [[(got, n_tiles)]]

    conv_one, conv_two, density_gain, _ = lax.optimization_barrier(
        (conv_one, conv_two, density_gain, sent[0])
    )
    code_weights = conv_two.transpose(0, 2, 1, 3).reshape(3, own, 3 * n_hidden)
    one_own = conv_one.transpose(0, 1, 3, 2)
    if pair:
        split_two = conv_two.reshape(3, 3, own, n_chan, own)
        halves = [split_two[:, :, :, i] for i in range(2)]
        mine = jnp.where(chan == 0, halves[0], halves[1])
        yours = jnp.where(chan == 0, halves[1], halves[0])
        columns = jnp.concatenate([mine, swap_chan(yours)], axis=2)
        one_peer = swap_chan(one_own)
        gain_peer = swap_chan(density_gain)
        one_full = jnp.where(
            chan == 0,
            jnp.concatenate([one_own, one_peer], axis=3),
            jnp.concatenate([one_peer, one_own], axis=3),
        )
        gain = jnp.where(
            chan == 0,
            jnp.concatenate([density_gain, gain_peer]),
            jnp.concatenate([gain_peer, density_gain]),
        )
    else:
        columns = lax.all_to_all(conv_two, "chan", split_axis=3, concat_axis=2, tiled=True)
        one_full = lax.all_gather(one_own, "chan", axis=3, tiled=True)
        gain = lax.all_gather(density_gain, "chan", axis=0, tiled=True)
    back_weights = columns.transpose(0, 3, 1, 2).reshape(3, own, 3 * n_hidden)
    one_weights = one_full.transpose(0, 3, 1, 2).reshape(3, n_hidden, 3 * chans)
    gain = gain[:, None]

    part = None
    for step in steps[:-1]:
        part = grid(step, part, False, n_rows, n_cols)[0]
    part, message = grid(steps[-1], part, True, n_rows, n_cols)
    shape = (n_rows, chans + META, n_cols)
    part = part.reshape(shape)
    message = message.reshape(shape)
    if not pair:
        part = lax.psum(part, "chan")
        density = part[:, chans]
        dense = density.astype(BF16)
        rest = (density - dense.astype(F32)).astype(BF16)
        message = part.astype(BF16).at[:, chans].set(dense).at[:, chans + 1].set(rest)
    low, high = edges(message, 2, n_tile)
    edge = jnp.concatenate([low, high], axis=0)
    back_out = back(index, back_weights, pieces, cot_side, n_cols)
    if pair:
        peer, peer_edge = swap_chan(message), swap_chan(edge)
        peer_edge, back_out = lax.optimization_barrier((peer_edge, back_out))
        side = side_rows([(message, edge), (peer, peer_edge)], sub)
    else:
        peer, peer_edge = None, None
        side = side_rows([(message, edge)], sub)

    scale = 1.0 / math.sqrt(n_tiles * n_rows * n_cols)
    split = pair and n_tile == 4
    hidden, *partial = grads(
        split, index, one_weights, gain, part, edge, peer, peer_edge, side, cot, back_out
    )
    encoded = encode(code_weights, hidden).transpose(1, 0, 2)

    if split:
        keep, give = partial
        mine, *others = quarters(index, keep, swap_sub(give), n_tile)
        for k, other in enumerate(others, 1):
            mine = mine + swap_tile(other, n_tile, k).astype(F32)
        mine, encoded = lax.optimization_barrier((mine.astype(BF16), encoded))
        mine = jnp.stack([mine] + [swap_tile(mine, n_tile, k) for k in range(1, n_tile)])
        grad_two, grad_one, grad_gain = finish(index, mine, swap_sub(mine), scale, own, chans)
        return encoded, grad_one.transpose(0, 1, 3, 2), grad_two, grad_gain[0]

    total = lax.psum(partial[0], ("tile", "sub")) * scale
    three = 3 * own
    half_rows = 3 * chans // 2
    lanes = 3 * n_hidden
    grad_two = total[:three].reshape(3, own, 3, n_hidden).transpose(0, 2, 1, 3)
    lines = total[three : three + half_rows]
    lines = jnp.concatenate([lines[:, :three], lines[:, lanes // 2 : lanes // 2 + three]], axis=0)
    grad_one = lines.reshape(3, chans, 3, own).transpose(2, 0, 3, 1)
    grad_gain = total[three + half_rows, own : 2 * own]
    return encoded, grad_one, grad_two, grad_gain


def solution(mesh):
    placed = (
        P(("member", "tile", "chan", "sub"), None),
        P(("member", "tile", "chan", "sub")),
        P(("member", "tile", "chan", "sub")),
        P(("member", "tile", "chan", "sub")),
        P(None, None, "chan", None),
        P(None, None, "chan", None),
        P("chan"),
        P(("member", "chan"), "tile", "sub"),
    )
    return jax.shard_map(
        body,
        mesh=mesh,
        in_specs=placed,
        out_specs=(
            P(("member", "chan"), "tile", "sub"),
            P("member", None, "chan", None),
            P("member", None, "chan", None),
            P(("member", "chan")),
        ),
        check_vma=False,
    )
```

```python
import functools
import math

import jax
import jax.numpy as jnp
from jax import lax
from jax.experimental import pallas as pl
from jax.experimental.pallas import tpu as pltpu
from jax.sharding import PartitionSpec as P

BF16 = jnp.bfloat16
F32 = jnp.float32
LANES = 128
BLOCK = 256
META = 8
MIB = 1024 * 1024


def dot_nt(a, b):
    return lax.dot_general(a, b, (((1,), (1,)), ((), ())), preferred_element_type=F32)


def dot_nn(a, b):
    return lax.dot_general(a, b, (((1,), (0,)), ((), ())), preferred_element_type=F32)


def iota(shape, dim, dtype=jnp.int32):
    return lax.broadcasted_iota(jnp.int32, shape, dim).astype(dtype)


def vmem_spec():
    return pl.BlockSpec(memory_space=pltpu.VMEM)


def smem_spec():
    return pl.BlockSpec(memory_space=pltpu.SMEM)


def call(kernel, out_shape, in_specs, scratch, flops, moved, name, vmem=32):
    n_out = len(out_shape) if isinstance(out_shape, (tuple, list)) else None
    out_specs = vmem_spec() if n_out is None else [vmem_spec() for _ in range(n_out)]
    return pl.pallas_call(
        kernel,
        out_shape=out_shape,
        in_specs=in_specs,
        out_specs=out_specs,
        scratch_shapes=scratch,
        compiler_params=pltpu.CompilerParams(vmem_limit_bytes=vmem * MIB),
        cost_estimate=pl.CostEstimate(flops=flops, bytes_accessed=moved, transcendentals=0),
        name=name,
    )


def route_kernel(n_tiles, cap, relative, index_ref, tile_hbm, weight_hbm, cell_hbm, values_hbm, *rest):
    n_outs = 5 if relative else 1
    outs = rest[:n_outs]
    (tile_ref, weight_ref, cell_ref, values_ref, onehot_ref, slot_ref, weight32_ref, all_ref,
     info_ref, info_smem, sems) = rest[n_outs:]
    loads = [
        pltpu.make_async_copy(tile_hbm, tile_ref, sems.at[0]),
        pltpu.make_async_copy(weight_hbm, weight_ref, sems.at[1]),
        pltpu.make_async_copy(cell_hbm, cell_ref, sems.at[2]),
        pltpu.make_async_copy(values_hbm, values_ref, sems.at[3]),
    ]
    for load in loads:
        load.start()
    all_ref[...] = jnp.zeros(all_ref.shape, BF16)
    loads[0].wait()
    n_lines = tile_ref.shape[0]
    n_blocks = n_lines // 2
    n_obs_chans = values_ref.shape[0]
    pairs = n_tiles * n_lines
    tiles = tile_ref[...]
    for t in range(n_tiles):
        onehot_ref[t * n_lines : (t + 1) * n_lines, :] = jnp.where(tiles == t, 1.0, 0.0).astype(BF16)
    onehot = onehot_ref[...]
    upper = jnp.where(
        iota((LANES, LANES), 0) <= iota((LANES, LANES), 1), 1.0, 0.0
    ).astype(BF16)
    here = iota((pairs, pairs), 0)
    there = iota((pairs, pairs), 1)
    earlier = jnp.where(
        (here // n_lines == there // n_lines) & (there < here), 1.0, 0.0
    ).astype(BF16)
    total_row = dot_nt(jnp.ones((8, LANES), BF16), onehot)
    offset_row = dot_nt(total_row.astype(BF16), earlier)
    base_row = jnp.minimum(jnp.floor(offset_row * (1.0 / LANES)) * LANES, float(cap - BLOCK))
    even = iota((8, pairs), 1) % 2 == 0
    base_pair = jnp.where(even, base_row, pltpu.roll(base_row, 1, 1))
    spill = jnp.where(offset_row + total_row > base_pair + BLOCK, 1.0, 0.0)
    any_spill = jnp.max(spill, axis=1, keepdims=True)
    info_ref[...] = jnp.where(
        iota((8, pairs), 0) == 0, base_row, any_spill
    ).astype(jnp.int32)
    copy = pltpu.make_async_copy(info_ref, info_smem, sems.at[4])
    copy.start()
    cum = dot_nn(onehot, upper)
    totals = dot_nn(onehot, jnp.ones((LANES, LANES), BF16))
    offset = dot_nn(earlier, totals.astype(BF16))
    place = cum + offset - 1.0
    slots = jnp.zeros(tiles.shape, F32)
    for t in range(n_tiles):
        slots = jnp.where(tiles == t, place[t * n_lines : (t + 1) * n_lines, :], slots)
    slot_ref[...] = slots
    for load in loads[1:]:
        load.wait()
    weight32_ref[...] = weight_ref[...].astype(F32)
    meta_row = iota((16, BLOCK), 0)
    window = iota((BLOCK, BLOCK), 0, F32)
    copy.wait()

    def line(ref, b):
        return jnp.concatenate([ref[pl.ds(2 * b, 1), :], ref[pl.ds(2 * b + 1, 1), :]], axis=1)

    def columns(b):
        values = values_ref[:, pl.ds(pl.multiple_of(b * BLOCK, BLOCK), BLOCK)]
        cell = line(cell_ref, b)
        weight = line(weight32_ref, b)
        high = (cell // LANES).astype(F32)
        low = (cell % LANES).astype(F32)
        meta = jnp.where(
            meta_row == 0,
            weight,
            jnp.where(meta_row == 1, high, jnp.where(meta_row == 2, low, 0.0)),
        ).astype(BF16)
        return jnp.concatenate([values, meta], axis=0)

    def add(t, base, wide, key):
        chosen = jnp.where(window == key, 1.0, 0.0).astype(BF16)
        part = dot_nt(wide, chosen)[: n_obs_chans + META].astype(BF16)
        where = pl.ds(pl.multiple_of(base, LANES), BLOCK)
        all_ref[t, :, where] = all_ref[t, :, where] + part

    def first(b):
        wide = columns(b)
        tile = line(tile_ref, b)
        slot = line(slot_ref, b)
        for t in range(n_tiles):
            base = info_smem[0, t * n_lines + 2 * b]
            key = jnp.where(tile == t, slot - base.astype(F32), -1.0)
            add(t, base, wide, key)

    def first_two(i, carry):
        first(2 * i)
        first(2 * i + 1)
        return carry

    lax.fori_loop(0, n_blocks // 2, first_two, 0)

    if cap > BLOCK:

        @pl.when(info_smem[1, 0] > 0)
        def _():
            def second(b, carry):
                wide = columns(b)
                tile = line(tile_ref, b)
                slot = line(slot_ref, b)
                for t in range(n_tiles):
                    start = info_smem[0, t * n_lines + 2 * b]
                    base = jnp.minimum(start + BLOCK, cap - BLOCK)
                    far = (tile == t) & (slot >= (start + BLOCK).astype(F32))
                    key = jnp.where(far, slot - base.astype(F32), -1.0)
                    add(t, base, wide, key)
                return carry

            lax.fori_loop(0, n_blocks, second, 0)

    if relative:
        me = index_ref[4]
        outs[0][0] = all_ref[me]
        outs[1][0] = all_ref[jnp.bitwise_xor(me, 1)]
        for k in range(1, 4):
            for s in range(2):
                outs[k + 1][s] = all_ref[jnp.bitwise_xor(me, 2 * k + s)]
    else:
        outs[0][...] = all_ref[...]


def route(index, obs_values, obs_weight, obs_tile, obs_cell, n_tiles, cap, relative):
    n_obs, chans = obs_values.shape
    n_lines = n_obs // LANES
    rows = chans + META
    outs = [(n, rows, cap) for n in ((1, 1, 2, 2, 2) if relative else (n_tiles,))]
    hbm_spec = pl.BlockSpec(memory_space=pltpu.HBM)
    return call(
        functools.partial(route_kernel, n_tiles, cap, relative),
        [jax.ShapeDtypeStruct(shape, BF16) for shape in outs],
        [smem_spec()] + [hbm_spec] * 4,
        [
            pltpu.VMEM((n_lines, LANES), jnp.int32),
            pltpu.VMEM((n_lines, LANES), BF16),
            pltpu.VMEM((n_lines, LANES), jnp.int32),
            pltpu.VMEM((chans, n_obs), BF16),
            pltpu.VMEM((n_tiles * n_lines, LANES), BF16),
            pltpu.VMEM((n_lines, LANES), F32),
            pltpu.VMEM((n_lines, LANES), F32),
            pltpu.VMEM((n_tiles, rows, cap), BF16),
            pltpu.VMEM((8, n_tiles * n_lines), jnp.int32),
            pltpu.SMEM((8, n_tiles * n_lines), jnp.int32),
            pltpu.SemaphoreType.DMA((5,)),
        ],
        2 * n_obs * n_tiles * BLOCK * 80,
        n_tiles * rows * cap * 2,
        "route",
    )(
        index,
        obs_tile.reshape(n_lines, LANES),
        obs_weight.reshape(n_lines, LANES),
        obs_cell.reshape(n_lines, LANES),
        obs_values.T,
    )


def grid_kernel(n_rows, n_cols, group, takes, first, last, *rest):
    rest = list(rest)
    got_refs = [rest.pop(0) for _ in takes]
    senders = [ref.at[i] for ref, n in zip(got_refs, takes) for i in range(n)]
    before_ref = None if first else rest.pop(0)
    own_ref = rest.pop(0)
    send_ref = rest.pop(0) if last else None
    left_ref, right_ref = rest
    n_send = len(senders)
    rows, cap = senders[0].shape
    chans = rows - META
    per_row = n_cols // LANES
    columns = iota((n_cols, cap), 0, F32)
    row_ids = iota((META, cap), 0)
    total = None
    for g in range(n_send // group):
        slot = g % 2
        for i in range(group):
            s = g * group + i
            at = slice(i * cap, (i + 1) * cap)
            values = senders[s][0:chans, :]
            meta = senders[s][chans:rows, :].astype(F32)
            weight = meta[0:1]
            high = meta[1:2]
            row = jnp.floor((high + 0.5) * (1.0 / per_row))
            column = (high - row * per_row) * LANES + meta[2:3]
            right_ref[slot, :, at] = jnp.where(columns == column, weight, 0.0).astype(BF16)
            for r in range(n_rows):
                mask = jnp.where(row == r, 1.0, 0.0)
                left_ref[slot, r * rows : r * rows + chans, at] = values * mask.astype(BF16)
                left_ref[slot, r * rows + chans : (r + 1) * rows, at] = jnp.where(
                    row_ids == 0, mask, 0.0
                ).astype(BF16)
        part = dot_nt(left_ref[slot], right_ref[slot])
        total = part if total is None else total + part
    if before_ref is not None:
        total = total + before_ref[...]
    own_ref[...] = total
    if last:
        line = iota((META, n_cols), 0)
        for r in range(n_rows):
            send_ref[r * rows : r * rows + chans, :] = own_ref[r * rows : r * rows + chans, :].astype(BF16)
            extra = own_ref[r * rows + chans : (r + 1) * rows, :]
            density = extra[0:1]
            high = density.astype(BF16).astype(F32)
            send_ref[r * rows + chans : (r + 1) * rows, :] = jnp.where(
                line == 0, high, jnp.where(line == 1, density - high, 0.0)
            ).astype(BF16)


def grid(got, before, last, n_rows, n_cols):
    takes = [n for _, n in got]
    got = [x for x, _ in got]
    n_send = sum(takes)
    rows, cap = got[0].shape[1:]
    group = max(1, min(2048 // cap, n_send))
    total = n_rows * rows
    outs = [jax.ShapeDtypeStruct((total, n_cols), F32)]
    if last:
        outs.append(jax.ShapeDtypeStruct((total, n_cols), BF16))
    ins = list(got) if before is None else list(got) + [before]
    return call(
        functools.partial(grid_kernel, n_rows, n_cols, group, takes, before is None, last),
        outs,
        [vmem_spec()] * len(ins),
        [
            pltpu.VMEM((2, total, group * cap), BF16),
            pltpu.VMEM((2, n_cols, group * cap), BF16),
        ],
        2 * n_send * cap * total * n_cols,
        n_send * rows * cap * 2,
        "grid_last" if last else "grid_part",
    )(*ins)


def lane_mask(shape, n_cols, sub, depth):
    lane = iota(shape, 1)
    width = n_cols + LANES
    keep_right = (lane >= n_cols) & (lane < n_cols + depth) & (sub == 0)
    keep_left = (lane >= width - depth) & (sub == 1)
    return (lane < n_cols) | keep_right | keep_left


def back_kernel(n_cols, n_pieces, index_ref, kernel_ref, *rest):
    pieces = [(rest[2 * i], rest[2 * i + 1]) for i in range(n_pieces)]
    side_ref, out_ref, wide_ref = rest[2 * n_pieces :]
    n_ext, all_chans = side_ref.shape[0], side_ref.shape[1]
    n_rows = n_ext - 2
    width = n_cols + LANES
    keep = lane_mask((1, width), n_cols, index_ref[2], 1)
    for h in range(n_ext):
        if h == 0 or h == n_ext - 1:
            mids = [edge[min(h, 1)] for _, edge in pieces]
        else:
            mids = [middle[h - 1] for middle, _ in pieces]
        mid = mids[0] if n_pieces == 1 else jnp.concatenate(mids, axis=0)
        ext = jnp.concatenate([mid, side_ref[h]], axis=1).astype(F32)
        ext = jnp.where(keep, ext, 0.0)
        at = slice(h * n_cols, (h + 1) * n_cols)
        wide_ref[0:all_chans, at] = pltpu.roll(ext, width - 1, 1)[:, :n_cols].astype(BF16)
        wide_ref[all_chans : 2 * all_chans, at] = mid
        wide_ref[2 * all_chans :, at] = pltpu.roll(ext, 1, 1)[:, :n_cols].astype(BF16)
    total = None
    for a in range(3):
        at = slice((2 - a) * n_cols, (2 - a + n_rows) * n_cols)
        part = dot_nn(kernel_ref[a], wide_ref[:, at])
        total = part if total is None else total + part
    out_ref[...] = total


def back(index, kernel, pieces, side, n_cols):
    n_ext, all_chans = side.shape[0], side.shape[1]
    n_out = kernel.shape[1]
    return call(
        functools.partial(back_kernel, n_cols, len(pieces)),
        jax.ShapeDtypeStruct((n_out, (n_ext - 2) * n_cols), F32),
        [smem_spec()] + [vmem_spec()] * (2 + 2 * len(pieces)),
        [pltpu.VMEM((3 * all_chans, n_ext * n_cols), BF16)],
        2 * n_ext * 9 * all_chans * n_out * n_cols,
        n_ext * all_chans * n_cols * 2,
        "back",
    )(index, kernel, *[x for piece in pieces for x in piece], side)


def grads_kernel(
    split, chans, index_ref, kernel_ref, gain_ref, own_ref, edge_ref, peer_ref, peer_edge_ref,
    side_ref, cot_ref, back_ref, hidden_ref, *rest,
):
    rest = list(rest)
    if split:
        keep_out, give_out = rest.pop(0), rest.pop(0)
    else:
        all_out = rest.pop(0)
    taps_ref, logs_ref, wide_ref, out_left_ref, pre_left_ref, acc_ref = rest
    n_rows, own, n_cols = cot_ref.shape
    n_hidden = kernel_ref.shape[1]
    rows = chans + META
    taps_rows = 3 * chans
    width = n_cols + LANES
    tile, chan, sub, n_tile = index_ref[0], index_ref[1], index_ref[2], index_ref[3]
    keep_two = lane_mask((1, width), n_cols, sub, 2)

    log_line = iota((16, width), 0)
    for i in range(n_rows + 4):
        if 2 <= i < n_rows + 2:
            mid = own_ref[i - 2]
            if peer_ref is not None:
                mid = mid + peer_ref[i - 2].astype(F32)
        else:
            e = i if i < 2 else i - n_rows
            mid = edge_ref[e].astype(F32)
            if peer_ref is not None:
                mid = mid + peer_edge_ref[e].astype(F32)
        side = side_ref[i, 0:rows].astype(F32)
        if peer_ref is not None:
            side = side + side_ref[i, rows : 2 * rows].astype(F32)
        ext = jnp.concatenate([mid, side], axis=1)
        density = ext[chans : chans + 1] + ext[chans + 1 : chans + 2]
        logs = jnp.log(1.0 + density)
        logs_ref[i] = logs
        shrink = jnp.where(keep_two, 1.0 / (1.0 + density), 0.0)
        feats = ext[0:chans] * shrink
        at = slice(i * width, (i + 1) * width)
        taps_ref[0:chans, at] = pltpu.roll(feats, 1, 1).astype(BF16)
        taps_ref[chans : 2 * chans, at] = feats.astype(BF16)
        taps_ref[2 * chans : taps_rows, at] = pltpu.roll(feats, width - 1, 1).astype(BF16)
        high = logs.astype(BF16).astype(F32)
        middle = (logs - high).astype(BF16).astype(F32)
        taps_ref[taps_rows:, at] = jnp.where(
            log_line == 0,
            high,
            jnp.where(log_line == 1, middle, jnp.where(log_line == 2, logs - high - middle, 0.0)),
        ).astype(BF16)

    nothing = jnp.zeros((own, n_cols), BF16)
    for h in range(n_rows + 2):
        for a in range(3):
            inside = 0 <= h - a < n_rows
            put = slice(a * own, (a + 1) * own)
            out_left_ref[put, h * n_cols : (h + 1) * n_cols] = cot_ref[h - a] if inside else nothing
            if not inside:
                pre_left_ref[put, h * width : h * width + n_cols] = nothing
        pre_left_ref[:, h * width + n_cols : (h + 1) * width] = jnp.zeros((3 * own, LANES), BF16)

    gain = gain_ref[:, 0:1]
    keep_one = lane_mask((1, width), n_cols, sub, 1)
    group = 2
    for first in range(0, n_rows + 2, group):
        pre_all = None
        for a in range(3):
            at = slice((first + a) * width, (first + a + group) * width)
            part = dot_nn(kernel_ref[a], taps_ref[0:taps_rows, at])
            pre_all = part if pre_all is None else pre_all + part
        for k in range(group):
            h = first + k
            pre = pre_all[:, k * width : (k + 1) * width] + gain * logs_ref[h + 1]
            at = slice(h * n_cols, (h + 1) * n_cols)
            keep = keep_one
            if h == 0:
                keep = keep & (tile > 0)
            elif h == n_rows + 1:
                keep = keep & (tile < n_tile - 1)
            else:
                mine = pre[0:own, :n_cols]
                for c in range(1, n_hidden // own):
                    mine = jnp.where(chan == c, pre[c * own : (c + 1) * own, :n_cols], mine)
                s = 0.5 + 0.5 * jnp.tanh(0.5 * mine)
                there = slice((h - 1) * n_cols, h * n_cols)
                grad = (back_ref[:, there] * s * (1.0 + mine * (1.0 - s))).astype(BF16)
                for a in range(3):
                    put = (h - 1 + a) * width
                    pre_left_ref[a * own : (a + 1) * own, put : put + n_cols] = grad
            half = 0.5 * pre
            hidden = jnp.where(keep, half + half * jnp.tanh(half), 0.0)
            hidden_ref[h] = hidden.astype(BF16)
            wide_ref[0:n_hidden, at] = pltpu.roll(hidden, 1, 1)[:, :n_cols].astype(BF16)
            wide_ref[n_hidden : 2 * n_hidden, at] = hidden[:, :n_cols].astype(BF16)
            wide_ref[2 * n_hidden :, at] = pltpu.roll(hidden, width - 1, 1)[:, :n_cols].astype(BF16)

    three = 3 * own
    lanes = 3 * n_hidden
    half_rows = taps_rows // 2
    acc_ref[0:three, :] = dot_nt(out_left_ref[...], wide_ref[...])
    one = dot_nt(taps_ref[:, width : (n_rows + 3) * width], pre_left_ref[...])
    acc_ref[three:, :] = jnp.zeros((acc_ref.shape[0] - three, lanes), F32)
    acc_ref[three : three + half_rows, 0:three] = one[0:half_rows]
    acc_ref[three : three + half_rows, lanes // 2 : lanes // 2 + three] = one[half_rows:taps_rows]
    gains = one[taps_rows : taps_rows + 1] + one[taps_rows + 1 : taps_rows + 2] + one[taps_rows + 2 : taps_rows + 3]
    acc_ref[three + half_rows : three + half_rows + 1, 0:three] = gains
    if split:
        half = acc_ref.shape[0] // 2
        keep_out[...] = acc_ref[pl.ds(pl.multiple_of(sub * half, half), half), :]
        give_out[...] = acc_ref[pl.ds(pl.multiple_of((1 - sub) * half, half), half), :].astype(BF16)
    else:
        all_out[...] = acc_ref[...]


def grads(split, index, kernel, gain, own, edge, peer, peer_edge, side, cot, back_out):
    n_rows, n_own, n_cols = cot.shape
    n_hidden = kernel.shape[1]
    chans = kernel.shape[2] // 3
    width = n_cols + LANES
    lanes = 3 * n_hidden
    acc_rows = 3 * n_own + 3 * chans // 2 + 32
    body = functools.partial(grads_kernel, split, chans)
    ins = [own, edge, peer, peer_edge, side, cot, back_out]
    if peer is None:
        ins = [own, edge, side, cot, back_out]
        body = lambda i, k, g, o, e, *rest: grads_kernel(split, chans, i, k, g, o, e, None, None, *rest)
    outs = [jax.ShapeDtypeStruct((n_rows + 2, n_hidden, width), BF16)]
    if split:
        outs.append(jax.ShapeDtypeStruct((acc_rows // 2, lanes), F32))
        outs.append(jax.ShapeDtypeStruct((acc_rows // 2, lanes), BF16))
    else:
        outs.append(jax.ShapeDtypeStruct((acc_rows, lanes), F32))
    return call(
        body,
        outs,
        [smem_spec()] + [vmem_spec()] * (2 + len(ins)),
        [
            pltpu.VMEM((3 * chans + 16, (n_rows + 4) * width), BF16),
            pltpu.VMEM((n_rows + 4, 1, width), F32),
            pltpu.VMEM((3 * n_hidden, (n_rows + 2) * n_cols), BF16),
            pltpu.VMEM((3 * n_own, (n_rows + 2) * n_cols), BF16),
            pltpu.VMEM((3 * n_own, (n_rows + 2) * width), BF16),
            pltpu.VMEM((acc_rows, lanes), F32),
        ],
        2 * (n_rows + 2) * 9 * n_cols * n_hidden * (n_own + chans),
        (n_rows + 2) * 3 * n_hidden * n_cols * 2,
        "grads",
    )(index, kernel, gain, *ins)


def encode_kernel(kernel_ref, hidden_ref, out_ref, wide_ref):
    n_ext, n_hidden, width = hidden_ref.shape
    n_rows = n_ext - 2
    n_cols = width - LANES
    for h in range(n_ext):
        hidden = hidden_ref[h].astype(F32)
        at = slice(h * n_cols, (h + 1) * n_cols)
        wide_ref[0:n_hidden, at] = pltpu.roll(hidden, 1, 1)[:, :n_cols].astype(BF16)
        wide_ref[n_hidden : 2 * n_hidden, at] = hidden_ref[h, :, 0:n_cols]
        wide_ref[2 * n_hidden :, at] = pltpu.roll(hidden, width - 1, 1)[:, :n_cols].astype(BF16)
    total = None
    for a in range(3):
        part = dot_nn(kernel_ref[a], wide_ref[:, a * n_cols : (a + n_rows) * n_cols])
        total = part if total is None else total + part
    for r in range(n_rows):
        out_ref[r] = total[:, r * n_cols : (r + 1) * n_cols].astype(BF16)


def encode(kernel, hidden):
    n_ext, n_hidden, width = hidden.shape
    own = kernel.shape[1]
    n_cols = width - LANES
    return call(
        encode_kernel,
        jax.ShapeDtypeStruct((n_ext - 2, own, n_cols), BF16),
        [vmem_spec()] * 2,
        [pltpu.VMEM((3 * n_hidden, n_ext * n_cols), BF16)],
        2 * n_ext * 9 * own * n_hidden * n_cols,
        hidden.size * 2,
        "encode",
    )(kernel, hidden)


def quarters_kernel(index_ref, keep_ref, got_ref, *outs):
    n = len(outs)
    rows = keep_ref.shape[0] // n
    for k in range(n):
        other = jnp.bitwise_xor(index_ref[0], k)
        at = pl.ds(pl.multiple_of(other * rows, rows), rows)
        outs[k][...] = (keep_ref[at, :] + got_ref[at, :].astype(F32)).astype(outs[k].dtype)


def quarters(index, keep, got, n):
    rows, lanes = keep.shape
    return call(
        quarters_kernel,
        [jax.ShapeDtypeStruct((rows // n, lanes), F32 if k == 0 else BF16) for k in range(n)],
        [smem_spec(), vmem_spec(), vmem_spec()],
        [],
        rows * lanes,
        rows * lanes * 8,
        "quarters",
    )(index, keep, got)


def finish_kernel(scale, own, chans, index_ref, mine_ref, other_ref, two_ref, one_ref, gain_ref, all_ref):
    n, rows, lanes = mine_ref.shape
    n_hidden = lanes // 3
    tile, sub = index_ref[0], index_ref[2]
    for k in range(n):
        at = jnp.bitwise_xor(tile, k) * rows
        here = pl.multiple_of(sub * (n * rows) + at, rows)
        there = pl.multiple_of((1 - sub) * (n * rows) + at, rows)
        all_ref[pl.ds(here, rows), :] = mine_ref[k].astype(F32) * scale
        all_ref[pl.ds(there, rows), :] = other_ref[k].astype(F32) * scale
    half_rows = 3 * chans // 2
    for a in range(3):
        for b in range(3):
            two_ref[a, b] = all_ref[a * own : (a + 1) * own, b * n_hidden : (b + 1) * n_hidden]
        lines = jnp.concatenate(
            [
                all_ref[3 * own : 3 * own + half_rows, s + a * own : s + (a + 1) * own]
                for s in (0, lanes // 2)
            ],
            axis=0,
        )
        for b in range(3):
            one_ref[a, b] = lines[b * chans : (b + 1) * chans]
    gain_ref[...] = all_ref[3 * own + half_rows : 3 * own + half_rows + 1, own : 2 * own]


def finish(index, mine, other, scale, own, chans):
    n, rows, lanes = mine.shape
    n_hidden = lanes // 3
    return call(
        functools.partial(finish_kernel, scale, own, chans),
        [
            jax.ShapeDtypeStruct((3, 3, own, n_hidden), F32),
            jax.ShapeDtypeStruct((3, 3, chans, own), F32),
            jax.ShapeDtypeStruct((1, own), F32),
        ],
        [smem_spec(), vmem_spec(), vmem_spec()],
        [pltpu.VMEM((2 * n * rows, lanes), F32)],
        n * rows * lanes,
        n * rows * lanes * 12,
        "finish",
    )(index, mine, other)


def offer_kernel(index_ref, two_ref, one_ref, gain_ref, out_ref):
    own = two_ref.shape[2]
    chans = one_ref.shape[2]
    at = pl.ds(pl.multiple_of((1 - index_ref[1]) * own, own), own)
    gain = gain_ref[...]
    high = gain.astype(BF16).astype(F32)
    middle = (gain - high).astype(BF16).astype(F32)
    line = iota((8, own), 0)
    terms = jnp.where(
        line == 0, high, jnp.where(line == 1, middle, jnp.where(line == 2, gain - high - middle, 0.0))
    ).astype(BF16)
    for a in range(3):
        for b in range(3):
            out_ref[a, b, 0:own] = two_ref[a, b, :, at]
            out_ref[a, b, own : own + chans] = one_ref[a, b]
            out_ref[a, b, own + chans :] = terms


def offer(index, two, one, gain):
    own, chans = two.shape[2], one.shape[2]
    return call(
        offer_kernel,
        jax.ShapeDtypeStruct((3, 3, own + chans + 8, own), BF16),
        [smem_spec()] + [vmem_spec()] * 3,
        [],
        9 * own * (own + chans),
        9 * own * (own + chans) * 4,
        "offer",
    )(index, two, one, gain[None])


def arrange_kernel(index_ref, two_ref, one_ref, gain_ref, theirs_ref, back_ref, code_ref, first_ref, column_ref):
    own = two_ref.shape[2]
    chans = one_ref.shape[2]
    chan = index_ref[1]
    mine = pl.ds(pl.multiple_of(chan * own, own), own)
    peer = pl.ds(pl.multiple_of((1 - chan) * own, own), own)

    def turned(block):
        return block.astype(F32).T.astype(BF16)

    for a in range(3):
        for b in range(3):
            left = b * 2 * own
            back_ref[a, :, left : left + own] = turned(two_ref[a, b, :, mine])
            back_ref[a, :, left + own : left + 2 * own] = turned(theirs_ref[a, b, 0:own])
            code_ref[a, :, left : left + 2 * own] = two_ref[a, b]
        first_ref[a, mine, :] = turned(jnp.concatenate([one_ref[a, b] for b in range(3)], axis=0))
        first_ref[a, peer, :] = turned(
            jnp.concatenate([theirs_ref[a, b, own : own + chans] for b in range(3)], axis=0)
        )
    terms = theirs_ref[0, 0, own + chans :].astype(F32)
    other = terms[0:1] + terms[1:2] + terms[2:3]
    column_ref[mine, :] = jnp.broadcast_to(gain_ref[...], (own, own)).T
    column_ref[peer, :] = jnp.broadcast_to(other, (own, own)).T


def arrange(index, two, one, gain, theirs):
    own, chans = two.shape[2], one.shape[2]
    return call(
        arrange_kernel,
        [
            jax.ShapeDtypeStruct((3, own, 6 * own), BF16),
            jax.ShapeDtypeStruct((3, own, 6 * own), BF16),
            jax.ShapeDtypeStruct((3, 2 * own, 3 * chans), BF16),
            jax.ShapeDtypeStruct((2 * own, LANES), F32),
        ],
        [smem_spec()] + [vmem_spec()] * 4,
        [],
        9 * own * (4 * own + 2 * chans),
        9 * own * (4 * own + 2 * chans) * 4,
        "arrange",
    )(index, two, one, gain[None], theirs)


def step_perm(count, by):
    return [(i, i + by) for i in range(count) if 0 <= i + by < count]


def swap_sub(x):
    return lax.ppermute(x, "sub", [(0, 1), (1, 0)])


def swap_chan(x):
    return lax.ppermute(x, "chan", [(0, 1), (1, 0)])


def swap_tile(x, n_tile, k):
    return lax.ppermute(x, "tile", [(i, i ^ k) for i in range(n_tile)])


def edges(block, depth, n_tile):
    low = lax.ppermute(block[-depth:], "tile", step_perm(n_tile, 1))
    high = lax.ppermute(block[:depth], "tile", step_perm(n_tile, -1))
    return low, high


def near(block, sub):
    n_cols = block.shape[-1]
    return jnp.where(sub == 0, block[..., n_cols - LANES :], block[..., :LANES])


def side_rows(parts, sub):
    columns = [
        jnp.concatenate([near(edge[: edge.shape[0] // 2], sub), near(mid, sub), near(edge[edge.shape[0] // 2 :], sub)], axis=0)
        for mid, edge in parts
    ]
    both = columns[0] if len(columns) == 1 else jnp.concatenate(columns, axis=1)
    return swap_sub(both)


def body(obs_values, obs_weight, obs_tile, obs_cell, conv_one, conv_two, density_gain, cotangent):
    own, n_rows, n_cols = cotangent.shape
    n_tile = lax.axis_size("tile")
    n_sub = lax.axis_size("sub")
    n_chan = lax.axis_size("chan")
    pair = n_chan == 2 and own == LANES
    n_tiles = n_tile * n_sub
    chans = obs_values.shape[1]
    n_hidden = own * n_chan
    cap = 2 * obs_values.shape[0] // n_tiles
    tile, chan, sub = lax.axis_index("tile"), lax.axis_index("chan"), lax.axis_index("sub")
    index = jnp.stack([tile, chan, sub, jnp.int32(n_tile), tile * n_sub + sub]).astype(jnp.int32)

    bottom, top = cotangent[:, -1], cotangent[:, 0]
    one_own = conv_one.transpose(0, 1, 3, 2)
    if pair:
        offered = offer(index, conv_two, one_own, density_gain)
        obs_tile, bottom, top, offered = lax.optimization_barrier((obs_tile, bottom, top, offered))
        theirs = swap_chan(offered)
    low = lax.ppermute(bottom, "tile", step_perm(n_tile, 1))
    high = lax.ppermute(top, "tile", step_perm(n_tile, -1))

    few = n_tiles == 8
    sent = route(index, obs_values, obs_weight, obs_tile, obs_cell, n_tiles, cap, few)
    if pair:
        sent, low, high, theirs = lax.optimization_barrier((sent, low, high, theirs))
    if few:
        beside = swap_sub(sent[1])
        far = [swap_tile(sent[k + 1], n_tile, k) for k in (1, 2, 3)]
        steps = [
            [(sent[0], 1), (beside, 1)],
            [(far[0], 1), (swap_sub(far[0][1:]), 1), (far[1], 1), (far[2], 1)],
            [(swap_sub(far[1][1:]), 1), (swap_sub(far[2][1:]), 1)],
        ]
    else:
        got = lax.all_to_all(sent[0], ("tile", "sub"), split_axis=0, concat_axis=0, tiled=True)
        steps = [[(got, n_tiles)]]

    if pair:
        cotangent, _ = lax.optimization_barrier((cotangent, sent[0]))
        cot = cotangent.transpose(1, 0, 2)
        cot_edge = jnp.stack([low, high])
        cot_peer = swap_chan(cotangent)
        pieces = [(cot, cot_edge), (cot_peer.transpose(1, 0, 2), swap_chan(cot_edge))]
    else:
        cot = cotangent.transpose(1, 0, 2)
        pieces = [
            (
                lax.all_gather(cot, "chan", axis=1, tiled=True),
                lax.all_gather(jnp.stack([low, high]), "chan", axis=1, tiled=True),
            )
        ]
    cot_side = side_rows(pieces, sub)

    if pair:
        back_weights, code_weights, one_weights, gain = arrange(
            index, conv_two, one_own, density_gain, theirs
        )
    else:
        columns = lax.all_to_all(conv_two, "chan", split_axis=3, concat_axis=2, tiled=True)
        one_full = lax.all_gather(one_own, "chan", axis=3, tiled=True)
        gain = lax.all_gather(density_gain, "chan", axis=0, tiled=True)
        gain = jnp.broadcast_to(gain[:, None], (n_hidden, LANES))
        code_weights = conv_two.transpose(0, 2, 1, 3).reshape(3, own, 3 * n_hidden)
        back_weights = columns.transpose(0, 3, 1, 2).reshape(3, own, 3 * n_hidden)
        one_weights = one_full.transpose(0, 3, 1, 2).reshape(3, n_hidden, 3 * chans)

    part = None
    for step in steps[:-1]:
        part = grid(step, part, False, n_rows, n_cols)[0]
    if few:
        part, back_weights, one_weights, code_weights, gain = lax.optimization_barrier(
            (part, back_weights, one_weights, code_weights, gain)
        )
    part, message = grid(steps[-1], part, True, n_rows, n_cols)
    shape = (n_rows, chans + META, n_cols)
    part = part.reshape(shape)
    message = message.reshape(shape)
    if not pair:
        part = lax.psum(part, "chan")
        density = part[:, chans]
        dense = density.astype(BF16)
        rest = (density - dense.astype(F32)).astype(BF16)
        message = part.astype(BF16).at[:, chans].set(dense).at[:, chans + 1].set(rest)
    low, high = edges(message, 2, n_tile)
    edge = jnp.concatenate([low, high], axis=0)
    back_out = back(index, back_weights, pieces, cot_side, n_cols)
    if pair:
        peer, peer_edge = swap_chan(message), swap_chan(edge)
        peer_edge, back_out = lax.optimization_barrier((peer_edge, back_out))
        side = side_rows([(message, edge), (peer, peer_edge)], sub)
    else:
        peer, peer_edge = None, None
        side = side_rows([(message, edge)], sub)

    scale = 1.0 / math.sqrt(n_tiles * n_rows * n_cols)
    split = pair and n_tile == 4
    hidden, *partial = grads(
        split, index, one_weights, gain, part, edge, peer, peer_edge, side, cot, back_out
    )
    encoded = encode(code_weights, hidden).transpose(1, 0, 2)

    if split:
        keep, give = partial
        mine, *others = quarters(index, keep, swap_sub(give), n_tile)
        for k, other in enumerate(others, 1):
            mine = mine + swap_tile(other, n_tile, k).astype(F32)
        mine, encoded = lax.optimization_barrier((mine.astype(BF16), encoded))
        mine = jnp.stack([mine] + [swap_tile(mine, n_tile, k) for k in range(1, n_tile)])
        grad_two, grad_one, grad_gain = finish(index, mine, swap_sub(mine), scale, own, chans)
        return encoded, grad_one.transpose(0, 1, 3, 2), grad_two, grad_gain[0]

    total = lax.psum(partial[0], ("tile", "sub")) * scale
    three = 3 * own
    half_rows = 3 * chans // 2
    lanes = 3 * n_hidden
    grad_two = total[:three].reshape(3, own, 3, n_hidden).transpose(0, 2, 1, 3)
    lines = total[three : three + half_rows]
    lines = jnp.concatenate([lines[:, :three], lines[:, lanes // 2 : lanes // 2 + three]], axis=0)
    grad_one = lines.reshape(3, chans, 3, own).transpose(2, 0, 3, 1)
    grad_gain = total[three + half_rows, own : 2 * own]
    return encoded, grad_one, grad_two, grad_gain


def solution(mesh):
    placed = (
        P(("member", "tile", "chan", "sub"), None),
        P(("member", "tile", "chan", "sub")),
        P(("member", "tile", "chan", "sub")),
        P(("member", "tile", "chan", "sub")),
        P(None, None, "chan", None),
        P(None, None, "chan", None),
        P("chan"),
        P(("member", "chan"), "tile", "sub"),
    )
    return jax.shard_map(
        body,
        mesh=mesh,
        in_specs=placed,
        out_specs=(
            P(("member", "chan"), "tile", "sub"),
            P("member", None, "chan", None),
            P("member", None, "chan", None),
            P(("member", "chan")),
        ),
        check_vma=False,
    )
```

```python
import functools
import math

import jax
import jax.numpy as jnp
from jax import lax
from jax.experimental import pallas as pl
from jax.experimental.pallas import tpu as pltpu
from jax.sharding import PartitionSpec as P

BF16 = jnp.bfloat16
F32 = jnp.float32
LANES = 128
BLOCK = 256
META = 8
MIB = 1024 * 1024


def dot_nt(a, b):
    return lax.dot_general(a, b, (((1,), (1,)), ((), ())), preferred_element_type=F32)


def dot_nn(a, b):
    return lax.dot_general(a, b, (((1,), (0,)), ((), ())), preferred_element_type=F32)


def iota(shape, dim, dtype=jnp.int32):
    return lax.broadcasted_iota(jnp.int32, shape, dim).astype(dtype)


def vmem_spec():
    return pl.BlockSpec(memory_space=pltpu.VMEM)


def smem_spec():
    return pl.BlockSpec(memory_space=pltpu.SMEM)


def call(kernel, out_shape, in_specs, scratch, flops, moved, name, vmem=32):
    n_out = len(out_shape) if isinstance(out_shape, (tuple, list)) else None
    out_specs = vmem_spec() if n_out is None else [vmem_spec() for _ in range(n_out)]
    return pl.pallas_call(
        kernel,
        out_shape=out_shape,
        in_specs=in_specs,
        out_specs=out_specs,
        scratch_shapes=scratch,
        compiler_params=pltpu.CompilerParams(vmem_limit_bytes=vmem * MIB),
        cost_estimate=pl.CostEstimate(flops=flops, bytes_accessed=moved, transcendentals=0),
        name=name,
    )


def route_kernel(n_tiles, cap, relative, index_ref, tile_hbm, weight_hbm, cell_hbm, values_hbm, *rest):
    n_outs = 5 if relative else 1
    outs = rest[:n_outs]
    (tile_ref, weight_ref, cell_ref, values_ref, onehot_ref, slot_ref, weight32_ref, all_ref,
     info_ref, info_smem, sems) = rest[n_outs:]
    loads = [
        pltpu.make_async_copy(tile_hbm, tile_ref, sems.at[0]),
        pltpu.make_async_copy(weight_hbm, weight_ref, sems.at[1]),
        pltpu.make_async_copy(cell_hbm, cell_ref, sems.at[2]),
        pltpu.make_async_copy(values_hbm, values_ref, sems.at[3]),
    ]
    for load in loads:
        load.start()
    all_ref[...] = jnp.zeros(all_ref.shape, BF16)
    loads[0].wait()
    n_lines = tile_ref.shape[0]
    n_blocks = n_lines // 2
    n_obs_chans = values_ref.shape[0]
    pairs = n_tiles * n_lines
    tiles = tile_ref[...]
    for t in range(n_tiles):
        onehot_ref[t * n_lines : (t + 1) * n_lines, :] = jnp.where(tiles == t, 1.0, 0.0).astype(BF16)
    onehot = onehot_ref[...]
    upper = jnp.where(
        iota((LANES, LANES), 0) <= iota((LANES, LANES), 1), 1.0, 0.0
    ).astype(BF16)
    here = iota((pairs, pairs), 0)
    there = iota((pairs, pairs), 1)
    earlier = jnp.where(
        (here // n_lines == there // n_lines) & (there < here), 1.0, 0.0
    ).astype(BF16)
    total_row = dot_nt(jnp.ones((8, LANES), BF16), onehot)
    offset_row = dot_nt(total_row.astype(BF16), earlier)
    odd = iota((8, pairs), 1) % 2 == 1
    both = jnp.where(odd, total_row + pltpu.roll(total_row, 1, 1), 0.0)
    spill = jnp.where(jnp.max(both, axis=1, keepdims=True) > LANES, 1.0, 0.0)
    info_ref[...] = jnp.where(
        iota((8, pairs), 0) == 0, offset_row, spill
    ).astype(jnp.int32)
    copy = pltpu.make_async_copy(info_ref, info_smem, sems.at[4])
    copy.start()
    cum = dot_nn(onehot, upper)
    totals = dot_nn(onehot, jnp.ones((LANES, LANES), BF16))
    offset = dot_nn(earlier, totals.astype(BF16))
    place = cum + offset - 1.0
    slots = jnp.zeros(tiles.shape, F32)
    for t in range(n_tiles):
        slots = jnp.where(tiles == t, place[t * n_lines : (t + 1) * n_lines, :], slots)
    slot_ref[...] = slots
    for load in loads[1:]:
        load.wait()
    weight32_ref[...] = weight_ref[...].astype(F32)
    meta_row = iota((16, BLOCK), 0)
    window = iota((LANES, BLOCK), 0, F32)
    blank = jnp.zeros((n_obs_chans + 16, LANES), F32)
    copy.wait()

    def line(ref, b):
        return jnp.concatenate([ref[pl.ds(2 * b, 1), :], ref[pl.ds(2 * b + 1, 1), :]], axis=1)

    def columns(b):
        values = values_ref[:, pl.ds(pl.multiple_of(b * BLOCK, BLOCK), BLOCK)]
        cell = line(cell_ref, b)
        weight = line(weight32_ref, b)
        high = (cell // LANES).astype(F32)
        low = (cell % LANES).astype(F32)
        meta = jnp.where(
            meta_row == 0,
            weight,
            jnp.where(meta_row == 1, high, jnp.where(meta_row == 2, low, 0.0)),
        ).astype(BF16)
        return jnp.concatenate([values, meta], axis=0)

    def add(t, wide, tile, slot, start):
        key = jnp.where(tile == t, slot - start.astype(F32), -1.0)
        chosen = jnp.where(window == key, 1.0, 0.0).astype(BF16)
        part = jnp.concatenate([dot_nt(wide, chosen), blank], axis=1)
        base = jnp.minimum(start // LANES * LANES, cap - BLOCK)
        turn = jnp.bitwise_and(start - base, BLOCK - 1)
        part = pltpu.roll(part, turn, 1)[: n_obs_chans + META].astype(BF16)
        where = pl.ds(pl.multiple_of(base, LANES), BLOCK)
        all_ref[t, :, where] = all_ref[t, :, where] + part

    def place_block(b, skip):
        wide = columns(b)
        tile = line(tile_ref, b)
        slot = line(slot_ref, b)
        for t in range(n_tiles):
            add(t, wide, tile, slot, info_smem[0, t * n_lines + 2 * b] + skip)

    def first_two(i, carry):
        place_block(2 * i, 0)
        place_block(2 * i + 1, 0)
        return carry

    lax.fori_loop(0, n_blocks // 2, first_two, 0)

    @pl.when(info_smem[1, 0] > 0)
    def _():
        def rest_of(b, carry):
            place_block(b, LANES)
            return carry

        lax.fori_loop(0, n_blocks, rest_of, 0)

    if relative:
        me = index_ref[4]
        outs[0][0] = all_ref[me]
        outs[1][0] = all_ref[jnp.bitwise_xor(me, 1)]
        for k in range(1, 4):
            for s in range(2):
                outs[k + 1][s] = all_ref[jnp.bitwise_xor(me, 2 * k + s)]
    else:
        outs[0][...] = all_ref[...]


def route(index, obs_values, obs_weight, obs_tile, obs_cell, n_tiles, cap, relative):
    n_obs, chans = obs_values.shape
    n_lines = n_obs // LANES
    rows = chans + META
    outs = [(n, rows, cap) for n in ((1, 1, 2, 2, 2) if relative else (n_tiles,))]
    hbm_spec = pl.BlockSpec(memory_space=pltpu.HBM)
    return call(
        functools.partial(route_kernel, n_tiles, cap, relative),
        [jax.ShapeDtypeStruct(shape, BF16) for shape in outs],
        [smem_spec()] + [hbm_spec] * 4,
        [
            pltpu.VMEM((n_lines, LANES), jnp.int32),
            pltpu.VMEM((n_lines, LANES), BF16),
            pltpu.VMEM((n_lines, LANES), jnp.int32),
            pltpu.VMEM((chans, n_obs), BF16),
            pltpu.VMEM((n_tiles * n_lines, LANES), BF16),
            pltpu.VMEM((n_lines, LANES), F32),
            pltpu.VMEM((n_lines, LANES), F32),
            pltpu.VMEM((n_tiles, rows, cap), BF16),
            pltpu.VMEM((8, n_tiles * n_lines), jnp.int32),
            pltpu.SMEM((8, n_tiles * n_lines), jnp.int32),
            pltpu.SemaphoreType.DMA((5,)),
        ],
        2 * n_obs * n_tiles * BLOCK * 80,
        n_tiles * rows * cap * 2,
        "route",
    )(
        index,
        obs_tile.reshape(n_lines, LANES),
        obs_weight.reshape(n_lines, LANES),
        obs_cell.reshape(n_lines, LANES),
        obs_values.T,
    )


def grid_kernel(n_rows, n_cols, group, takes, first, last, *rest):
    rest = list(rest)
    got_refs = [rest.pop(0) for _ in takes]
    senders = [ref.at[i] for ref, picked in zip(got_refs, takes) for i in picked]
    before_ref = None if first else rest.pop(0)
    own_ref = rest.pop(0)
    send_refs = [rest.pop(0) for _ in range(3)] if last else None
    left_ref, right_ref = rest
    n_send = len(senders)
    rows, cap = senders[0].shape
    chans = rows - META
    data = n_rows * chans
    per_row = n_cols // LANES
    columns = iota((n_cols, cap), 0, F32)
    row_ids = iota((2 * n_rows, cap), 0, F32)
    total = None
    for g in range(n_send // group):
        slot = g % 2
        for i in range(group):
            sender = senders[g * group + i]
            at = slice(i * cap, (i + 1) * cap)
            values = sender[0:chans, :]
            meta = sender[chans:rows, :].astype(F32)
            weight = meta[0:1]
            high = meta[1:2]
            row = jnp.floor((high + 0.5) * (1.0 / per_row))
            column = (high - row * per_row) * LANES + meta[2:3]
            right_ref[slot, :, at] = jnp.where(columns == column, weight, 0.0).astype(BF16)
            in_row = jnp.where(row_ids == row, 1.0, 0.0)
            for r in range(n_rows):
                left_ref[slot, r * chans : (r + 1) * chans, at] = values * in_row[r : r + 1].astype(BF16)
            left_ref[slot, data:, at] = in_row.astype(BF16)
        part = dot_nt(left_ref[slot], right_ref[slot])
        total = part if total is None else total + part
    if before_ref is not None:
        total = total + before_ref[...]
    own_ref[...] = total
    if last:
        send_ref, low_ref, high_ref = send_refs
        density = own_ref[data : data + n_rows, :]
        high = density.astype(BF16).astype(F32)
        low = density - high
        send_ref[0:data, :] = own_ref[0:data, :].astype(BF16)
        send_ref[data:, :] = jnp.concatenate([high, low], axis=0).astype(BF16)
        for ref, at in ((high_ref, 0), (low_ref, n_rows - 2)):
            ref[0 : 2 * chans, :] = own_ref[at * chans : (at + 2) * chans, :].astype(BF16)
            ref[2 * chans :, :] = jnp.concatenate(
                [high[at : at + 2], low[at : at + 2], jnp.zeros((4, n_cols), F32)], axis=0
            ).astype(BF16)


def grid(got, before, last, n_rows, n_cols):
    takes = [picked for _, picked in got]
    got = [x for x, _ in got]
    n_send = sum(len(picked) for picked in takes)
    rows, cap = got[0].shape[1:]
    group = max(1, min(2048 // cap, n_send))
    chans = rows - META
    total = n_rows * chans + 2 * n_rows
    outs = [jax.ShapeDtypeStruct((total, n_cols), F32)]
    if last:
        outs.append(jax.ShapeDtypeStruct((total, n_cols), BF16))
        outs += [jax.ShapeDtypeStruct((2 * chans + 8, n_cols), BF16)] * 2
    ins = list(got) if before is None else list(got) + [before]
    return call(
        functools.partial(grid_kernel, n_rows, n_cols, group, takes, before is None, last),
        outs,
        [vmem_spec()] * len(ins),
        [
            pltpu.VMEM((2, total, group * cap), BF16),
            pltpu.VMEM((2, n_cols, group * cap), BF16),
        ],
        2 * n_send * cap * total * n_cols,
        n_send * rows * cap * 2,
        "grid_last" if last else "grid_part",
    )(*ins)


def lane_mask(shape, n_cols, sub, depth):
    lane = iota(shape, 1)
    width = n_cols + LANES
    keep_right = (lane >= n_cols) & (lane < n_cols + depth) & (sub == 0)
    keep_left = (lane >= width - depth) & (sub == 1)
    return (lane < n_cols) | keep_right | keep_left


def back_kernel(n_cols, n_pieces, index_ref, kernel_ref, *rest):
    pieces = [(rest[2 * i], rest[2 * i + 1]) for i in range(n_pieces)]
    side_ref, out_ref, wide_ref = rest[2 * n_pieces :]
    n_ext, all_chans = side_ref.shape[0], side_ref.shape[1]
    n_rows = n_ext - 2
    width = n_cols + LANES
    keep = lane_mask((1, width), n_cols, index_ref[2], 1)
    for h in range(n_ext):
        if h == 0 or h == n_ext - 1:
            mids = [edge[min(h, 1)] for _, edge in pieces]
        else:
            mids = [middle[h - 1] for middle, _ in pieces]
        mid = mids[0] if n_pieces == 1 else jnp.concatenate(mids, axis=0)
        ext = jnp.concatenate([mid, side_ref[h]], axis=1).astype(F32)
        ext = jnp.where(keep, ext, 0.0)
        at = slice(h * n_cols, (h + 1) * n_cols)
        wide_ref[0:all_chans, at] = pltpu.roll(ext, width - 1, 1)[:, :n_cols].astype(BF16)
        wide_ref[all_chans : 2 * all_chans, at] = mid
        wide_ref[2 * all_chans :, at] = pltpu.roll(ext, 1, 1)[:, :n_cols].astype(BF16)
    total = None
    for a in range(3):
        at = slice((2 - a) * n_cols, (2 - a + n_rows) * n_cols)
        part = dot_nn(kernel_ref[a], wide_ref[:, at])
        total = part if total is None else total + part
    out_ref[...] = total


def back(index, kernel, pieces, side, n_cols):
    n_ext, all_chans = side.shape[0], side.shape[1]
    n_out = kernel.shape[1]
    return call(
        functools.partial(back_kernel, n_cols, len(pieces)),
        jax.ShapeDtypeStruct((n_out, (n_ext - 2) * n_cols), F32),
        [smem_spec()] + [vmem_spec()] * (2 + 2 * len(pieces)),
        [pltpu.VMEM((3 * all_chans, n_ext * n_cols), BF16)],
        2 * n_ext * 9 * all_chans * n_out * n_cols,
        n_ext * all_chans * n_cols * 2,
        "back",
    )(index, kernel, *[x for piece in pieces for x in piece], side)


def grads_kernel(
    split, chans, index_ref, kernel_ref, gain_ref, own_ref, edge_ref, peer_ref, peer_edge_ref,
    side_ref, cot_ref, back_ref, hidden_ref, *rest,
):
    rest = list(rest)
    if split:
        keep_out, give_out = rest.pop(0), rest.pop(0)
    else:
        all_out = rest.pop(0)
    taps_ref, logs_ref, wide_ref, out_left_ref, pre_left_ref, acc_ref = rest
    n_rows, own, n_cols = cot_ref.shape
    n_hidden = kernel_ref.shape[1]
    taps_rows = 3 * chans
    width = n_cols + LANES
    tile, chan, sub, n_tile = index_ref[0], index_ref[1], index_ref[2], index_ref[3]
    keep_two = lane_mask((1, width), n_cols, sub, 2)

    log_line = iota((16, width), 0)
    data = n_rows * chans
    middle_rows = data + 2 * n_rows
    edge_rows = 2 * chans + 8
    side_half = middle_rows + 2 * edge_rows
    lefts = [(own_ref, edge_ref)] + ([] if peer_ref is None else [(peer_ref, peer_edge_ref)])
    sources = []
    for i in range(n_rows + 4):
        found = []
        for p, (middle_ref, ends_ref) in enumerate(lefts):
            if 2 <= i < n_rows + 2:
                r = i - 2
                base, lines = r * chans, (data + r, data + n_rows + r)
                found.append((middle_ref, base, lines, p * side_half))
            else:
                e = i if i < 2 else i - n_rows
                start = e // 2 * edge_rows
                base = start + e % 2 * chans
                lines = (start + 2 * chans + e % 2, start + 2 * chans + 2 + e % 2)
                found.append((ends_ref, base, lines, p * side_half + middle_rows))
        sources.append(found)

    def gather(found, wanted):
        total = None
        for ref, base, lines, at in found:
            for line in [base] if wanted == chans else lines:
                ext = jnp.concatenate(
                    [
                        ref[line : line + wanted, :].astype(F32),
                        side_ref[at + line : at + line + wanted, :].astype(F32),
                    ],
                    axis=1,
                )
                total = ext if total is None else total + ext
        return total

    for i in range(n_rows + 4):
        ext = gather(sources[i], chans)
        density = gather(sources[i], 1)
        logs = jnp.log(1.0 + density)
        logs_ref[i] = logs
        shrink = jnp.where(keep_two, 1.0 / (1.0 + density), 0.0)
        feats = ext * shrink
        at = slice(i * width, (i + 1) * width)
        taps_ref[0:chans, at] = pltpu.roll(feats, 1, 1).astype(BF16)
        taps_ref[chans : 2 * chans, at] = feats.astype(BF16)
        taps_ref[2 * chans : taps_rows, at] = pltpu.roll(feats, width - 1, 1).astype(BF16)
        high = logs.astype(BF16).astype(F32)
        middle = (logs - high).astype(BF16).astype(F32)
        taps_ref[taps_rows:, at] = jnp.where(
            log_line == 0,
            high,
            jnp.where(log_line == 1, middle, jnp.where(log_line == 2, logs - high - middle, 0.0)),
        ).astype(BF16)

    nothing = jnp.zeros((own, n_cols), BF16)
    for h in range(n_rows + 2):
        for a in range(3):
            inside = 0 <= h - a < n_rows
            put = slice(a * own, (a + 1) * own)
            out_left_ref[put, h * n_cols : (h + 1) * n_cols] = cot_ref[h - a] if inside else nothing
            if not inside:
                pre_left_ref[put, h * width : h * width + n_cols] = nothing
        pre_left_ref[:, h * width + n_cols : (h + 1) * width] = jnp.zeros((3 * own, LANES), BF16)

    gain = gain_ref[:, 0:1]
    keep_one = lane_mask((1, width), n_cols, sub, 1)
    group = 2
    for first in range(0, n_rows + 2, group):
        pre_all = None
        for a in range(3):
            at = slice((first + a) * width, (first + a + group) * width)
            part = dot_nn(kernel_ref[a], taps_ref[0:taps_rows, at])
            pre_all = part if pre_all is None else pre_all + part
        for k in range(group):
            h = first + k
            pre = pre_all[:, k * width : (k + 1) * width] + gain * logs_ref[h + 1]
            at = slice(h * n_cols, (h + 1) * n_cols)
            keep = keep_one
            if h == 0:
                keep = keep & (tile > 0)
            elif h == n_rows + 1:
                keep = keep & (tile < n_tile - 1)
            else:
                mine = pre[0:own, :n_cols]
                for c in range(1, n_hidden // own):
                    mine = jnp.where(chan == c, pre[c * own : (c + 1) * own, :n_cols], mine)
                s = 0.5 + 0.5 * jnp.tanh(0.5 * mine)
                there = slice((h - 1) * n_cols, h * n_cols)
                grad = (back_ref[:, there] * s * (1.0 + mine * (1.0 - s))).astype(BF16)
                for a in range(3):
                    put = (h - 1 + a) * width
                    pre_left_ref[a * own : (a + 1) * own, put : put + n_cols] = grad
            half = 0.5 * pre
            hidden = jnp.where(keep, half + half * jnp.tanh(half), 0.0)
            hidden_ref[h] = hidden.astype(BF16)
            wide_ref[0:n_hidden, at] = pltpu.roll(hidden, 1, 1)[:, :n_cols].astype(BF16)
            wide_ref[n_hidden : 2 * n_hidden, at] = hidden[:, :n_cols].astype(BF16)
            wide_ref[2 * n_hidden :, at] = pltpu.roll(hidden, width - 1, 1)[:, :n_cols].astype(BF16)

    three = 3 * own
    lanes = 3 * n_hidden
    half_rows = taps_rows // 2
    acc_ref[0:three, :] = dot_nt(out_left_ref[...], wide_ref[...])
    one = dot_nt(taps_ref[:, width : (n_rows + 3) * width], pre_left_ref[...])
    acc_ref[three:, :] = jnp.zeros((acc_ref.shape[0] - three, lanes), F32)
    acc_ref[three : three + half_rows, 0:three] = one[0:half_rows]
    acc_ref[three : three + half_rows, lanes // 2 : lanes // 2 + three] = one[half_rows:taps_rows]
    gains = one[taps_rows : taps_rows + 1] + one[taps_rows + 1 : taps_rows + 2] + one[taps_rows + 2 : taps_rows + 3]
    acc_ref[three + half_rows : three + half_rows + 1, 0:three] = gains
    if split:
        half = acc_ref.shape[0] // 2
        keep_out[...] = acc_ref[pl.ds(pl.multiple_of(sub * half, half), half), :]
        give_out[...] = acc_ref[pl.ds(pl.multiple_of((1 - sub) * half, half), half), :].astype(BF16)
    else:
        all_out[...] = acc_ref[...]


def grads(split, index, kernel, gain, own, edge, peer, peer_edge, side, cot, back_out):
    n_rows, n_own, n_cols = cot.shape
    n_hidden = kernel.shape[1]
    chans = kernel.shape[2] // 3
    width = n_cols + LANES
    lanes = 3 * n_hidden
    acc_rows = 3 * n_own + 3 * chans // 2 + 32
    body = functools.partial(grads_kernel, split, chans)
    ins = [own, edge, peer, peer_edge, side, cot, back_out]
    if peer is None:
        ins = [own, edge, side, cot, back_out]
        body = lambda i, k, g, o, e, *rest: grads_kernel(split, chans, i, k, g, o, e, None, None, *rest)
    outs = [jax.ShapeDtypeStruct((n_rows + 2, n_hidden, width), BF16)]
    if split:
        outs.append(jax.ShapeDtypeStruct((acc_rows // 2, lanes), F32))
        outs.append(jax.ShapeDtypeStruct((acc_rows // 2, lanes), BF16))
    else:
        outs.append(jax.ShapeDtypeStruct((acc_rows, lanes), F32))
    return call(
        body,
        outs,
        [smem_spec()] + [vmem_spec()] * (2 + len(ins)),
        [
            pltpu.VMEM((3 * chans + 16, (n_rows + 4) * width), BF16),
            pltpu.VMEM((n_rows + 4, 1, width), F32),
            pltpu.VMEM((3 * n_hidden, (n_rows + 2) * n_cols), BF16),
            pltpu.VMEM((3 * n_own, (n_rows + 2) * n_cols), BF16),
            pltpu.VMEM((3 * n_own, (n_rows + 2) * width), BF16),
            pltpu.VMEM((acc_rows, lanes), F32),
        ],
        2 * (n_rows + 2) * 9 * n_cols * n_hidden * (n_own + chans),
        (n_rows + 2) * 3 * n_hidden * n_cols * 2,
        "grads",
    )(index, kernel, gain, *ins)


def encode_kernel(kernel_ref, hidden_ref, out_ref, wide_ref):
    n_ext, n_hidden, width = hidden_ref.shape
    n_rows = n_ext - 2
    n_cols = width - LANES
    for h in range(n_ext):
        hidden = hidden_ref[h].astype(F32)
        at = slice(h * n_cols, (h + 1) * n_cols)
        wide_ref[0:n_hidden, at] = pltpu.roll(hidden, 1, 1)[:, :n_cols].astype(BF16)
        wide_ref[n_hidden : 2 * n_hidden, at] = hidden_ref[h, :, 0:n_cols]
        wide_ref[2 * n_hidden :, at] = pltpu.roll(hidden, width - 1, 1)[:, :n_cols].astype(BF16)
    total = None
    for a in range(3):
        part = dot_nn(kernel_ref[a], wide_ref[:, a * n_cols : (a + n_rows) * n_cols])
        total = part if total is None else total + part
    for r in range(n_rows):
        out_ref[r] = total[:, r * n_cols : (r + 1) * n_cols].astype(BF16)


def encode(kernel, hidden):
    n_ext, n_hidden, width = hidden.shape
    own = kernel.shape[1]
    n_cols = width - LANES
    return call(
        encode_kernel,
        jax.ShapeDtypeStruct((n_ext - 2, own, n_cols), BF16),
        [vmem_spec()] * 2,
        [pltpu.VMEM((3 * n_hidden, n_ext * n_cols), BF16)],
        2 * n_ext * 9 * own * n_hidden * n_cols,
        hidden.size * 2,
        "encode",
    )(kernel, hidden)


def quarters_kernel(index_ref, keep_ref, got_ref, *outs):
    n = len(outs)
    rows = keep_ref.shape[0] // n
    for k in range(n):
        other = jnp.bitwise_xor(index_ref[0], k)
        at = pl.ds(pl.multiple_of(other * rows, rows), rows)
        outs[k][...] = (keep_ref[at, :] + got_ref[at, :].astype(F32)).astype(outs[k].dtype)


def quarters(index, keep, got, n):
    rows, lanes = keep.shape
    return call(
        quarters_kernel,
        [jax.ShapeDtypeStruct((rows // n, lanes), F32 if k == 0 else BF16) for k in range(n)],
        [smem_spec(), vmem_spec(), vmem_spec()],
        [],
        rows * lanes,
        rows * lanes * 8,
        "quarters",
    )(index, keep, got)


def finish_kernel(scale, own, chans, index_ref, mine_ref, other_ref, two_ref, one_ref, gain_ref, all_ref):
    n, rows, lanes = mine_ref.shape
    n_hidden = lanes // 3
    tile, sub = index_ref[0], index_ref[2]
    for k in range(n):
        at = jnp.bitwise_xor(tile, k) * rows
        here = pl.multiple_of(sub * (n * rows) + at, rows)
        there = pl.multiple_of((1 - sub) * (n * rows) + at, rows)
        all_ref[pl.ds(here, rows), :] = mine_ref[k].astype(F32) * scale
        all_ref[pl.ds(there, rows), :] = other_ref[k].astype(F32) * scale
    half_rows = 3 * chans // 2
    for a in range(3):
        for b in range(3):
            two_ref[a, b] = all_ref[a * own : (a + 1) * own, b * n_hidden : (b + 1) * n_hidden]
        lines = jnp.concatenate(
            [
                all_ref[3 * own : 3 * own + half_rows, s + a * own : s + (a + 1) * own]
                for s in (0, lanes // 2)
            ],
            axis=0,
        )
        for b in range(3):
            one_ref[a, b] = lines[b * chans : (b + 1) * chans]
    gain_ref[...] = all_ref[3 * own + half_rows : 3 * own + half_rows + 1, own : 2 * own]


def finish(index, mine, other, scale, own, chans):
    n, rows, lanes = mine.shape
    n_hidden = lanes // 3
    return call(
        functools.partial(finish_kernel, scale, own, chans),
        [
            jax.ShapeDtypeStruct((3, 3, own, n_hidden), F32),
            jax.ShapeDtypeStruct((3, 3, chans, own), F32),
            jax.ShapeDtypeStruct((1, own), F32),
        ],
        [smem_spec(), vmem_spec(), vmem_spec()],
        [pltpu.VMEM((2 * n * rows, lanes), F32)],
        n * rows * lanes,
        n * rows * lanes * 12,
        "finish",
    )(index, mine, other)


def offer_kernel(index_ref, two_ref, one_ref, gain_ref, out_ref):
    own = two_ref.shape[2]
    chans = one_ref.shape[2]
    at = pl.ds(pl.multiple_of((1 - index_ref[1]) * own, own), own)
    gain = gain_ref[...]
    high = gain.astype(BF16).astype(F32)
    middle = (gain - high).astype(BF16).astype(F32)
    line = iota((8, own), 0)
    terms = jnp.where(
        line == 0, high, jnp.where(line == 1, middle, jnp.where(line == 2, gain - high - middle, 0.0))
    ).astype(BF16)
    for a in range(3):
        for b in range(3):
            out_ref[a, b, 0:own] = two_ref[a, b, :, at]
            out_ref[a, b, own : own + chans] = one_ref[a, b]
            out_ref[a, b, own + chans :] = terms


def offer(index, two, one, gain):
    own, chans = two.shape[2], one.shape[2]
    return call(
        offer_kernel,
        jax.ShapeDtypeStruct((3, 3, own + chans + 8, own), BF16),
        [smem_spec()] + [vmem_spec()] * 3,
        [],
        9 * own * (own + chans),
        9 * own * (own + chans) * 4,
        "offer",
    )(index, two, one, gain[None])


def arrange_kernel(index_ref, two_ref, one_ref, gain_ref, theirs_ref, back_ref, code_ref, first_ref, column_ref):
    own = two_ref.shape[2]
    chans = one_ref.shape[2]
    chan = index_ref[1]
    mine = pl.ds(pl.multiple_of(chan * own, own), own)
    peer = pl.ds(pl.multiple_of((1 - chan) * own, own), own)

    def turned(block):
        return block.astype(F32).T.astype(BF16)

    for a in range(3):
        for b in range(3):
            left = b * 2 * own
            back_ref[a, :, left : left + own] = turned(two_ref[a, b, :, mine])
            back_ref[a, :, left + own : left + 2 * own] = turned(theirs_ref[a, b, 0:own])
            code_ref[a, :, left : left + 2 * own] = two_ref[a, b]
        first_ref[a, mine, :] = turned(jnp.concatenate([one_ref[a, b] for b in range(3)], axis=0))
        first_ref[a, peer, :] = turned(
            jnp.concatenate([theirs_ref[a, b, own : own + chans] for b in range(3)], axis=0)
        )
    terms = theirs_ref[0, 0, own + chans :].astype(F32)
    other = terms[0:1] + terms[1:2] + terms[2:3]
    column_ref[mine, :] = jnp.broadcast_to(gain_ref[...], (own, own)).T
    column_ref[peer, :] = jnp.broadcast_to(other, (own, own)).T


def arrange(index, two, one, gain, theirs):
    own, chans = two.shape[2], one.shape[2]
    return call(
        arrange_kernel,
        [
            jax.ShapeDtypeStruct((3, own, 6 * own), BF16),
            jax.ShapeDtypeStruct((3, own, 6 * own), BF16),
            jax.ShapeDtypeStruct((3, 2 * own, 3 * chans), BF16),
            jax.ShapeDtypeStruct((2 * own, LANES), F32),
        ],
        [smem_spec()] + [vmem_spec()] * 4,
        [],
        9 * own * (4 * own + 2 * chans),
        9 * own * (4 * own + 2 * chans) * 4,
        "arrange",
    )(index, two, one, gain[None], theirs)


def step_perm(count, by):
    return [(i, i + by) for i in range(count) if 0 <= i + by < count]


def swap_sub(x):
    return lax.ppermute(x, "sub", [(0, 1), (1, 0)])


def swap_chan(x):
    return lax.ppermute(x, "chan", [(0, 1), (1, 0)])


def swap_tile(x, n_tile, k):
    return lax.ppermute(x, "tile", [(i, i ^ k) for i in range(n_tile)])


def near(block, sub):
    n_cols = block.shape[-1]
    return jnp.where(sub == 0, block[..., n_cols - LANES :], block[..., :LANES])


def side_rows(parts, sub):
    columns = [
        jnp.concatenate([near(edge[: edge.shape[0] // 2], sub), near(mid, sub), near(edge[edge.shape[0] // 2 :], sub)], axis=0)
        for mid, edge in parts
    ]
    both = columns[0] if len(columns) == 1 else jnp.concatenate(columns, axis=1)
    return swap_sub(both)


def body(obs_values, obs_weight, obs_tile, obs_cell, conv_one, conv_two, density_gain, cotangent):
    own, n_rows, n_cols = cotangent.shape
    n_tile = lax.axis_size("tile")
    n_sub = lax.axis_size("sub")
    n_chan = lax.axis_size("chan")
    pair = n_chan == 2 and own == LANES
    n_tiles = n_tile * n_sub
    chans = obs_values.shape[1]
    n_hidden = own * n_chan
    cap = 2 * obs_values.shape[0] // n_tiles
    tile, chan, sub = lax.axis_index("tile"), lax.axis_index("chan"), lax.axis_index("sub")
    index = jnp.stack([tile, chan, sub, jnp.int32(n_tile), tile * n_sub + sub]).astype(jnp.int32)

    bottom, top = cotangent[:, -1], cotangent[:, 0]
    one_own = conv_one.transpose(0, 1, 3, 2)
    if pair:
        offered = offer(index, conv_two, one_own, density_gain)
        obs_tile, bottom, top, offered = lax.optimization_barrier((obs_tile, bottom, top, offered))
        theirs = swap_chan(offered)
    low = lax.ppermute(bottom, "tile", step_perm(n_tile, 1))
    high = lax.ppermute(top, "tile", step_perm(n_tile, -1))

    few = n_tiles == 8
    sent = route(index, obs_values, obs_weight, obs_tile, obs_cell, n_tiles, cap, few)
    if pair:
        sent, low, high, theirs = lax.optimization_barrier((sent, low, high, theirs))
    if few:
        far = [swap_tile(sent[k + 1], n_tile, k) for k in (1, 2, 3)]
        beside = swap_sub(sent[1])
        steps = [
            [(sent[0], (0,)), (beside, (0,))],
            [(far[0], (0,)), (swap_sub(far[0][1:]), (0,)), (far[1], (0,)), (far[2], (0,))],
            [(swap_sub(far[1][1:]), (0,)), (swap_sub(far[2][1:]), (0,))],
        ]
    else:
        got = lax.all_to_all(sent[0], ("tile", "sub"), split_axis=0, concat_axis=0, tiled=True)
        steps = [[(got, tuple(range(n_tiles)))]]

    if pair:
        cotangent, _ = lax.optimization_barrier((cotangent, sent[0]))
        cot = cotangent.transpose(1, 0, 2)
        cot_edge = jnp.stack([low, high])
        cot_peer = swap_chan(cotangent)
        pieces = [(cot, cot_edge), (cot_peer.transpose(1, 0, 2), swap_chan(cot_edge))]
    else:
        cot = cotangent.transpose(1, 0, 2)
        pieces = [
            (
                lax.all_gather(cot, "chan", axis=1, tiled=True),
                lax.all_gather(jnp.stack([low, high]), "chan", axis=1, tiled=True),
            )
        ]
    cot_side = side_rows(pieces, sub)

    if pair:
        back_weights, code_weights, one_weights, gain = arrange(
            index, conv_two, one_own, density_gain, theirs
        )
    else:
        columns = lax.all_to_all(conv_two, "chan", split_axis=3, concat_axis=2, tiled=True)
        one_full = lax.all_gather(one_own, "chan", axis=3, tiled=True)
        gain = lax.all_gather(density_gain, "chan", axis=0, tiled=True)
        gain = jnp.broadcast_to(gain[:, None], (n_hidden, LANES))
        code_weights = conv_two.transpose(0, 2, 1, 3).reshape(3, own, 3 * n_hidden)
        back_weights = columns.transpose(0, 3, 1, 2).reshape(3, own, 3 * n_hidden)
        one_weights = one_full.transpose(0, 3, 1, 2).reshape(3, n_hidden, 3 * chans)

    part = None
    for step in steps[:-1]:
        part = grid(step, part, False, n_rows, n_cols)[0]
    if few:
        part, back_weights, one_weights, code_weights, gain = lax.optimization_barrier(
            (part, back_weights, one_weights, code_weights, gain)
        )
    part, message, up, down = grid(steps[-1], part, True, n_rows, n_cols)
    data = n_rows * chans
    if not pair:
        part = lax.psum(part, "chan")
        density = part[data : data + n_rows]
        dense = density.astype(BF16)
        rest = (density - dense.astype(F32)).astype(BF16)
        message = jnp.concatenate([part[:data].astype(BF16), dense, rest], axis=0)
        blank = jnp.zeros((4, n_cols), BF16)
        up, down = [
            jnp.concatenate(
                [message[r * chans : (r + 2) * chans], dense[r : r + 2], rest[r : r + 2], blank], axis=0
            )
            for r in (n_rows - 2, 0)
        ]
    low = lax.ppermute(up, "tile", step_perm(n_tile, 1))
    high = lax.ppermute(down, "tile", step_perm(n_tile, -1))
    edge = jnp.concatenate([low, high], axis=0)
    back_out = back(index, back_weights, pieces, cot_side, n_cols)
    if pair:
        peer, peer_edge = swap_chan(message), swap_chan(edge)
        peer, peer_edge, back_out = lax.optimization_barrier((peer, peer_edge, back_out))
        side = [message, edge, peer, peer_edge]
    else:
        peer, peer_edge = None, None
        side = [message, edge]
    side = swap_sub(jnp.concatenate([near(x, sub) for x in side], axis=0))

    scale = 1.0 / math.sqrt(n_tiles * n_rows * n_cols)
    split = pair and n_tile == 4
    hidden, *partial = grads(
        split, index, one_weights, gain, part, edge, peer, peer_edge, side, cot, back_out
    )
    encoded = encode(code_weights, hidden).transpose(1, 0, 2)

    if split:
        keep, give = partial
        mine, *others = quarters(index, keep, swap_sub(give), n_tile)
        for k, other in enumerate(others, 1):
            mine = mine + swap_tile(other, n_tile, k).astype(F32)
        mine, encoded = lax.optimization_barrier((mine.astype(BF16), encoded))
        mine = jnp.stack([mine] + [swap_tile(mine, n_tile, k) for k in range(1, n_tile)])
        grad_two, grad_one, grad_gain = finish(index, mine, swap_sub(mine), scale, own, chans)
        return encoded, grad_one.transpose(0, 1, 3, 2), grad_two, grad_gain[0]

    total = lax.psum(partial[0], ("tile", "sub")) * scale
    three = 3 * own
    half_rows = 3 * chans // 2
    lanes = 3 * n_hidden
    grad_two = total[:three].reshape(3, own, 3, n_hidden).transpose(0, 2, 1, 3)
    lines = total[three : three + half_rows]
    lines = jnp.concatenate([lines[:, :three], lines[:, lanes // 2 : lanes // 2 + three]], axis=0)
    grad_one = lines.reshape(3, chans, 3, own).transpose(2, 0, 3, 1)
    grad_gain = total[three + half_rows, own : 2 * own]
    return encoded, grad_one, grad_two, grad_gain


def solution(mesh):
    placed = (
        P(("member", "tile", "chan", "sub"), None),
        P(("member", "tile", "chan", "sub")),
        P(("member", "tile", "chan", "sub")),
        P(("member", "tile", "chan", "sub")),
        P(None, None, "chan", None),
        P(None, None, "chan", None),
        P("chan"),
        P(("member", "chan"), "tile", "sub"),
    )
    return jax.shard_map(
        body,
        mesh=mesh,
        in_specs=placed,
        out_specs=(
            P(("member", "chan"), "tile", "sub"),
            P("member", None, "chan", None),
            P("member", None, "chan", None),
            P(("member", "chan")),
        ),
        check_vma=False,
    )
```

```python
import functools
import math

import jax
import jax.numpy as jnp
from jax import lax
from jax.experimental import pallas as pl
from jax.experimental.pallas import tpu as pltpu
from jax.sharding import PartitionSpec as P

BF16 = jnp.bfloat16
F32 = jnp.float32
LANES = 128
BLOCK = 256
META = 8
MIB = 1024 * 1024


def dot_nt(a, b):
    return lax.dot_general(a, b, (((1,), (1,)), ((), ())), preferred_element_type=F32)


def dot_nn(a, b):
    return lax.dot_general(a, b, (((1,), (0,)), ((), ())), preferred_element_type=F32)


def iota(shape, dim, dtype=jnp.int32):
    return lax.broadcasted_iota(jnp.int32, shape, dim).astype(dtype)


def vmem_spec():
    return pl.BlockSpec(memory_space=pltpu.VMEM)


def smem_spec():
    return pl.BlockSpec(memory_space=pltpu.SMEM)


def call(kernel, out_shape, in_specs, scratch, flops, moved, name, vmem=32):
    n_out = len(out_shape) if isinstance(out_shape, (tuple, list)) else None
    out_specs = vmem_spec() if n_out is None else [vmem_spec() for _ in range(n_out)]
    return pl.pallas_call(
        kernel,
        out_shape=out_shape,
        in_specs=in_specs,
        out_specs=out_specs,
        scratch_shapes=scratch,
        compiler_params=pltpu.CompilerParams(vmem_limit_bytes=vmem * MIB),
        cost_estimate=pl.CostEstimate(flops=flops, bytes_accessed=moved, transcendentals=0),
        name=name,
    )


def route_kernel(n_tiles, cap, relative, index_ref, tile_hbm, weight_hbm, cell_hbm, values_hbm, *rest):
    n_outs = 5 if relative else 1
    outs = rest[:n_outs]
    (tile_ref, weight_ref, cell_ref, values_ref, onehot_ref, slot_ref, weight32_ref, all_ref,
     info_ref, info_smem, sems) = rest[n_outs:]
    loads = [
        pltpu.make_async_copy(tile_hbm, tile_ref, sems.at[0]),
        pltpu.make_async_copy(weight_hbm, weight_ref, sems.at[1]),
        pltpu.make_async_copy(cell_hbm, cell_ref, sems.at[2]),
        pltpu.make_async_copy(values_hbm, values_ref, sems.at[3]),
    ]
    for load in loads:
        load.start()
    all_ref[...] = jnp.zeros(all_ref.shape, BF16)
    loads[0].wait()
    n_lines = tile_ref.shape[0]
    n_blocks = n_lines // 2
    n_obs_chans = values_ref.shape[0]
    pairs = n_tiles * n_lines
    tiles = tile_ref[...]
    for t in range(n_tiles):
        onehot_ref[t * n_lines : (t + 1) * n_lines, :] = jnp.where(tiles == t, 1.0, 0.0).astype(BF16)
    onehot = onehot_ref[...]
    upper = jnp.where(
        iota((LANES, LANES), 0) <= iota((LANES, LANES), 1), 1.0, 0.0
    ).astype(BF16)
    here = iota((pairs, pairs), 0)
    there = iota((pairs, pairs), 1)
    earlier = jnp.where(
        (here // n_lines == there // n_lines) & (there < here), 1.0, 0.0
    ).astype(BF16)
    total_row = dot_nt(jnp.ones((8, LANES), BF16), onehot)
    offset_row = dot_nt(total_row.astype(BF16), earlier)
    odd = iota((8, pairs), 1) % 2 == 1
    both = jnp.where(odd, total_row + pltpu.roll(total_row, 1, 1), 0.0)
    spill = jnp.where(jnp.max(both, axis=1, keepdims=True) > LANES, 1.0, 0.0)
    info_ref[...] = jnp.where(
        iota((8, pairs), 0) == 0, offset_row, spill
    ).astype(jnp.int32)
    copy = pltpu.make_async_copy(info_ref, info_smem, sems.at[4])
    copy.start()
    cum = dot_nn(onehot, upper)
    totals = dot_nn(onehot, jnp.ones((LANES, LANES), BF16))
    offset = dot_nn(earlier, totals.astype(BF16))
    place = cum + offset - 1.0
    slots = jnp.zeros(tiles.shape, F32)
    for t in range(n_tiles):
        slots = jnp.where(tiles == t, place[t * n_lines : (t + 1) * n_lines, :], slots)
    slot_ref[...] = slots
    for load in loads[1:]:
        load.wait()
    weight32_ref[...] = weight_ref[...].astype(F32)
    meta_row = iota((16, BLOCK), 0)
    window = iota((LANES, BLOCK), 0, F32)
    blank = jnp.zeros((n_obs_chans + 16, LANES), F32)
    copy.wait()

    def line(ref, b):
        return jnp.concatenate([ref[pl.ds(2 * b, 1), :], ref[pl.ds(2 * b + 1, 1), :]], axis=1)

    def columns(b):
        values = values_ref[:, pl.ds(pl.multiple_of(b * BLOCK, BLOCK), BLOCK)]
        cell = line(cell_ref, b)
        weight = line(weight32_ref, b)
        high = (cell // LANES).astype(F32)
        low = (cell % LANES).astype(F32)
        meta = jnp.where(
            meta_row == 0,
            weight,
            jnp.where(meta_row == 1, high, jnp.where(meta_row == 2, low, 0.0)),
        ).astype(BF16)
        return jnp.concatenate([values, meta], axis=0)

    def add(t, wide, tile, slot, start):
        key = jnp.where(tile == t, slot - start.astype(F32), -1.0)
        chosen = jnp.where(window == key, 1.0, 0.0).astype(BF16)
        part = jnp.concatenate([dot_nt(wide, chosen), blank], axis=1)
        base = jnp.minimum(start // LANES * LANES, cap - BLOCK)
        turn = jnp.bitwise_and(start - base, BLOCK - 1)
        part = pltpu.roll(part, turn, 1)[: n_obs_chans + META].astype(BF16)
        where = pl.ds(pl.multiple_of(base, LANES), BLOCK)
        all_ref[t, :, where] = all_ref[t, :, where] + part

    def place_block(b, skip):
        wide = columns(b)
        tile = line(tile_ref, b)
        slot = line(slot_ref, b)
        for t in range(n_tiles):
            add(t, wide, tile, slot, info_smem[0, t * n_lines + 2 * b] + skip)

    def first_some(i, carry):
        for j in range(8):
            place_block(8 * i + j, 0)
        return carry

    lax.fori_loop(0, n_blocks // 8, first_some, 0)

    @pl.when(info_smem[1, 0] > 0)
    def _():
        def rest_of(b, carry):
            place_block(b, LANES)
            return carry

        lax.fori_loop(0, n_blocks, rest_of, 0)

    if relative:
        me = index_ref[4]
        outs[0][0] = all_ref[me]
        outs[1][0] = all_ref[jnp.bitwise_xor(me, 1)]
        for k in range(1, 4):
            for s in range(2):
                outs[k + 1][s] = all_ref[jnp.bitwise_xor(me, 2 * k + s)]
    else:
        outs[0][...] = all_ref[...]


def route(index, obs_values, obs_weight, obs_tile, obs_cell, n_tiles, cap, relative):
    n_obs, chans = obs_values.shape
    n_lines = n_obs // LANES
    rows = chans + META
    outs = [(n, rows, cap) for n in ((1, 1, 2, 2, 2) if relative else (n_tiles,))]
    hbm_spec = pl.BlockSpec(memory_space=pltpu.HBM)
    return call(
        functools.partial(route_kernel, n_tiles, cap, relative),
        [jax.ShapeDtypeStruct(shape, BF16) for shape in outs],
        [smem_spec()] + [hbm_spec] * 4,
        [
            pltpu.VMEM((n_lines, LANES), jnp.int32),
            pltpu.VMEM((n_lines, LANES), BF16),
            pltpu.VMEM((n_lines, LANES), jnp.int32),
            pltpu.VMEM((chans, n_obs), BF16),
            pltpu.VMEM((n_tiles * n_lines, LANES), BF16),
            pltpu.VMEM((n_lines, LANES), F32),
            pltpu.VMEM((n_lines, LANES), F32),
            pltpu.VMEM((n_tiles, rows, cap), BF16),
            pltpu.VMEM((8, n_tiles * n_lines), jnp.int32),
            pltpu.SMEM((8, n_tiles * n_lines), jnp.int32),
            pltpu.SemaphoreType.DMA((5,)),
        ],
        2 * n_obs * n_tiles * BLOCK * 80,
        n_tiles * rows * cap * 2,
        "route",
    )(
        index,
        obs_tile.reshape(n_lines, LANES),
        obs_weight.reshape(n_lines, LANES),
        obs_cell.reshape(n_lines, LANES),
        obs_values.T,
    )


def grid_kernel(n_rows, n_cols, group, takes, first, last, *rest):
    rest = list(rest)
    got_refs = [rest.pop(0) for _ in takes]
    senders = [ref.at[i] for ref, picked in zip(got_refs, takes) for i in picked]
    before_ref = None if first else rest.pop(0)
    own_ref = rest.pop(0)
    send_refs = [rest.pop(0) for _ in range(3)] if last else None
    left_ref, right_ref = rest
    n_send = len(senders)
    rows, cap = senders[0].shape
    chans = rows - META
    data = n_rows * chans
    per_row = n_cols // LANES
    columns = iota((n_cols, cap), 0, F32)
    row_ids = iota((2 * n_rows, cap), 0, F32)
    total = None
    for g in range(n_send // group):
        slot = g % 2
        for i in range(group):
            sender = senders[g * group + i]
            at = slice(i * cap, (i + 1) * cap)
            values = sender[0:chans, :]
            meta = sender[chans:rows, :].astype(F32)
            weight = meta[0:1]
            high = meta[1:2]
            row = jnp.floor((high + 0.5) * (1.0 / per_row))
            column = (high - row * per_row) * LANES + meta[2:3]
            right_ref[slot, :, at] = jnp.where(columns == column, weight, 0.0).astype(BF16)
            in_row = jnp.where(row_ids == row, 1.0, 0.0)
            for r in range(n_rows):
                left_ref[slot, r * chans : (r + 1) * chans, at] = values * in_row[r : r + 1].astype(BF16)
            left_ref[slot, data:, at] = in_row.astype(BF16)
        part = dot_nt(left_ref[slot], right_ref[slot])
        total = part if total is None else total + part
    if before_ref is not None:
        total = total + before_ref[...]
    own_ref[...] = total
    if last:
        send_ref, low_ref, high_ref = send_refs
        density = own_ref[data : data + n_rows, :]
        high = density.astype(BF16).astype(F32)
        low = density - high
        send_ref[0:data, :] = own_ref[0:data, :].astype(BF16)
        send_ref[data:, :] = jnp.concatenate([high, low], axis=0).astype(BF16)
        for ref, at in ((high_ref, 0), (low_ref, n_rows - 2)):
            ref[0 : 2 * chans, :] = own_ref[at * chans : (at + 2) * chans, :].astype(BF16)
            ref[2 * chans :, :] = jnp.concatenate(
                [high[at : at + 2], low[at : at + 2], jnp.zeros((4, n_cols), F32)], axis=0
            ).astype(BF16)


def grid(got, before, last, n_rows, n_cols):
    takes = [picked for _, picked in got]
    got = [x for x, _ in got]
    n_send = sum(len(picked) for picked in takes)
    rows, cap = got[0].shape[1:]
    group = max(1, min(2048 // cap, n_send))
    chans = rows - META
    total = n_rows * chans + 2 * n_rows
    outs = [jax.ShapeDtypeStruct((total, n_cols), F32)]
    if last:
        outs.append(jax.ShapeDtypeStruct((total, n_cols), BF16))
        outs += [jax.ShapeDtypeStruct((2 * chans + 8, n_cols), BF16)] * 2
    ins = list(got) if before is None else list(got) + [before]
    return call(
        functools.partial(grid_kernel, n_rows, n_cols, group, takes, before is None, last),
        outs,
        [vmem_spec()] * len(ins),
        [
            pltpu.VMEM((2, total, group * cap), BF16),
            pltpu.VMEM((2, n_cols, group * cap), BF16),
        ],
        2 * n_send * cap * total * n_cols,
        n_send * rows * cap * 2,
        "grid_last" if last else "grid_part",
    )(*ins)


def lane_mask(shape, n_cols, sub, depth):
    lane = iota(shape, 1)
    width = n_cols + LANES
    keep_right = (lane >= n_cols) & (lane < n_cols + depth) & (sub == 0)
    keep_left = (lane >= width - depth) & (sub == 1)
    return (lane < n_cols) | keep_right | keep_left


def back_kernel(n_cols, n_pieces, index_ref, kernel_ref, *rest):
    pieces = [(rest[2 * i], rest[2 * i + 1]) for i in range(n_pieces)]
    side_ref, out_ref, wide_ref = rest[2 * n_pieces :]
    n_ext, all_chans = side_ref.shape[0], side_ref.shape[1]
    n_rows = n_ext - 2
    width = n_cols + LANES
    keep = lane_mask((1, width), n_cols, index_ref[2], 1)
    for h in range(n_ext):
        if h == 0 or h == n_ext - 1:
            mids = [edge[min(h, 1)] for _, edge in pieces]
        else:
            mids = [middle[h - 1] for middle, _ in pieces]
        mid = mids[0] if n_pieces == 1 else jnp.concatenate(mids, axis=0)
        ext = jnp.concatenate([mid, side_ref[h]], axis=1).astype(F32)
        ext = jnp.where(keep, ext, 0.0)
        at = slice(h * n_cols, (h + 1) * n_cols)
        wide_ref[0:all_chans, at] = pltpu.roll(ext, width - 1, 1)[:, :n_cols].astype(BF16)
        wide_ref[all_chans : 2 * all_chans, at] = mid
        wide_ref[2 * all_chans :, at] = pltpu.roll(ext, 1, 1)[:, :n_cols].astype(BF16)
    total = None
    for a in range(3):
        at = slice((2 - a) * n_cols, (2 - a + n_rows) * n_cols)
        part = dot_nn(kernel_ref[a], wide_ref[:, at])
        total = part if total is None else total + part
    out_ref[...] = total


def back(index, kernel, pieces, side, n_cols):
    n_ext, all_chans = side.shape[0], side.shape[1]
    n_out = kernel.shape[1]
    return call(
        functools.partial(back_kernel, n_cols, len(pieces)),
        jax.ShapeDtypeStruct((n_out, (n_ext - 2) * n_cols), F32),
        [smem_spec()] + [vmem_spec()] * (2 + 2 * len(pieces)),
        [pltpu.VMEM((3 * all_chans, n_ext * n_cols), BF16)],
        2 * n_ext * 9 * all_chans * n_out * n_cols,
        n_ext * all_chans * n_cols * 2,
        "back",
    )(index, kernel, *[x for piece in pieces for x in piece], side)


def grads_kernel(
    split, chans, index_ref, kernel_ref, gain_ref, own_ref, edge_ref, peer_ref, peer_edge_ref,
    side_ref, cot_ref, back_ref, hidden_ref, *rest,
):
    rest = list(rest)
    if split:
        keep_out, give_out = rest.pop(0), rest.pop(0)
    else:
        all_out = rest.pop(0)
    taps_ref, logs_ref, wide_ref, out_left_ref, pre_left_ref, acc_ref = rest
    n_rows, own, n_cols = cot_ref.shape
    n_hidden = kernel_ref.shape[1]
    taps_rows = 3 * chans
    width = n_cols + LANES
    tile, chan, sub, n_tile = index_ref[0], index_ref[1], index_ref[2], index_ref[3]
    keep_two = lane_mask((1, width), n_cols, sub, 2)

    log_line = iota((16, width), 0)
    data = n_rows * chans
    middle_rows = data + 2 * n_rows
    edge_rows = 2 * chans + 8
    side_half = middle_rows + 2 * edge_rows
    lefts = [(own_ref, edge_ref)] + ([] if peer_ref is None else [(peer_ref, peer_edge_ref)])
    sources = []
    for i in range(n_rows + 4):
        found = []
        for p, (middle_ref, ends_ref) in enumerate(lefts):
            if 2 <= i < n_rows + 2:
                r = i - 2
                base, lines = r * chans, (data + r, data + n_rows + r)
                found.append((middle_ref, base, lines, p * side_half))
            else:
                e = i if i < 2 else i - n_rows
                start = e // 2 * edge_rows
                base = start + e % 2 * chans
                lines = (start + 2 * chans + e % 2, start + 2 * chans + 2 + e % 2)
                found.append((ends_ref, base, lines, p * side_half + middle_rows))
        sources.append(found)

    def gather(found, wanted):
        total = None
        for ref, base, lines, at in found:
            for line in [base] if wanted == chans else lines:
                ext = jnp.concatenate(
                    [
                        ref[line : line + wanted, :].astype(F32),
                        side_ref[at + line : at + line + wanted, :].astype(F32),
                    ],
                    axis=1,
                )
                total = ext if total is None else total + ext
        return total

    for i in range(n_rows + 4):
        ext = gather(sources[i], chans)
        density = gather(sources[i], 1)
        logs = jnp.log(1.0 + density)
        logs_ref[i] = logs
        shrink = jnp.where(keep_two, 1.0 / (1.0 + density), 0.0)
        feats = ext * shrink
        at = slice(i * width, (i + 1) * width)
        taps_ref[0:chans, at] = pltpu.roll(feats, 1, 1).astype(BF16)
        taps_ref[chans : 2 * chans, at] = feats.astype(BF16)
        taps_ref[2 * chans : taps_rows, at] = pltpu.roll(feats, width - 1, 1).astype(BF16)
        high = logs.astype(BF16).astype(F32)
        middle = (logs - high).astype(BF16).astype(F32)
        taps_ref[taps_rows:, at] = jnp.where(
            log_line == 0,
            high,
            jnp.where(log_line == 1, middle, jnp.where(log_line == 2, logs - high - middle, 0.0)),
        ).astype(BF16)

    nothing = jnp.zeros((own, n_cols), BF16)
    for h in range(n_rows + 2):
        for a in range(3):
            inside = 0 <= h - a < n_rows
            put = slice(a * own, (a + 1) * own)
            out_left_ref[put, h * n_cols : (h + 1) * n_cols] = cot_ref[h - a] if inside else nothing
            if not inside:
                pre_left_ref[put, h * width : h * width + n_cols] = nothing
        pre_left_ref[:, h * width + n_cols : (h + 1) * width] = jnp.zeros((3 * own, LANES), BF16)

    gain = gain_ref[:, 0:1]
    keep_one = lane_mask((1, width), n_cols, sub, 1)
    group = 1
    for first in range(0, n_rows + 2, group):
        pre_all = None
        for a in range(3):
            at = slice((first + a) * width, (first + a + group) * width)
            part = dot_nn(kernel_ref[a], taps_ref[0:taps_rows, at])
            pre_all = part if pre_all is None else pre_all + part
        for k in range(group):
            h = first + k
            pre = pre_all[:, k * width : (k + 1) * width] + gain * logs_ref[h + 1]
            at = slice(h * n_cols, (h + 1) * n_cols)
            keep = keep_one
            if h == 0:
                keep = keep & (tile > 0)
            elif h == n_rows + 1:
                keep = keep & (tile < n_tile - 1)
            else:
                mine = pre[0:own, :n_cols]
                for c in range(1, n_hidden // own):
                    mine = jnp.where(chan == c, pre[c * own : (c + 1) * own, :n_cols], mine)
                s = 0.5 + 0.5 * jnp.tanh(0.5 * mine)
                there = slice((h - 1) * n_cols, h * n_cols)
                grad = (back_ref[:, there] * s * (1.0 + mine * (1.0 - s))).astype(BF16)
                for a in range(3):
                    put = (h - 1 + a) * width
                    pre_left_ref[a * own : (a + 1) * own, put : put + n_cols] = grad
            half = 0.5 * pre
            hidden = jnp.where(keep, half + half * jnp.tanh(half), 0.0)
            hidden_ref[h] = hidden.astype(BF16)
            wide_ref[0:n_hidden, at] = pltpu.roll(hidden, 1, 1)[:, :n_cols].astype(BF16)
            wide_ref[n_hidden : 2 * n_hidden, at] = hidden[:, :n_cols].astype(BF16)
            wide_ref[2 * n_hidden :, at] = pltpu.roll(hidden, width - 1, 1)[:, :n_cols].astype(BF16)

    three = 3 * own
    lanes = 3 * n_hidden
    half_rows = taps_rows // 2
    acc_ref[0:three, :] = dot_nt(out_left_ref[...], wide_ref[...])
    one = dot_nt(taps_ref[:, width : (n_rows + 3) * width], pre_left_ref[...])
    acc_ref[three:, :] = jnp.zeros((acc_ref.shape[0] - three, lanes), F32)
    acc_ref[three : three + half_rows, 0:three] = one[0:half_rows]
    acc_ref[three : three + half_rows, lanes // 2 : lanes // 2 + three] = one[half_rows:taps_rows]
    gains = one[taps_rows : taps_rows + 1] + one[taps_rows + 1 : taps_rows + 2] + one[taps_rows + 2 : taps_rows + 3]
    acc_ref[three + half_rows : three + half_rows + 1, 0:three] = gains
    if split:
        half = acc_ref.shape[0] // 2
        keep_out[...] = acc_ref[pl.ds(pl.multiple_of(sub * half, half), half), :]
        give_out[...] = acc_ref[pl.ds(pl.multiple_of((1 - sub) * half, half), half), :].astype(BF16)
    else:
        all_out[...] = acc_ref[...]


def grads(split, index, kernel, gain, own, edge, peer, peer_edge, side, cot, back_out):
    n_rows, n_own, n_cols = cot.shape
    n_hidden = kernel.shape[1]
    chans = kernel.shape[2] // 3
    width = n_cols + LANES
    lanes = 3 * n_hidden
    acc_rows = 3 * n_own + 3 * chans // 2 + 32
    body = functools.partial(grads_kernel, split, chans)
    ins = [own, edge, peer, peer_edge, side, cot, back_out]
    if peer is None:
        ins = [own, edge, side, cot, back_out]
        body = lambda i, k, g, o, e, *rest: grads_kernel(split, chans, i, k, g, o, e, None, None, *rest)
    outs = [jax.ShapeDtypeStruct((n_rows + 2, n_hidden, width), BF16)]
    if split:
        outs.append(jax.ShapeDtypeStruct((acc_rows // 2, lanes), F32))
        outs.append(jax.ShapeDtypeStruct((acc_rows // 2, lanes), BF16))
    else:
        outs.append(jax.ShapeDtypeStruct((acc_rows, lanes), F32))
    return call(
        body,
        outs,
        [smem_spec()] + [vmem_spec()] * (2 + len(ins)),
        [
            pltpu.VMEM((3 * chans + 16, (n_rows + 4) * width), BF16),
            pltpu.VMEM((n_rows + 4, 1, width), F32),
            pltpu.VMEM((3 * n_hidden, (n_rows + 2) * n_cols), BF16),
            pltpu.VMEM((3 * n_own, (n_rows + 2) * n_cols), BF16),
            pltpu.VMEM((3 * n_own, (n_rows + 2) * width), BF16),
            pltpu.VMEM((acc_rows, lanes), F32),
        ],
        2 * (n_rows + 2) * 9 * n_cols * n_hidden * (n_own + chans),
        (n_rows + 2) * 3 * n_hidden * n_cols * 2,
        "grads",
    )(index, kernel, gain, *ins)


def encode_kernel(kernel_ref, hidden_ref, out_ref, wide_ref):
    n_ext, n_hidden, width = hidden_ref.shape
    n_rows = n_ext - 2
    n_cols = width - LANES
    for h in range(n_ext):
        hidden = hidden_ref[h].astype(F32)
        at = slice(h * n_cols, (h + 1) * n_cols)
        wide_ref[0:n_hidden, at] = pltpu.roll(hidden, 1, 1)[:, :n_cols].astype(BF16)
        wide_ref[n_hidden : 2 * n_hidden, at] = hidden_ref[h, :, 0:n_cols]
        wide_ref[2 * n_hidden :, at] = pltpu.roll(hidden, width - 1, 1)[:, :n_cols].astype(BF16)
    total = None
    for a in range(3):
        part = dot_nn(kernel_ref[a], wide_ref[:, a * n_cols : (a + n_rows) * n_cols])
        total = part if total is None else total + part
    for r in range(n_rows):
        out_ref[r] = total[:, r * n_cols : (r + 1) * n_cols].astype(BF16)


def encode(kernel, hidden):
    n_ext, n_hidden, width = hidden.shape
    own = kernel.shape[1]
    n_cols = width - LANES
    return call(
        encode_kernel,
        jax.ShapeDtypeStruct((n_ext - 2, own, n_cols), BF16),
        [vmem_spec()] * 2,
        [pltpu.VMEM((3 * n_hidden, n_ext * n_cols), BF16)],
        2 * n_ext * 9 * own * n_hidden * n_cols,
        hidden.size * 2,
        "encode",
    )(kernel, hidden)


def quarters_kernel(index_ref, keep_ref, got_ref, *outs):
    n = len(outs)
    rows = keep_ref.shape[0] // n
    for k in range(n):
        other = jnp.bitwise_xor(index_ref[0], k)
        at = pl.ds(pl.multiple_of(other * rows, rows), rows)
        outs[k][...] = (keep_ref[at, :] + got_ref[at, :].astype(F32)).astype(outs[k].dtype)


def quarters(index, keep, got, n):
    rows, lanes = keep.shape
    return call(
        quarters_kernel,
        [jax.ShapeDtypeStruct((rows // n, lanes), F32 if k == 0 else BF16) for k in range(n)],
        [smem_spec(), vmem_spec(), vmem_spec()],
        [],
        rows * lanes,
        rows * lanes * 8,
        "quarters",
    )(index, keep, got)


def finish_kernel(scale, own, chans, index_ref, mine_ref, other_ref, two_ref, one_ref, gain_ref, all_ref):
    n, rows, lanes = mine_ref.shape
    n_hidden = lanes // 3
    tile, sub = index_ref[0], index_ref[2]
    for k in range(n):
        at = jnp.bitwise_xor(tile, k) * rows
        here = pl.multiple_of(sub * (n * rows) + at, rows)
        there = pl.multiple_of((1 - sub) * (n * rows) + at, rows)
        all_ref[pl.ds(here, rows), :] = mine_ref[k].astype(F32) * scale
        all_ref[pl.ds(there, rows), :] = other_ref[k].astype(F32) * scale
    half_rows = 3 * chans // 2
    for a in range(3):
        for b in range(3):
            two_ref[a, b] = all_ref[a * own : (a + 1) * own, b * n_hidden : (b + 1) * n_hidden]
        lines = jnp.concatenate(
            [
                all_ref[3 * own : 3 * own + half_rows, s + a * own : s + (a + 1) * own]
                for s in (0, lanes // 2)
            ],
            axis=0,
        )
        for b in range(3):
            one_ref[a, b] = lines[b * chans : (b + 1) * chans]
    gain_ref[...] = all_ref[3 * own + half_rows : 3 * own + half_rows + 1, own : 2 * own]


def finish(index, mine, other, scale, own, chans):
    n, rows, lanes = mine.shape
    n_hidden = lanes // 3
    return call(
        functools.partial(finish_kernel, scale, own, chans),
        [
            jax.ShapeDtypeStruct((3, 3, own, n_hidden), F32),
            jax.ShapeDtypeStruct((3, 3, chans, own), F32),
            jax.ShapeDtypeStruct((1, own), F32),
        ],
        [smem_spec(), vmem_spec(), vmem_spec()],
        [pltpu.VMEM((2 * n * rows, lanes), F32)],
        n * rows * lanes,
        n * rows * lanes * 12,
        "finish",
    )(index, mine, other)


def offer_kernel(index_ref, two_ref, one_ref, gain_ref, out_ref):
    own = two_ref.shape[2]
    chans = one_ref.shape[2]
    at = pl.ds(pl.multiple_of((1 - index_ref[1]) * own, own), own)
    gain = gain_ref[...]
    high = gain.astype(BF16).astype(F32)
    middle = (gain - high).astype(BF16).astype(F32)
    line = iota((8, own), 0)
    terms = jnp.where(
        line == 0, high, jnp.where(line == 1, middle, jnp.where(line == 2, gain - high - middle, 0.0))
    ).astype(BF16)
    for a in range(3):
        for b in range(3):
            out_ref[a, b, 0:own] = two_ref[a, b, :, at]
            out_ref[a, b, own : own + chans] = one_ref[a, b]
            out_ref[a, b, own + chans :] = terms


def offer(index, two, one, gain):
    own, chans = two.shape[2], one.shape[2]
    return call(
        offer_kernel,
        jax.ShapeDtypeStruct((3, 3, own + chans + 8, own), BF16),
        [smem_spec()] + [vmem_spec()] * 3,
        [],
        9 * own * (own + chans),
        9 * own * (own + chans) * 4,
        "offer",
    )(index, two, one, gain[None])


def arrange_kernel(index_ref, two_ref, one_ref, gain_ref, theirs_ref, back_ref, code_ref, first_ref, column_ref):
    own = two_ref.shape[2]
    chans = one_ref.shape[2]
    chan = index_ref[1]
    mine = pl.ds(pl.multiple_of(chan * own, own), own)
    peer = pl.ds(pl.multiple_of((1 - chan) * own, own), own)

    def turned(block):
        return block.astype(F32).T.astype(BF16)

    for a in range(3):
        for b in range(3):
            left = b * 2 * own
            back_ref[a, :, left : left + own] = turned(two_ref[a, b, :, mine])
            back_ref[a, :, left + own : left + 2 * own] = turned(theirs_ref[a, b, 0:own])
            code_ref[a, :, left : left + 2 * own] = two_ref[a, b]
        first_ref[a, mine, :] = turned(jnp.concatenate([one_ref[a, b] for b in range(3)], axis=0))
        first_ref[a, peer, :] = turned(
            jnp.concatenate([theirs_ref[a, b, own : own + chans] for b in range(3)], axis=0)
        )
    terms = theirs_ref[0, 0, own + chans :].astype(F32)
    other = terms[0:1] + terms[1:2] + terms[2:3]
    column_ref[mine, :] = jnp.broadcast_to(gain_ref[...], (own, own)).T
    column_ref[peer, :] = jnp.broadcast_to(other, (own, own)).T


def arrange(index, two, one, gain, theirs):
    own, chans = two.shape[2], one.shape[2]
    return call(
        arrange_kernel,
        [
            jax.ShapeDtypeStruct((3, own, 6 * own), BF16),
            jax.ShapeDtypeStruct((3, own, 6 * own), BF16),
            jax.ShapeDtypeStruct((3, 2 * own, 3 * chans), BF16),
            jax.ShapeDtypeStruct((2 * own, LANES), F32),
        ],
        [smem_spec()] + [vmem_spec()] * 4,
        [],
        9 * own * (4 * own + 2 * chans),
        9 * own * (4 * own + 2 * chans) * 4,
        "arrange",
    )(index, two, one, gain[None], theirs)


def step_perm(count, by):
    return [(i, i + by) for i in range(count) if 0 <= i + by < count]


def swap_sub(x):
    return lax.ppermute(x, "sub", [(0, 1), (1, 0)])


def swap_chan(x):
    return lax.ppermute(x, "chan", [(0, 1), (1, 0)])


def swap_tile(x, n_tile, k):
    return lax.ppermute(x, "tile", [(i, i ^ k) for i in range(n_tile)])


def near(block, sub):
    n_cols = block.shape[-1]
    return jnp.where(sub == 0, block[..., n_cols - LANES :], block[..., :LANES])


def side_rows(parts, sub):
    columns = [
        jnp.concatenate([near(edge[: edge.shape[0] // 2], sub), near(mid, sub), near(edge[edge.shape[0] // 2 :], sub)], axis=0)
        for mid, edge in parts
    ]
    both = columns[0] if len(columns) == 1 else jnp.concatenate(columns, axis=1)
    return swap_sub(both)


def body(obs_values, obs_weight, obs_tile, obs_cell, conv_one, conv_two, density_gain, cotangent):
    own, n_rows, n_cols = cotangent.shape
    n_tile = lax.axis_size("tile")
    n_sub = lax.axis_size("sub")
    n_chan = lax.axis_size("chan")
    pair = n_chan == 2 and own == LANES
    n_tiles = n_tile * n_sub
    chans = obs_values.shape[1]
    n_hidden = own * n_chan
    cap = 2 * obs_values.shape[0] // n_tiles
    tile, chan, sub = lax.axis_index("tile"), lax.axis_index("chan"), lax.axis_index("sub")
    index = jnp.stack([tile, chan, sub, jnp.int32(n_tile), tile * n_sub + sub]).astype(jnp.int32)

    bottom, top = cotangent[:, -1], cotangent[:, 0]
    one_own = conv_one.transpose(0, 1, 3, 2)
    if pair:
        offered = offer(index, conv_two, one_own, density_gain)
        obs_tile, bottom, top, offered = lax.optimization_barrier((obs_tile, bottom, top, offered))
        theirs = swap_chan(offered)
    low = lax.ppermute(bottom, "tile", step_perm(n_tile, 1))
    high = lax.ppermute(top, "tile", step_perm(n_tile, -1))

    few = n_tiles == 8
    sent = route(index, obs_values, obs_weight, obs_tile, obs_cell, n_tiles, cap, few)
    if pair:
        sent, low, high, theirs = lax.optimization_barrier((sent, low, high, theirs))
    if few:
        far = [swap_tile(sent[k + 1], n_tile, k) for k in (1, 2, 3)]
        beside = swap_sub(sent[1])
        steps = [
            [(sent[0], (0,)), (beside, (0,))],
            [(far[0], (0,)), (swap_sub(far[0][1:]), (0,)), (far[1], (0,)), (far[2], (0,))],
            [(swap_sub(far[1][1:]), (0,)), (swap_sub(far[2][1:]), (0,))],
        ]
    else:
        got = lax.all_to_all(sent[0], ("tile", "sub"), split_axis=0, concat_axis=0, tiled=True)
        steps = [[(got, tuple(range(n_tiles)))]]

    if pair:
        cotangent, _ = lax.optimization_barrier((cotangent, sent[0]))
        cot = cotangent.transpose(1, 0, 2)
        cot_edge = jnp.stack([low, high])
        cot_peer = swap_chan(cotangent)
        pieces = [(cot, cot_edge), (cot_peer.transpose(1, 0, 2), swap_chan(cot_edge))]
    else:
        cot = cotangent.transpose(1, 0, 2)
        pieces = [
            (
                lax.all_gather(cot, "chan", axis=1, tiled=True),
                lax.all_gather(jnp.stack([low, high]), "chan", axis=1, tiled=True),
            )
        ]
    cot_side = side_rows(pieces, sub)

    if pair:
        back_weights, code_weights, one_weights, gain = arrange(
            index, conv_two, one_own, density_gain, theirs
        )
    else:
        columns = lax.all_to_all(conv_two, "chan", split_axis=3, concat_axis=2, tiled=True)
        one_full = lax.all_gather(one_own, "chan", axis=3, tiled=True)
        gain = lax.all_gather(density_gain, "chan", axis=0, tiled=True)
        gain = jnp.broadcast_to(gain[:, None], (n_hidden, LANES))
        code_weights = conv_two.transpose(0, 2, 1, 3).reshape(3, own, 3 * n_hidden)
        back_weights = columns.transpose(0, 3, 1, 2).reshape(3, own, 3 * n_hidden)
        one_weights = one_full.transpose(0, 3, 1, 2).reshape(3, n_hidden, 3 * chans)

    part = None
    for step in steps[:-1]:
        part = grid(step, part, False, n_rows, n_cols)[0]
    if few:
        part, back_weights, one_weights, code_weights, gain = lax.optimization_barrier(
            (part, back_weights, one_weights, code_weights, gain)
        )
    part, message, up, down = grid(steps[-1], part, True, n_rows, n_cols)
    data = n_rows * chans
    if not pair:
        part = lax.psum(part, "chan")
        density = part[data : data + n_rows]
        dense = density.astype(BF16)
        rest = (density - dense.astype(F32)).astype(BF16)
        message = jnp.concatenate([part[:data].astype(BF16), dense, rest], axis=0)
        blank = jnp.zeros((4, n_cols), BF16)
        up, down = [
            jnp.concatenate(
                [message[r * chans : (r + 2) * chans], dense[r : r + 2], rest[r : r + 2], blank], axis=0
            )
            for r in (n_rows - 2, 0)
        ]
    low = lax.ppermute(up, "tile", step_perm(n_tile, 1))
    high = lax.ppermute(down, "tile", step_perm(n_tile, -1))
    edge = jnp.concatenate([low, high], axis=0)
    back_out = back(index, back_weights, pieces, cot_side, n_cols)
    if pair:
        peer, peer_edge = swap_chan(message), swap_chan(edge)
        peer, peer_edge, back_out = lax.optimization_barrier((peer, peer_edge, back_out))
        side = [message, edge, peer, peer_edge]
    else:
        peer, peer_edge = None, None
        side = [message, edge]
    side = swap_sub(jnp.concatenate([near(x, sub) for x in side], axis=0))

    scale = 1.0 / math.sqrt(n_tiles * n_rows * n_cols)
    split = pair and n_tile == 4
    hidden, *partial = grads(
        split, index, one_weights, gain, part, edge, peer, peer_edge, side, cot, back_out
    )
    encoded = encode(code_weights, hidden).transpose(1, 0, 2)

    if split:
        keep, give = partial
        mine, *others = quarters(index, keep, swap_sub(give), n_tile)
        for k, other in enumerate(others, 1):
            mine = mine + swap_tile(other, n_tile, k).astype(F32)
        mine, encoded = lax.optimization_barrier((mine.astype(BF16), encoded))
        mine = jnp.stack([mine] + [swap_tile(mine, n_tile, k) for k in range(1, n_tile)])
        grad_two, grad_one, grad_gain = finish(index, mine, swap_sub(mine), scale, own, chans)
        return encoded, grad_one.transpose(0, 1, 3, 2), grad_two, grad_gain[0]

    total = lax.psum(partial[0], ("tile", "sub")) * scale
    three = 3 * own
    half_rows = 3 * chans // 2
    lanes = 3 * n_hidden
    grad_two = total[:three].reshape(3, own, 3, n_hidden).transpose(0, 2, 1, 3)
    lines = total[three : three + half_rows]
    lines = jnp.concatenate([lines[:, :three], lines[:, lanes // 2 : lanes // 2 + three]], axis=0)
    grad_one = lines.reshape(3, chans, 3, own).transpose(2, 0, 3, 1)
    grad_gain = total[three + half_rows, own : 2 * own]
    return encoded, grad_one, grad_two, grad_gain


def solution(mesh):
    placed = (
        P(("member", "tile", "chan", "sub"), None),
        P(("member", "tile", "chan", "sub")),
        P(("member", "tile", "chan", "sub")),
        P(("member", "tile", "chan", "sub")),
        P(None, None, "chan", None),
        P(None, None, "chan", None),
        P("chan"),
        P(("member", "chan"), "tile", "sub"),
    )
    return jax.shard_map(
        body,
        mesh=mesh,
        in_specs=placed,
        out_specs=(
            P(("member", "chan"), "tile", "sub"),
            P("member", None, "chan", None),
            P("member", None, "chan", None),
            P(("member", "chan")),
        ),
        check_vma=False,
    )
```

```python
import functools
import math

import jax
import jax.numpy as jnp
from jax import lax
from jax.experimental import pallas as pl
from jax.experimental.pallas import tpu as pltpu
from jax.sharding import PartitionSpec as P

BF16 = jnp.bfloat16
F32 = jnp.float32
LANES = 128
BLOCK = 256
META = 8
MIB = 1024 * 1024


def dot_nt(a, b):
    return lax.dot_general(a, b, (((1,), (1,)), ((), ())), preferred_element_type=F32)


def dot_nn(a, b):
    return lax.dot_general(a, b, (((1,), (0,)), ((), ())), preferred_element_type=F32)


def iota(shape, dim, dtype=jnp.int32):
    return lax.broadcasted_iota(jnp.int32, shape, dim).astype(dtype)


def vmem_spec():
    return pl.BlockSpec(memory_space=pltpu.VMEM)


def smem_spec():
    return pl.BlockSpec(memory_space=pltpu.SMEM)


def call(kernel, out_shape, in_specs, scratch, flops, moved, name, vmem=32):
    n_out = len(out_shape) if isinstance(out_shape, (tuple, list)) else None
    out_specs = vmem_spec() if n_out is None else [vmem_spec() for _ in range(n_out)]
    return pl.pallas_call(
        kernel,
        out_shape=out_shape,
        in_specs=in_specs,
        out_specs=out_specs,
        scratch_shapes=scratch,
        compiler_params=pltpu.CompilerParams(vmem_limit_bytes=vmem * MIB),
        cost_estimate=pl.CostEstimate(flops=flops, bytes_accessed=moved, transcendentals=0),
        name=name,
    )


def route_kernel(n_tiles, cap, relative, index_ref, tile_hbm, weight_hbm, cell_hbm, values_hbm, *rest):
    n_outs = 5 if relative else 1
    outs = rest[:n_outs]
    (tile_ref, weight_ref, cell_ref, values_ref, onehot_ref, slot_ref, weight32_ref, all_ref,
     info_ref, info_smem, sems) = rest[n_outs:]
    loads = [
        pltpu.make_async_copy(tile_hbm, tile_ref, sems.at[0]),
        pltpu.make_async_copy(weight_hbm, weight_ref, sems.at[1]),
        pltpu.make_async_copy(cell_hbm, cell_ref, sems.at[2]),
        pltpu.make_async_copy(values_hbm, values_ref, sems.at[3]),
    ]
    for load in loads:
        load.start()
    all_ref[...] = jnp.zeros(all_ref.shape, BF16)
    loads[0].wait()
    n_lines = tile_ref.shape[0]
    n_blocks = n_lines // 2
    n_obs_chans = values_ref.shape[0]
    pairs = n_tiles * n_lines
    tiles = tile_ref[...]
    for t in range(n_tiles):
        onehot_ref[t * n_lines : (t + 1) * n_lines, :] = jnp.where(tiles == t, 1.0, 0.0).astype(BF16)
    onehot = onehot_ref[...]
    upper = jnp.where(
        iota((LANES, LANES), 0) <= iota((LANES, LANES), 1), 1.0, 0.0
    ).astype(BF16)
    here = iota((pairs, pairs), 0)
    there = iota((pairs, pairs), 1)
    earlier = jnp.where(
        (here // n_lines == there // n_lines) & (there < here), 1.0, 0.0
    ).astype(BF16)
    total_row = dot_nt(jnp.ones((8, LANES), BF16), onehot)
    offset_row = dot_nt(total_row.astype(BF16), earlier)
    odd = iota((8, pairs), 1) % 2 == 1
    both = jnp.where(odd, total_row + pltpu.roll(total_row, 1, 1), 0.0)
    spill = jnp.where(jnp.max(both, axis=1, keepdims=True) > LANES, 1.0, 0.0)
    info_ref[...] = jnp.where(
        iota((8, pairs), 0) == 0, offset_row, spill
    ).astype(jnp.int32)
    copy = pltpu.make_async_copy(info_ref, info_smem, sems.at[4])
    copy.start()
    cum = dot_nn(onehot, upper)
    totals = dot_nn(onehot, jnp.ones((LANES, LANES), BF16))
    offset = dot_nn(earlier, totals.astype(BF16))
    place = cum + offset - 1.0
    slots = jnp.zeros(tiles.shape, F32)
    for t in range(n_tiles):
        slots = jnp.where(tiles == t, place[t * n_lines : (t + 1) * n_lines, :], slots)
    slot_ref[...] = slots
    for load in loads[1:]:
        load.wait()
    weight32_ref[...] = weight_ref[...].astype(F32)
    meta_row = iota((16, BLOCK), 0)
    window = iota((LANES, BLOCK), 0, F32)
    blank = jnp.zeros((n_obs_chans + 16, LANES), F32)
    copy.wait()

    def line(ref, b):
        return jnp.concatenate([ref[pl.ds(2 * b, 1), :], ref[pl.ds(2 * b + 1, 1), :]], axis=1)

    def columns(b):
        values = values_ref[:, pl.ds(pl.multiple_of(b * BLOCK, BLOCK), BLOCK)]
        cell = line(cell_ref, b)
        weight = line(weight32_ref, b)
        high = (cell // LANES).astype(F32)
        low = (cell % LANES).astype(F32)
        meta = jnp.where(
            meta_row == 0,
            weight,
            jnp.where(meta_row == 1, high, jnp.where(meta_row == 2, low, 0.0)),
        ).astype(BF16)
        return jnp.concatenate([values, meta], axis=0)

    def add(t, wide, tile, slot, start):
        key = jnp.where(tile == t, slot - start.astype(F32), -1.0)
        chosen = jnp.where(window == key, 1.0, 0.0).astype(BF16)
        part = jnp.concatenate([dot_nt(wide, chosen), blank], axis=1)
        base = jnp.minimum(start // LANES * LANES, cap - BLOCK)
        turn = jnp.bitwise_and(start - base, BLOCK - 1)
        part = pltpu.roll(part, turn, 1)[: n_obs_chans + META].astype(BF16)
        where = pl.ds(pl.multiple_of(base, LANES), BLOCK)
        all_ref[t, :, where] = all_ref[t, :, where] + part

    def place_block(b, skip):
        wide = columns(b)
        tile = line(tile_ref, b)
        slot = line(slot_ref, b)
        for t in range(n_tiles):
            add(t, wide, tile, slot, info_smem[0, t * n_lines + 2 * b] + skip)

    def first_some(i, carry):
        for j in range(8):
            place_block(8 * i + j, 0)
        return carry

    lax.fori_loop(0, n_blocks // 8, first_some, 0)

    @pl.when(info_smem[1, 0] > 0)
    def _():
        def rest_of(b, carry):
            place_block(b, LANES)
            return carry

        lax.fori_loop(0, n_blocks, rest_of, 0)

    if relative:
        me = index_ref[4]
        outs[0][0] = all_ref[me]
        outs[1][0] = all_ref[jnp.bitwise_xor(me, 1)]
        for k in range(1, 4):
            for s in range(2):
                outs[k + 1][s] = all_ref[jnp.bitwise_xor(me, 2 * k + s)]
    else:
        outs[0][...] = all_ref[...]


def route(index, obs_values, obs_weight, obs_tile, obs_cell, n_tiles, cap, relative):
    n_obs, chans = obs_values.shape
    n_lines = n_obs // LANES
    rows = chans + META
    outs = [(n, rows, cap) for n in ((1, 1, 2, 2, 2) if relative else (n_tiles,))]
    hbm_spec = pl.BlockSpec(memory_space=pltpu.HBM)
    return call(
        functools.partial(route_kernel, n_tiles, cap, relative),
        [jax.ShapeDtypeStruct(shape, BF16) for shape in outs],
        [smem_spec()] + [hbm_spec] * 4,
        [
            pltpu.VMEM((n_lines, LANES), jnp.int32),
            pltpu.VMEM((n_lines, LANES), BF16),
            pltpu.VMEM((n_lines, LANES), jnp.int32),
            pltpu.VMEM((chans, n_obs), BF16),
            pltpu.VMEM((n_tiles * n_lines, LANES), BF16),
            pltpu.VMEM((n_lines, LANES), F32),
            pltpu.VMEM((n_lines, LANES), F32),
            pltpu.VMEM((n_tiles, rows, cap), BF16),
            pltpu.VMEM((8, n_tiles * n_lines), jnp.int32),
            pltpu.SMEM((8, n_tiles * n_lines), jnp.int32),
            pltpu.SemaphoreType.DMA((5,)),
        ],
        2 * n_obs * n_tiles * BLOCK * 80,
        n_tiles * rows * cap * 2,
        "route",
    )(
        index,
        obs_tile.reshape(n_lines, LANES),
        obs_weight.reshape(n_lines, LANES),
        obs_cell.reshape(n_lines, LANES),
        obs_values.T,
    )


def grid_kernel(n_rows, n_cols, group, takes, first, last, *rest):
    rest = list(rest)
    got_refs = [rest.pop(0) for _ in takes]
    senders = [ref.at[i] for ref, picked in zip(got_refs, takes) for i in picked]
    before_ref = None if first else rest.pop(0)
    own_ref = rest.pop(0)
    send_refs = [rest.pop(0) for _ in range(3)] if last else None
    left_ref, right_ref = rest
    n_send = len(senders)
    rows, cap = senders[0].shape
    chans = rows - META
    data = n_rows * chans
    per_row = n_cols // LANES
    columns = iota((n_cols, cap), 0, F32)
    row_ids = iota((2 * n_rows, cap), 0, F32)
    total = None
    for g in range(n_send // group):
        slot = g % 2
        for i in range(group):
            sender = senders[g * group + i]
            at = slice(i * cap, (i + 1) * cap)
            values = sender[0:chans, :]
            meta = sender[chans:rows, :].astype(F32)
            weight = meta[0:1]
            high = meta[1:2]
            row = jnp.floor((high + 0.5) * (1.0 / per_row))
            column = (high - row * per_row) * LANES + meta[2:3]
            right_ref[slot, :, at] = jnp.where(columns == column, weight, 0.0).astype(BF16)
            in_row = jnp.where(row_ids == row, 1.0, 0.0)
            for r in range(n_rows):
                left_ref[slot, r * chans : (r + 1) * chans, at] = values * in_row[r : r + 1].astype(BF16)
            left_ref[slot, data:, at] = in_row.astype(BF16)
        part = dot_nt(left_ref[slot], right_ref[slot])
        total = part if total is None else total + part
    if before_ref is not None:
        total = total + before_ref[...]
    own_ref[...] = total
    if last:
        send_ref, low_ref, high_ref = send_refs
        density = own_ref[data : data + n_rows, :]
        high = density.astype(BF16).astype(F32)
        low = density - high
        send_ref[0:data, :] = own_ref[0:data, :].astype(BF16)
        send_ref[data:, :] = jnp.concatenate([high, low], axis=0).astype(BF16)
        for ref, at in ((high_ref, 0), (low_ref, n_rows - 2)):
            ref[0 : 2 * chans, :] = own_ref[at * chans : (at + 2) * chans, :].astype(BF16)
            ref[2 * chans :, :] = jnp.concatenate(
                [high[at : at + 2], low[at : at + 2], jnp.zeros((4, n_cols), F32)], axis=0
            ).astype(BF16)


def grid(got, before, last, n_rows, n_cols):
    takes = [picked for _, picked in got]
    got = [x for x, _ in got]
    n_send = sum(len(picked) for picked in takes)
    rows, cap = got[0].shape[1:]
    group = max(1, min(2048 // cap, n_send))
    chans = rows - META
    total = n_rows * chans + 2 * n_rows
    outs = [jax.ShapeDtypeStruct((total, n_cols), F32)]
    if last:
        outs.append(jax.ShapeDtypeStruct((total, n_cols), BF16))
        outs += [jax.ShapeDtypeStruct((2 * chans + 8, n_cols), BF16)] * 2
    ins = list(got) if before is None else list(got) + [before]
    return call(
        functools.partial(grid_kernel, n_rows, n_cols, group, takes, before is None, last),
        outs,
        [vmem_spec()] * len(ins),
        [
            pltpu.VMEM((2, total, group * cap), BF16),
            pltpu.VMEM((2, n_cols, group * cap), BF16),
        ],
        2 * n_send * cap * total * n_cols,
        n_send * rows * cap * 2,
        "grid_last" if last else "grid_part",
    )(*ins)


def lane_mask(shape, n_cols, sub, depth):
    lane = iota(shape, 1)
    width = n_cols + LANES
    keep_right = (lane >= n_cols) & (lane < n_cols + depth) & (sub == 0)
    keep_left = (lane >= width - depth) & (sub == 1)
    return (lane < n_cols) | keep_right | keep_left


def back_kernel(n_cols, n_pieces, index_ref, kernel_ref, *rest):
    pieces = [(rest[2 * i], rest[2 * i + 1]) for i in range(n_pieces)]
    side_ref, out_ref, wide_ref = rest[2 * n_pieces :]
    n_ext, all_chans = side_ref.shape[0], side_ref.shape[1]
    n_rows = n_ext - 2
    width = n_cols + LANES
    keep = lane_mask((1, width), n_cols, index_ref[2], 1)
    for h in range(n_ext):
        if h == 0 or h == n_ext - 1:
            mids = [edge[min(h, 1)] for _, edge in pieces]
        else:
            mids = [middle[h - 1] for middle, _ in pieces]
        mid = mids[0] if n_pieces == 1 else jnp.concatenate(mids, axis=0)
        ext = jnp.concatenate([mid, side_ref[h]], axis=1).astype(F32)
        ext = jnp.where(keep, ext, 0.0)
        at = slice(h * n_cols, (h + 1) * n_cols)
        wide_ref[0:all_chans, at] = pltpu.roll(ext, width - 1, 1)[:, :n_cols].astype(BF16)
        wide_ref[all_chans : 2 * all_chans, at] = mid
        wide_ref[2 * all_chans :, at] = pltpu.roll(ext, 1, 1)[:, :n_cols].astype(BF16)
    total = None
    for a in range(3):
        at = slice((2 - a) * n_cols, (2 - a + n_rows) * n_cols)
        part = dot_nn(kernel_ref[a], wide_ref[:, at])
        total = part if total is None else total + part
    out_ref[...] = total


def back(index, kernel, pieces, side, n_cols):
    n_ext, all_chans = side.shape[0], side.shape[1]
    n_out = kernel.shape[1]
    return call(
        functools.partial(back_kernel, n_cols, len(pieces)),
        jax.ShapeDtypeStruct((n_out, (n_ext - 2) * n_cols), F32),
        [smem_spec()] + [vmem_spec()] * (2 + 2 * len(pieces)),
        [pltpu.VMEM((3 * all_chans, n_ext * n_cols), BF16)],
        2 * n_ext * 9 * all_chans * n_out * n_cols,
        n_ext * all_chans * n_cols * 2,
        "back",
    )(index, kernel, *[x for piece in pieces for x in piece], side)


def grads_kernel(
    split, chans, index_ref, kernel_ref, gain_ref, own_ref, edge_ref, peer_ref, peer_edge_ref,
    side_ref, cot_ref, back_ref, hidden_ref, *rest,
):
    rest = list(rest)
    if split:
        keep_out, give_out = rest.pop(0), rest.pop(0)
    else:
        all_out = rest.pop(0)
    taps_ref, logs_ref, wide_ref, out_left_ref, pre_left_ref, acc_ref = rest
    n_rows, own, n_cols = cot_ref.shape
    n_hidden = kernel_ref.shape[1]
    taps_rows = 3 * chans
    width = n_cols + LANES
    tile, chan, sub, n_tile = index_ref[0], index_ref[1], index_ref[2], index_ref[3]
    keep_two = lane_mask((1, width), n_cols, sub, 2)

    log_line = iota((16, width), 0)
    data = n_rows * chans
    middle_rows = data + 2 * n_rows
    edge_rows = 2 * chans + 8
    side_half = middle_rows + 2 * edge_rows
    lefts = [(own_ref, edge_ref)] + ([] if peer_ref is None else [(peer_ref, peer_edge_ref)])
    sources = []
    for i in range(n_rows + 4):
        found = []
        for p, (middle_ref, ends_ref) in enumerate(lefts):
            if 2 <= i < n_rows + 2:
                r = i - 2
                base, lines = r * chans, (data + r, data + n_rows + r)
                found.append((middle_ref, base, lines, p * side_half))
            else:
                e = i if i < 2 else i - n_rows
                start = e // 2 * edge_rows
                base = start + e % 2 * chans
                lines = (start + 2 * chans + e % 2, start + 2 * chans + 2 + e % 2)
                found.append((ends_ref, base, lines, p * side_half + middle_rows))
        sources.append(found)

    def gather(found, wanted):
        total = None
        for ref, base, lines, at in found:
            for line in [base] if wanted == chans else lines:
                ext = jnp.concatenate(
                    [
                        ref[line : line + wanted, :].astype(F32),
                        side_ref[at + line : at + line + wanted, :].astype(F32),
                    ],
                    axis=1,
                )
                total = ext if total is None else total + ext
        return total

    for i in range(n_rows + 4):
        ext = gather(sources[i], chans)
        density = gather(sources[i], 1)
        logs = jnp.log(1.0 + density)
        logs_ref[i] = logs
        shrink = jnp.where(keep_two, 1.0 / (1.0 + density), 0.0)
        feats = ext * shrink
        at = slice(i * width, (i + 1) * width)
        taps_ref[0:chans, at] = pltpu.roll(feats, 1, 1).astype(BF16)
        taps_ref[chans : 2 * chans, at] = feats.astype(BF16)
        taps_ref[2 * chans : taps_rows, at] = pltpu.roll(feats, width - 1, 1).astype(BF16)
        high = logs.astype(BF16).astype(F32)
        middle = (logs - high).astype(BF16).astype(F32)
        taps_ref[taps_rows:, at] = jnp.where(
            log_line == 0,
            high,
            jnp.where(log_line == 1, middle, jnp.where(log_line == 2, logs - high - middle, 0.0)),
        ).astype(BF16)

    nothing = jnp.zeros((own, n_cols), BF16)
    for h in range(n_rows + 2):
        for a in range(3):
            inside = 0 <= h - a < n_rows
            put = slice(a * own, (a + 1) * own)
            out_left_ref[put, h * n_cols : (h + 1) * n_cols] = cot_ref[h - a] if inside else nothing
            if not inside:
                pre_left_ref[put, h * width : h * width + n_cols] = nothing
        pre_left_ref[:, h * width + n_cols : (h + 1) * width] = jnp.zeros((3 * own, LANES), BF16)

    gain = gain_ref[:, 0:1]
    keep_one = lane_mask((1, width), n_cols, sub, 1)
    group = 1
    for first in range(0, n_rows + 2, group):
        pre_all = None
        for a in range(3):
            at = slice((first + a) * width, (first + a + group) * width)
            part = dot_nn(kernel_ref[a], taps_ref[0:taps_rows, at])
            pre_all = part if pre_all is None else pre_all + part
        for k in range(group):
            h = first + k
            pre = pre_all[:, k * width : (k + 1) * width] + gain * logs_ref[h + 1]
            at = slice(h * n_cols, (h + 1) * n_cols)
            keep = keep_one
            if h == 0:
                keep = keep & (tile > 0)
            elif h == n_rows + 1:
                keep = keep & (tile < n_tile - 1)
            else:
                mine = pre[0:own, :n_cols]
                for c in range(1, n_hidden // own):
                    mine = jnp.where(chan == c, pre[c * own : (c + 1) * own, :n_cols], mine)
                s = 0.5 + 0.5 * jnp.tanh(0.5 * mine)
                there = slice((h - 1) * n_cols, h * n_cols)
                grad = (back_ref[:, there] * s * (1.0 + mine * (1.0 - s))).astype(BF16)
                for a in range(3):
                    put = (h - 1 + a) * width
                    pre_left_ref[a * own : (a + 1) * own, put : put + n_cols] = grad
            half = 0.5 * pre
            hidden = jnp.where(keep, half + half * jnp.tanh(half), 0.0)
            hidden_ref[h] = hidden.astype(BF16)
            wide_ref[0:n_hidden, at] = pltpu.roll(hidden, 1, 1)[:, :n_cols].astype(BF16)
            wide_ref[n_hidden : 2 * n_hidden, at] = hidden[:, :n_cols].astype(BF16)
            wide_ref[2 * n_hidden :, at] = pltpu.roll(hidden, width - 1, 1)[:, :n_cols].astype(BF16)

    three = 3 * own
    lanes = 3 * n_hidden
    half_rows = taps_rows // 2
    acc_ref[0:three, :] = dot_nt(out_left_ref[...], wide_ref[...])
    one = dot_nt(taps_ref[:, width : (n_rows + 3) * width], pre_left_ref[...])
    acc_ref[three:, :] = jnp.zeros((acc_ref.shape[0] - three, lanes), F32)
    acc_ref[three : three + half_rows, 0:three] = one[0:half_rows]
    acc_ref[three : three + half_rows, lanes // 2 : lanes // 2 + three] = one[half_rows:taps_rows]
    gains = one[taps_rows : taps_rows + 1] + one[taps_rows + 1 : taps_rows + 2] + one[taps_rows + 2 : taps_rows + 3]
    acc_ref[three + half_rows : three + half_rows + 1, 0:three] = gains
    if split:
        half = acc_ref.shape[0] // 2
        keep_out[...] = acc_ref[pl.ds(pl.multiple_of(sub * half, half), half), :]
        give_out[...] = acc_ref[pl.ds(pl.multiple_of((1 - sub) * half, half), half), :].astype(BF16)
    else:
        all_out[...] = acc_ref[...]


def grads(split, index, kernel, gain, own, edge, peer, peer_edge, side, cot, back_out):
    n_rows, n_own, n_cols = cot.shape
    n_hidden = kernel.shape[1]
    chans = kernel.shape[2] // 3
    width = n_cols + LANES
    lanes = 3 * n_hidden
    acc_rows = 3 * n_own + 3 * chans // 2 + 32
    body = functools.partial(grads_kernel, split, chans)
    ins = [own, edge, peer, peer_edge, side, cot, back_out]
    if peer is None:
        ins = [own, edge, side, cot, back_out]
        body = lambda i, k, g, o, e, *rest: grads_kernel(split, chans, i, k, g, o, e, None, None, *rest)
    outs = [jax.ShapeDtypeStruct((n_rows + 2, n_hidden, width), BF16)]
    if split:
        outs.append(jax.ShapeDtypeStruct((acc_rows // 2, lanes), F32))
        outs.append(jax.ShapeDtypeStruct((acc_rows // 2, lanes), BF16))
    else:
        outs.append(jax.ShapeDtypeStruct((acc_rows, lanes), F32))
    return call(
        body,
        outs,
        [smem_spec()] + [vmem_spec()] * (2 + len(ins)),
        [
            pltpu.VMEM((3 * chans + 16, (n_rows + 4) * width), BF16),
            pltpu.VMEM((n_rows + 4, 1, width), F32),
            pltpu.VMEM((3 * n_hidden, (n_rows + 2) * n_cols), BF16),
            pltpu.VMEM((3 * n_own, (n_rows + 2) * n_cols), BF16),
            pltpu.VMEM((3 * n_own, (n_rows + 2) * width), BF16),
            pltpu.VMEM((acc_rows, lanes), F32),
        ],
        2 * (n_rows + 2) * 9 * n_cols * n_hidden * (n_own + chans),
        (n_rows + 2) * 3 * n_hidden * n_cols * 2,
        "grads",
    )(index, kernel, gain, *ins)


def encode_kernel(kernel_ref, hidden_ref, out_ref, wide_ref):
    n_ext, n_hidden, width = hidden_ref.shape
    n_rows = n_ext - 2
    n_cols = width - LANES
    for h in range(n_ext):
        hidden = hidden_ref[h].astype(F32)
        at = slice(h * n_cols, (h + 1) * n_cols)
        wide_ref[0:n_hidden, at] = pltpu.roll(hidden, 1, 1)[:, :n_cols].astype(BF16)
        wide_ref[n_hidden : 2 * n_hidden, at] = hidden_ref[h, :, 0:n_cols]
        wide_ref[2 * n_hidden :, at] = pltpu.roll(hidden, width - 1, 1)[:, :n_cols].astype(BF16)
    total = None
    for a in range(3):
        part = dot_nn(kernel_ref[a], wide_ref[:, a * n_cols : (a + n_rows) * n_cols])
        total = part if total is None else total + part
    for r in range(n_rows):
        out_ref[r] = total[:, r * n_cols : (r + 1) * n_cols].astype(BF16)


def encode(kernel, hidden):
    n_ext, n_hidden, width = hidden.shape
    own = kernel.shape[1]
    n_cols = width - LANES
    return call(
        encode_kernel,
        jax.ShapeDtypeStruct((n_ext - 2, own, n_cols), BF16),
        [vmem_spec()] * 2,
        [pltpu.VMEM((3 * n_hidden, n_ext * n_cols), BF16)],
        2 * n_ext * 9 * own * n_hidden * n_cols,
        hidden.size * 2,
        "encode",
    )(kernel, hidden)


def quarters_kernel(index_ref, keep_ref, got_ref, *outs):
    n = len(outs)
    rows = keep_ref.shape[0] // n
    for k in range(n):
        other = jnp.bitwise_xor(index_ref[0], k)
        at = pl.ds(pl.multiple_of(other * rows, rows), rows)
        outs[k][...] = (keep_ref[at, :] + got_ref[at, :].astype(F32)).astype(outs[k].dtype)


def quarters(index, keep, got, n):
    rows, lanes = keep.shape
    return call(
        quarters_kernel,
        [jax.ShapeDtypeStruct((rows // n, lanes), F32 if k == 0 else BF16) for k in range(n)],
        [smem_spec(), vmem_spec(), vmem_spec()],
        [],
        rows * lanes,
        rows * lanes * 8,
        "quarters",
    )(index, keep, got)


def finish_kernel(scale, own, chans, index_ref, mine_ref, other_ref, two_ref, one_ref, gain_ref, all_ref):
    n, rows, lanes = mine_ref.shape
    n_hidden = lanes // 3
    tile, sub = index_ref[0], index_ref[2]
    for k in range(n):
        at = jnp.bitwise_xor(tile, k) * rows
        here = pl.multiple_of(sub * (n * rows) + at, rows)
        there = pl.multiple_of((1 - sub) * (n * rows) + at, rows)
        all_ref[pl.ds(here, rows), :] = mine_ref[k].astype(F32) * scale
        all_ref[pl.ds(there, rows), :] = other_ref[k].astype(F32) * scale
    half_rows = 3 * chans // 2
    for a in range(3):
        for b in range(3):
            two_ref[a, b] = all_ref[a * own : (a + 1) * own, b * n_hidden : (b + 1) * n_hidden]
        lines = jnp.concatenate(
            [
                all_ref[3 * own : 3 * own + half_rows, s + a * own : s + (a + 1) * own]
                for s in (0, lanes // 2)
            ],
            axis=0,
        )
        for b in range(3):
            one_ref[a, b] = lines[b * chans : (b + 1) * chans]
    gain_ref[...] = all_ref[3 * own + half_rows : 3 * own + half_rows + 1, own : 2 * own]


def finish(index, mine, other, scale, own, chans):
    n, rows, lanes = mine.shape
    n_hidden = lanes // 3
    return call(
        functools.partial(finish_kernel, scale, own, chans),
        [
            jax.ShapeDtypeStruct((3, 3, own, n_hidden), F32),
            jax.ShapeDtypeStruct((3, 3, chans, own), F32),
            jax.ShapeDtypeStruct((1, own), F32),
        ],
        [smem_spec(), vmem_spec(), vmem_spec()],
        [pltpu.VMEM((2 * n * rows, lanes), F32)],
        n * rows * lanes,
        n * rows * lanes * 12,
        "finish",
    )(index, mine, other)


def offer_kernel(index_ref, two_ref, one_ref, gain_ref, out_ref):
    own = two_ref.shape[2]
    chans = one_ref.shape[2]
    at = pl.ds(pl.multiple_of((1 - index_ref[1]) * own, own), own)
    gain = gain_ref[...]
    high = gain.astype(BF16).astype(F32)
    middle = (gain - high).astype(BF16).astype(F32)
    line = iota((8, own), 0)
    terms = jnp.where(
        line == 0, high, jnp.where(line == 1, middle, jnp.where(line == 2, gain - high - middle, 0.0))
    ).astype(BF16)
    for a in range(3):
        for b in range(3):
            out_ref[a, b, 0:own] = two_ref[a, b, :, at]
            out_ref[a, b, own : own + chans] = one_ref[a, b]
            out_ref[a, b, own + chans :] = terms


def offer(index, two, one, gain):
    own, chans = two.shape[2], one.shape[2]
    return call(
        offer_kernel,
        jax.ShapeDtypeStruct((3, 3, own + chans + 8, own), BF16),
        [smem_spec()] + [vmem_spec()] * 3,
        [],
        9 * own * (own + chans),
        9 * own * (own + chans) * 4,
        "offer",
    )(index, two, one, gain[None])


def arrange_kernel(index_ref, two_ref, one_ref, gain_ref, theirs_ref, back_ref, code_ref, first_ref, column_ref):
    own = two_ref.shape[2]
    chans = one_ref.shape[2]
    chan = index_ref[1]
    mine = pl.ds(pl.multiple_of(chan * own, own), own)
    peer = pl.ds(pl.multiple_of((1 - chan) * own, own), own)

    def turned(block):
        return block.astype(F32).T.astype(BF16)

    for a in range(3):
        for b in range(3):
            left = b * 2 * own
            back_ref[a, :, left : left + own] = turned(two_ref[a, b, :, mine])
            back_ref[a, :, left + own : left + 2 * own] = turned(theirs_ref[a, b, 0:own])
            code_ref[a, :, left : left + 2 * own] = two_ref[a, b]
        first_ref[a, mine, :] = turned(jnp.concatenate([one_ref[a, b] for b in range(3)], axis=0))
        first_ref[a, peer, :] = turned(
            jnp.concatenate([theirs_ref[a, b, own : own + chans] for b in range(3)], axis=0)
        )
    terms = theirs_ref[0, 0, own + chans :].astype(F32)
    other = terms[0:1] + terms[1:2] + terms[2:3]
    column_ref[mine, :] = jnp.broadcast_to(gain_ref[...], (own, own)).T
    column_ref[peer, :] = jnp.broadcast_to(other, (own, own)).T


def arrange(index, two, one, gain, theirs):
    own, chans = two.shape[2], one.shape[2]
    return call(
        arrange_kernel,
        [
            jax.ShapeDtypeStruct((3, own, 6 * own), BF16),
            jax.ShapeDtypeStruct((3, own, 6 * own), BF16),
            jax.ShapeDtypeStruct((3, 2 * own, 3 * chans), BF16),
            jax.ShapeDtypeStruct((2 * own, LANES), F32),
        ],
        [smem_spec()] + [vmem_spec()] * 4,
        [],
        9 * own * (4 * own + 2 * chans),
        9 * own * (4 * own + 2 * chans) * 4,
        "arrange",
    )(index, two, one, gain[None], theirs)


def step_perm(count, by):
    return [(i, i + by) for i in range(count) if 0 <= i + by < count]


def swap_sub(x):
    return lax.ppermute(x, "sub", [(0, 1), (1, 0)])


def swap_chan(x):
    return lax.ppermute(x, "chan", [(0, 1), (1, 0)])


def swap_tile(x, n_tile, k):
    return lax.ppermute(x, "tile", [(i, i ^ k) for i in range(n_tile)])


def near(block, sub):
    n_cols = block.shape[-1]
    return jnp.where(sub == 0, block[..., n_cols - LANES :], block[..., :LANES])


def side_rows(parts, sub):
    columns = [
        jnp.concatenate([near(edge[: edge.shape[0] // 2], sub), near(mid, sub), near(edge[edge.shape[0] // 2 :], sub)], axis=0)
        for mid, edge in parts
    ]
    both = columns[0] if len(columns) == 1 else jnp.concatenate(columns, axis=1)
    return swap_sub(both)


def body(obs_values, obs_weight, obs_tile, obs_cell, conv_one, conv_two, density_gain, cotangent):
    own, n_rows, n_cols = cotangent.shape
    n_tile = lax.axis_size("tile")
    n_sub = lax.axis_size("sub")
    n_chan = lax.axis_size("chan")
    pair = n_chan == 2 and own == LANES
    n_tiles = n_tile * n_sub
    chans = obs_values.shape[1]
    n_hidden = own * n_chan
    cap = 2 * obs_values.shape[0] // n_tiles
    tile, chan, sub = lax.axis_index("tile"), lax.axis_index("chan"), lax.axis_index("sub")
    index = jnp.stack([tile, chan, sub, jnp.int32(n_tile), tile * n_sub + sub]).astype(jnp.int32)

    bottom, top = cotangent[:, -1], cotangent[:, 0]
    one_own = conv_one.transpose(0, 1, 3, 2)
    if pair:
        offered = offer(index, conv_two, one_own, density_gain)
        obs_tile, bottom, top, offered = lax.optimization_barrier((obs_tile, bottom, top, offered))
        theirs = swap_chan(offered)
    low = lax.ppermute(bottom, "tile", step_perm(n_tile, 1))
    high = lax.ppermute(top, "tile", step_perm(n_tile, -1))

    few = n_tiles == 8
    sent = route(index, obs_values, obs_weight, obs_tile, obs_cell, n_tiles, cap, few)
    if pair:
        sent, low, high, theirs = lax.optimization_barrier((sent, low, high, theirs))
    if few:
        far = [swap_tile(sent[k + 1], n_tile, k) for k in (1, 2, 3)]
        near_side = swap_sub(jnp.concatenate([sent[1], far[0][1:]], axis=0))
        steps = [
            [(sent[0], (0,)), (far[0], (0,)), (near_side, (0, 1))],
            [(far[1], (0,)), (far[2], (0,))],
            [(swap_sub(far[1][1:]), (0,)), (swap_sub(far[2][1:]), (0,))],
        ]
    else:
        got = lax.all_to_all(sent[0], ("tile", "sub"), split_axis=0, concat_axis=0, tiled=True)
        steps = [[(got, tuple(range(n_tiles)))]]

    if pair:
        cotangent, _ = lax.optimization_barrier((cotangent, sent[0]))
        cot = cotangent.transpose(1, 0, 2)
        cot_edge = jnp.stack([low, high])
        cot_peer = swap_chan(cotangent)
        pieces = [(cot, cot_edge), (cot_peer.transpose(1, 0, 2), swap_chan(cot_edge))]
    else:
        cot = cotangent.transpose(1, 0, 2)
        pieces = [
            (
                lax.all_gather(cot, "chan", axis=1, tiled=True),
                lax.all_gather(jnp.stack([low, high]), "chan", axis=1, tiled=True),
            )
        ]
    cot_side = side_rows(pieces, sub)

    if pair:
        back_weights, code_weights, one_weights, gain = arrange(
            index, conv_two, one_own, density_gain, theirs
        )
    else:
        columns = lax.all_to_all(conv_two, "chan", split_axis=3, concat_axis=2, tiled=True)
        one_full = lax.all_gather(one_own, "chan", axis=3, tiled=True)
        gain = lax.all_gather(density_gain, "chan", axis=0, tiled=True)
        gain = jnp.broadcast_to(gain[:, None], (n_hidden, LANES))
        code_weights = conv_two.transpose(0, 2, 1, 3).reshape(3, own, 3 * n_hidden)
        back_weights = columns.transpose(0, 3, 1, 2).reshape(3, own, 3 * n_hidden)
        one_weights = one_full.transpose(0, 3, 1, 2).reshape(3, n_hidden, 3 * chans)

    part = None
    for step in steps[:-1]:
        part = grid(step, part, False, n_rows, n_cols)[0]
    if few:
        part, back_weights, one_weights, code_weights, gain = lax.optimization_barrier(
            (part, back_weights, one_weights, code_weights, gain)
        )
    part, message, up, down = grid(steps[-1], part, True, n_rows, n_cols)
    data = n_rows * chans
    if not pair:
        part = lax.psum(part, "chan")
        density = part[data : data + n_rows]
        dense = density.astype(BF16)
        rest = (density - dense.astype(F32)).astype(BF16)
        message = jnp.concatenate([part[:data].astype(BF16), dense, rest], axis=0)
        blank = jnp.zeros((4, n_cols), BF16)
        up, down = [
            jnp.concatenate(
                [message[r * chans : (r + 2) * chans], dense[r : r + 2], rest[r : r + 2], blank], axis=0
            )
            for r in (n_rows - 2, 0)
        ]
    low = lax.ppermute(up, "tile", step_perm(n_tile, 1))
    high = lax.ppermute(down, "tile", step_perm(n_tile, -1))
    edge = jnp.concatenate([low, high], axis=0)
    back_out = back(index, back_weights, pieces, cot_side, n_cols)
    if pair:
        peer, peer_edge = swap_chan(message), swap_chan(edge)
        peer, peer_edge, back_out = lax.optimization_barrier((peer, peer_edge, back_out))
        side = [message, edge, peer, peer_edge]
    else:
        peer, peer_edge = None, None
        side = [message, edge]
    side = swap_sub(jnp.concatenate([near(x, sub) for x in side], axis=0))

    scale = 1.0 / math.sqrt(n_tiles * n_rows * n_cols)
    split = pair and n_tile == 4
    hidden, *partial = grads(
        split, index, one_weights, gain, part, edge, peer, peer_edge, side, cot, back_out
    )
    encoded = encode(code_weights, hidden).transpose(1, 0, 2)

    if split:
        keep, give = partial
        mine, *others = quarters(index, keep, swap_sub(give), n_tile)
        for k, other in enumerate(others, 1):
            mine = mine + swap_tile(other, n_tile, k).astype(F32)
        mine, encoded = lax.optimization_barrier((mine.astype(BF16), encoded))
        mine = jnp.stack([mine] + [swap_tile(mine, n_tile, k) for k in range(1, n_tile)])
        grad_two, grad_one, grad_gain = finish(index, mine, swap_sub(mine), scale, own, chans)
        return encoded, grad_one.transpose(0, 1, 3, 2), grad_two, grad_gain[0]

    total = lax.psum(partial[0], ("tile", "sub")) * scale
    three = 3 * own
    half_rows = 3 * chans // 2
    lanes = 3 * n_hidden
    grad_two = total[:three].reshape(3, own, 3, n_hidden).transpose(0, 2, 1, 3)
    lines = total[three : three + half_rows]
    lines = jnp.concatenate([lines[:, :three], lines[:, lanes // 2 : lanes // 2 + three]], axis=0)
    grad_one = lines.reshape(3, chans, 3, own).transpose(2, 0, 3, 1)
    grad_gain = total[three + half_rows, own : 2 * own]
    return encoded, grad_one, grad_two, grad_gain


def solution(mesh):
    placed = (
        P(("member", "tile", "chan", "sub"), None),
        P(("member", "tile", "chan", "sub")),
        P(("member", "tile", "chan", "sub")),
        P(("member", "tile", "chan", "sub")),
        P(None, None, "chan", None),
        P(None, None, "chan", None),
        P("chan"),
        P(("member", "chan"), "tile", "sub"),
    )
    return jax.shard_map(
        body,
        mesh=mesh,
        in_specs=placed,
        out_specs=(
            P(("member", "chan"), "tile", "sub"),
            P("member", None, "chan", None),
            P("member", None, "chan", None),
            P(("member", "chan")),
        ),
        check_vma=False,
    )
```

```python
import functools
import math

import jax
import jax.numpy as jnp
from jax import lax
from jax.experimental import pallas as pl
from jax.experimental.pallas import tpu as pltpu
from jax.sharding import PartitionSpec as P

BF16 = jnp.bfloat16
F32 = jnp.float32
LANES = 128
BLOCK = 256
META = 8
MIB = 1024 * 1024


def dot_nt(a, b):
    return lax.dot_general(a, b, (((1,), (1,)), ((), ())), preferred_element_type=F32)


def dot_nn(a, b):
    return lax.dot_general(a, b, (((1,), (0,)), ((), ())), preferred_element_type=F32)


def iota(shape, dim, dtype=jnp.int32):
    return lax.broadcasted_iota(jnp.int32, shape, dim).astype(dtype)


def vmem_spec():
    return pl.BlockSpec(memory_space=pltpu.VMEM)


def smem_spec():
    return pl.BlockSpec(memory_space=pltpu.SMEM)


def call(kernel, out_shape, in_specs, scratch, flops, moved, name, vmem=32):
    n_out = len(out_shape) if isinstance(out_shape, (tuple, list)) else None
    out_specs = vmem_spec() if n_out is None else [vmem_spec() for _ in range(n_out)]
    return pl.pallas_call(
        kernel,
        out_shape=out_shape,
        in_specs=in_specs,
        out_specs=out_specs,
        scratch_shapes=scratch,
        compiler_params=pltpu.CompilerParams(vmem_limit_bytes=vmem * MIB),
        cost_estimate=pl.CostEstimate(flops=flops, bytes_accessed=moved, transcendentals=0),
        name=name,
    )


def route_kernel(n_tiles, cap, relative, index_ref, tile_hbm, weight_hbm, cell_hbm, values_hbm, *rest):
    n_outs = 5 if relative else 1
    outs = rest[:n_outs]
    (tile_ref, weight_ref, cell_ref, values_ref, onehot_ref, slot_ref, weight32_ref, all_ref,
     info_ref, info_smem, sems) = rest[n_outs:]
    loads = [
        pltpu.make_async_copy(tile_hbm, tile_ref, sems.at[0]),
        pltpu.make_async_copy(weight_hbm, weight_ref, sems.at[1]),
        pltpu.make_async_copy(cell_hbm, cell_ref, sems.at[2]),
        pltpu.make_async_copy(values_hbm, values_ref, sems.at[3]),
    ]
    for load in loads:
        load.start()
    all_ref[...] = jnp.zeros(all_ref.shape, BF16)
    loads[0].wait()
    n_lines = tile_ref.shape[0]
    n_blocks = n_lines // 2
    n_obs_chans = values_ref.shape[0]
    pairs = n_tiles * n_lines
    tiles = tile_ref[...]
    for t in range(n_tiles):
        onehot_ref[t * n_lines : (t + 1) * n_lines, :] = jnp.where(tiles == t, 1.0, 0.0).astype(BF16)
    onehot = onehot_ref[...]
    upper = jnp.where(
        iota((LANES, LANES), 0) <= iota((LANES, LANES), 1), 1.0, 0.0
    ).astype(BF16)
    here = iota((pairs, pairs), 0)
    there = iota((pairs, pairs), 1)
    earlier = jnp.where(
        (here // n_lines == there // n_lines) & (there < here), 1.0, 0.0
    ).astype(BF16)
    total_row = dot_nt(jnp.ones((8, LANES), BF16), onehot)
    offset_row = dot_nt(total_row.astype(BF16), earlier)
    odd = iota((8, pairs), 1) % 2 == 1
    both = jnp.where(odd, total_row + pltpu.roll(total_row, 1, 1), 0.0)
    spill = jnp.where(jnp.max(both, axis=1, keepdims=True) > LANES, 1.0, 0.0)
    info_ref[...] = jnp.where(
        iota((8, pairs), 0) == 0, offset_row, spill
    ).astype(jnp.int32)
    copy = pltpu.make_async_copy(info_ref, info_smem, sems.at[4])
    copy.start()
    cum = dot_nn(onehot, upper)
    totals = dot_nn(onehot, jnp.ones((LANES, LANES), BF16))
    offset = dot_nn(earlier, totals.astype(BF16))
    place = cum + offset - 1.0
    slots = jnp.zeros(tiles.shape, F32)
    for t in range(n_tiles):
        slots = jnp.where(tiles == t, place[t * n_lines : (t + 1) * n_lines, :], slots)
    slot_ref[...] = slots
    for load in loads[1:]:
        load.wait()
    weight32_ref[...] = weight_ref[...].astype(F32)
    meta_row = iota((16, BLOCK), 0)
    window = iota((LANES, BLOCK), 0, F32)
    blank = jnp.zeros((n_obs_chans + 16, LANES), F32)
    copy.wait()

    def line(ref, b):
        return jnp.concatenate([ref[pl.ds(2 * b, 1), :], ref[pl.ds(2 * b + 1, 1), :]], axis=1)

    def columns(b):
        values = values_ref[:, pl.ds(pl.multiple_of(b * BLOCK, BLOCK), BLOCK)]
        cell = line(cell_ref, b)
        weight = line(weight32_ref, b)
        high = (cell // LANES).astype(F32)
        low = (cell % LANES).astype(F32)
        meta = jnp.where(
            meta_row == 0,
            weight,
            jnp.where(meta_row == 1, high, jnp.where(meta_row == 2, low, 0.0)),
        ).astype(BF16)
        return jnp.concatenate([values, meta], axis=0)

    def add(t, wide, tile, slot, start):
        key = jnp.where(tile == t, slot - start.astype(F32), -1.0)
        chosen = jnp.where(window == key, 1.0, 0.0).astype(BF16)
        part = jnp.concatenate([dot_nt(wide, chosen), blank], axis=1)
        base = jnp.minimum(start // LANES * LANES, cap - BLOCK)
        turn = jnp.bitwise_and(start - base, BLOCK - 1)
        part = pltpu.roll(part, turn, 1)[: n_obs_chans + META].astype(BF16)
        where = pl.ds(pl.multiple_of(base, LANES), BLOCK)
        all_ref[t, :, where] = all_ref[t, :, where] + part

    def place_block(b, skip):
        wide = columns(b)
        tile = line(tile_ref, b)
        slot = line(slot_ref, b)
        for t in range(n_tiles):
            add(t, wide, tile, slot, info_smem[0, t * n_lines + 2 * b] + skip)

    def first_some(i, carry):
        for j in range(n_blocks):
            place_block(n_blocks * i + j, 0)
        return carry

    lax.fori_loop(0, 1, first_some, 0)

    @pl.when(info_smem[1, 0] > 0)
    def _():
        def rest_of(b, carry):
            place_block(b, LANES)
            return carry

        lax.fori_loop(0, n_blocks, rest_of, 0)

    if relative:
        me = index_ref[4]
        outs[0][0] = all_ref[me]
        outs[1][0] = all_ref[jnp.bitwise_xor(me, 1)]
        for k in range(1, 4):
            for s in range(2):
                outs[k + 1][s] = all_ref[jnp.bitwise_xor(me, 2 * k + s)]
    else:
        outs[0][...] = all_ref[...]


def route(index, obs_values, obs_weight, obs_tile, obs_cell, n_tiles, cap, relative):
    n_obs, chans = obs_values.shape
    n_lines = n_obs // LANES
    rows = chans + META
    outs = [(n, rows, cap) for n in ((1, 1, 2, 2, 2) if relative else (n_tiles,))]
    hbm_spec = pl.BlockSpec(memory_space=pltpu.HBM)
    return call(
        functools.partial(route_kernel, n_tiles, cap, relative),
        [jax.ShapeDtypeStruct(shape, BF16) for shape in outs],
        [smem_spec()] + [hbm_spec] * 4,
        [
            pltpu.VMEM((n_lines, LANES), jnp.int32),
            pltpu.VMEM((n_lines, LANES), BF16),
            pltpu.VMEM((n_lines, LANES), jnp.int32),
            pltpu.VMEM((chans, n_obs), BF16),
            pltpu.VMEM((n_tiles * n_lines, LANES), BF16),
            pltpu.VMEM((n_lines, LANES), F32),
            pltpu.VMEM((n_lines, LANES), F32),
            pltpu.VMEM((n_tiles, rows, cap), BF16),
            pltpu.VMEM((8, n_tiles * n_lines), jnp.int32),
            pltpu.SMEM((8, n_tiles * n_lines), jnp.int32),
            pltpu.SemaphoreType.DMA((5,)),
        ],
        2 * n_obs * n_tiles * BLOCK * 80,
        n_tiles * rows * cap * 2,
        "route",
    )(
        index,
        obs_tile.reshape(n_lines, LANES),
        obs_weight.reshape(n_lines, LANES),
        obs_cell.reshape(n_lines, LANES),
        obs_values.T,
    )


def grid_kernel(n_rows, n_cols, group, takes, first, last, *rest):
    rest = list(rest)
    got_refs = [rest.pop(0) for _ in takes]
    senders = [ref.at[i] for ref, picked in zip(got_refs, takes) for i in picked]
    before_ref = None if first else rest.pop(0)
    own_ref = rest.pop(0)
    send_refs = [rest.pop(0) for _ in range(3)] if last else None
    left_ref, right_ref = rest
    n_send = len(senders)
    rows, cap = senders[0].shape
    chans = rows - META
    data = n_rows * chans
    per_row = n_cols // LANES
    columns = iota((n_cols, cap), 0, F32)
    row_ids = iota((2 * n_rows, cap), 0, F32)
    total = None
    for g in range(n_send // group):
        slot = g % 2
        for i in range(group):
            sender = senders[g * group + i]
            at = slice(i * cap, (i + 1) * cap)
            values = sender[0:chans, :]
            meta = sender[chans:rows, :].astype(F32)
            weight = meta[0:1]
            high = meta[1:2]
            row = jnp.floor((high + 0.5) * (1.0 / per_row))
            column = (high - row * per_row) * LANES + meta[2:3]
            right_ref[slot, :, at] = jnp.where(columns == column, weight, 0.0).astype(BF16)
            in_row = jnp.where(row_ids == row, 1.0, 0.0)
            for r in range(n_rows):
                left_ref[slot, r * chans : (r + 1) * chans, at] = values * in_row[r : r + 1].astype(BF16)
            left_ref[slot, data:, at] = in_row.astype(BF16)
        part = dot_nt(left_ref[slot], right_ref[slot])
        total = part if total is None else total + part
    if before_ref is not None:
        total = total + before_ref[...]
    own_ref[...] = total
    if last:
        send_ref, low_ref, high_ref = send_refs
        density = own_ref[data : data + n_rows, :]
        high = density.astype(BF16).astype(F32)
        low = density - high
        send_ref[0:data, :] = own_ref[0:data, :].astype(BF16)
        send_ref[data:, :] = jnp.concatenate([high, low], axis=0).astype(BF16)
        for ref, at in ((high_ref, 0), (low_ref, n_rows - 2)):
            ref[0 : 2 * chans, :] = own_ref[at * chans : (at + 2) * chans, :].astype(BF16)
            ref[2 * chans :, :] = jnp.concatenate(
                [high[at : at + 2], low[at : at + 2], jnp.zeros((4, n_cols), F32)], axis=0
            ).astype(BF16)


def grid(got, before, last, n_rows, n_cols):
    takes = [picked for _, picked in got]
    got = [x for x, _ in got]
    n_send = sum(len(picked) for picked in takes)
    rows, cap = got[0].shape[1:]
    group = max(1, min(2048 // cap, n_send))
    chans = rows - META
    total = n_rows * chans + 2 * n_rows
    outs = [jax.ShapeDtypeStruct((total, n_cols), F32)]
    if last:
        outs.append(jax.ShapeDtypeStruct((total, n_cols), BF16))
        outs += [jax.ShapeDtypeStruct((2 * chans + 8, n_cols), BF16)] * 2
    ins = list(got) if before is None else list(got) + [before]
    return call(
        functools.partial(grid_kernel, n_rows, n_cols, group, takes, before is None, last),
        outs,
        [vmem_spec()] * len(ins),
        [
            pltpu.VMEM((2, total, group * cap), BF16),
            pltpu.VMEM((2, n_cols, group * cap), BF16),
        ],
        2 * n_send * cap * total * n_cols,
        n_send * rows * cap * 2,
        "grid_last" if last else "grid_part",
    )(*ins)


def lane_mask(shape, n_cols, sub, depth):
    lane = iota(shape, 1)
    width = n_cols + LANES
    keep_right = (lane >= n_cols) & (lane < n_cols + depth) & (sub == 0)
    keep_left = (lane >= width - depth) & (sub == 1)
    return (lane < n_cols) | keep_right | keep_left


def back_kernel(n_cols, n_pieces, index_ref, kernel_ref, *rest):
    pieces = [(rest[2 * i], rest[2 * i + 1]) for i in range(n_pieces)]
    side_ref, out_ref, wide_ref = rest[2 * n_pieces :]
    n_ext, all_chans = side_ref.shape[0], side_ref.shape[1]
    n_rows = n_ext - 2
    width = n_cols + LANES
    keep = lane_mask((1, width), n_cols, index_ref[2], 1)
    for h in range(n_ext):
        if h == 0 or h == n_ext - 1:
            mids = [edge[min(h, 1)] for _, edge in pieces]
        else:
            mids = [middle[h - 1] for middle, _ in pieces]
        mid = mids[0] if n_pieces == 1 else jnp.concatenate(mids, axis=0)
        ext = jnp.concatenate([mid, side_ref[h]], axis=1).astype(F32)
        ext = jnp.where(keep, ext, 0.0)
        at = slice(h * n_cols, (h + 1) * n_cols)
        wide_ref[0:all_chans, at] = pltpu.roll(ext, width - 1, 1)[:, :n_cols].astype(BF16)
        wide_ref[all_chans : 2 * all_chans, at] = mid
        wide_ref[2 * all_chans :, at] = pltpu.roll(ext, 1, 1)[:, :n_cols].astype(BF16)
    total = None
    for a in range(3):
        at = slice((2 - a) * n_cols, (2 - a + n_rows) * n_cols)
        part = dot_nn(kernel_ref[a], wide_ref[:, at])
        total = part if total is None else total + part
    out_ref[...] = total


def back(index, kernel, pieces, side, n_cols):
    n_ext, all_chans = side.shape[0], side.shape[1]
    n_out = kernel.shape[1]
    return call(
        functools.partial(back_kernel, n_cols, len(pieces)),
        jax.ShapeDtypeStruct((n_out, (n_ext - 2) * n_cols), F32),
        [smem_spec()] + [vmem_spec()] * (2 + 2 * len(pieces)),
        [pltpu.VMEM((3 * all_chans, n_ext * n_cols), BF16)],
        2 * n_ext * 9 * all_chans * n_out * n_cols,
        n_ext * all_chans * n_cols * 2,
        "back",
    )(index, kernel, *[x for piece in pieces for x in piece], side)


def grads_kernel(
    split, chans, index_ref, kernel_ref, gain_ref, own_ref, edge_ref, peer_ref, peer_edge_ref,
    side_ref, cot_ref, back_ref, hidden_ref, *rest,
):
    rest = list(rest)
    if split:
        keep_out, give_out = rest.pop(0), rest.pop(0)
    else:
        all_out = rest.pop(0)
    taps_ref, logs_ref, wide_ref, out_left_ref, pre_left_ref, acc_ref = rest
    n_rows, own, n_cols = cot_ref.shape
    n_hidden = kernel_ref.shape[1]
    taps_rows = 3 * chans
    width = n_cols + LANES
    tile, chan, sub, n_tile = index_ref[0], index_ref[1], index_ref[2], index_ref[3]
    keep_two = lane_mask((1, width), n_cols, sub, 2)

    log_line = iota((16, width), 0)
    data = n_rows * chans
    middle_rows = data + 2 * n_rows
    edge_rows = 2 * chans + 8
    side_half = middle_rows + 2 * edge_rows
    lefts = [(own_ref, edge_ref)] + ([] if peer_ref is None else [(peer_ref, peer_edge_ref)])
    sources = []
    for i in range(n_rows + 4):
        found = []
        for p, (middle_ref, ends_ref) in enumerate(lefts):
            if 2 <= i < n_rows + 2:
                r = i - 2
                base, lines = r * chans, (data + r, data + n_rows + r)
                found.append((middle_ref, base, lines, p * side_half))
            else:
                e = i if i < 2 else i - n_rows
                start = e // 2 * edge_rows
                base = start + e % 2 * chans
                lines = (start + 2 * chans + e % 2, start + 2 * chans + 2 + e % 2)
                found.append((ends_ref, base, lines, p * side_half + middle_rows))
        sources.append(found)

    def gather(found, wanted):
        total = None
        for ref, base, lines, at in found:
            for line in [base] if wanted == chans else lines:
                ext = jnp.concatenate(
                    [
                        ref[line : line + wanted, :].astype(F32),
                        side_ref[at + line : at + line + wanted, :].astype(F32),
                    ],
                    axis=1,
                )
                total = ext if total is None else total + ext
        return total

    for i in range(n_rows + 4):
        ext = gather(sources[i], chans)
        density = gather(sources[i], 1)
        logs = jnp.log(1.0 + density)
        logs_ref[i] = logs
        shrink = jnp.where(keep_two, 1.0 / (1.0 + density), 0.0)
        feats = ext * shrink
        at = slice(i * width, (i + 1) * width)
        taps_ref[0:chans, at] = pltpu.roll(feats, 1, 1).astype(BF16)
        taps_ref[chans : 2 * chans, at] = feats.astype(BF16)
        taps_ref[2 * chans : taps_rows, at] = pltpu.roll(feats, width - 1, 1).astype(BF16)
        high = logs.astype(BF16).astype(F32)
        middle = (logs - high).astype(BF16).astype(F32)
        taps_ref[taps_rows:, at] = jnp.where(
            log_line == 0,
            high,
            jnp.where(log_line == 1, middle, jnp.where(log_line == 2, logs - high - middle, 0.0)),
        ).astype(BF16)

    nothing = jnp.zeros((own, n_cols), BF16)
    for h in range(n_rows + 2):
        for a in range(3):
            inside = 0 <= h - a < n_rows
            put = slice(a * own, (a + 1) * own)
            out_left_ref[put, h * n_cols : (h + 1) * n_cols] = cot_ref[h - a] if inside else nothing
            if not inside:
                pre_left_ref[put, h * width : h * width + n_cols] = nothing
        pre_left_ref[:, h * width + n_cols : (h + 1) * width] = jnp.zeros((3 * own, LANES), BF16)

    gain = gain_ref[:, 0:1]
    keep_one = lane_mask((1, width), n_cols, sub, 1)
    group = 1
    for first in range(0, n_rows + 2, group):
        pre_all = None
        for a in range(3):
            at = slice((first + a) * width, (first + a + group) * width)
            part = dot_nn(kernel_ref[a], taps_ref[0:taps_rows, at])
            pre_all = part if pre_all is None else pre_all + part
        for k in range(group):
            h = first + k
            pre = pre_all[:, k * width : (k + 1) * width] + gain * logs_ref[h + 1]
            at = slice(h * n_cols, (h + 1) * n_cols)
            keep = keep_one
            if h == 0:
                keep = keep & (tile > 0)
            elif h == n_rows + 1:
                keep = keep & (tile < n_tile - 1)
            else:
                mine = pre[0:own, :n_cols]
                for c in range(1, n_hidden // own):
                    mine = jnp.where(chan == c, pre[c * own : (c + 1) * own, :n_cols], mine)
                s = 0.5 + 0.5 * jnp.tanh(0.5 * mine)
                there = slice((h - 1) * n_cols, h * n_cols)
                grad = (back_ref[:, there] * s * (1.0 + mine * (1.0 - s))).astype(BF16)
                for a in range(3):
                    put = (h - 1 + a) * width
                    pre_left_ref[a * own : (a + 1) * own, put : put + n_cols] = grad
            half = 0.5 * pre
            hidden = jnp.where(keep, half + half * jnp.tanh(half), 0.0)
            hidden_ref[h] = hidden.astype(BF16)
            wide_ref[0:n_hidden, at] = pltpu.roll(hidden, 1, 1)[:, :n_cols].astype(BF16)
            wide_ref[n_hidden : 2 * n_hidden, at] = hidden[:, :n_cols].astype(BF16)
            wide_ref[2 * n_hidden :, at] = pltpu.roll(hidden, width - 1, 1)[:, :n_cols].astype(BF16)

    three = 3 * own
    lanes = 3 * n_hidden
    half_rows = taps_rows // 2
    acc_ref[0:three, :] = dot_nt(out_left_ref[...], wide_ref[...])
    one = dot_nt(taps_ref[:, width : (n_rows + 3) * width], pre_left_ref[...])
    acc_ref[three:, :] = jnp.zeros((acc_ref.shape[0] - three, lanes), F32)
    acc_ref[three : three + half_rows, 0:three] = one[0:half_rows]
    acc_ref[three : three + half_rows, lanes // 2 : lanes // 2 + three] = one[half_rows:taps_rows]
    gains = one[taps_rows : taps_rows + 1] + one[taps_rows + 1 : taps_rows + 2] + one[taps_rows + 2 : taps_rows + 3]
    acc_ref[three + half_rows : three + half_rows + 1, 0:three] = gains
    if split:
        half = acc_ref.shape[0] // 2
        keep_out[...] = acc_ref[pl.ds(pl.multiple_of(sub * half, half), half), :]
        give_out[...] = acc_ref[pl.ds(pl.multiple_of((1 - sub) * half, half), half), :].astype(BF16)
    else:
        all_out[...] = acc_ref[...]


def grads(split, index, kernel, gain, own, edge, peer, peer_edge, side, cot, back_out):
    n_rows, n_own, n_cols = cot.shape
    n_hidden = kernel.shape[1]
    chans = kernel.shape[2] // 3
    width = n_cols + LANES
    lanes = 3 * n_hidden
    acc_rows = 3 * n_own + 3 * chans // 2 + 32
    body = functools.partial(grads_kernel, split, chans)
    ins = [own, edge, peer, peer_edge, side, cot, back_out]
    if peer is None:
        ins = [own, edge, side, cot, back_out]
        body = lambda i, k, g, o, e, *rest: grads_kernel(split, chans, i, k, g, o, e, None, None, *rest)
    outs = [jax.ShapeDtypeStruct((n_rows + 2, n_hidden, width), BF16)]
    if split:
        outs.append(jax.ShapeDtypeStruct((acc_rows // 2, lanes), F32))
        outs.append(jax.ShapeDtypeStruct((acc_rows // 2, lanes), BF16))
    else:
        outs.append(jax.ShapeDtypeStruct((acc_rows, lanes), F32))
    return call(
        body,
        outs,
        [smem_spec()] + [vmem_spec()] * (2 + len(ins)),
        [
            pltpu.VMEM((3 * chans + 16, (n_rows + 4) * width), BF16),
            pltpu.VMEM((n_rows + 4, 1, width), F32),
            pltpu.VMEM((3 * n_hidden, (n_rows + 2) * n_cols), BF16),
            pltpu.VMEM((3 * n_own, (n_rows + 2) * n_cols), BF16),
            pltpu.VMEM((3 * n_own, (n_rows + 2) * width), BF16),
            pltpu.VMEM((acc_rows, lanes), F32),
        ],
        2 * (n_rows + 2) * 9 * n_cols * n_hidden * (n_own + chans),
        (n_rows + 2) * 3 * n_hidden * n_cols * 2,
        "grads",
    )(index, kernel, gain, *ins)


def encode_kernel(kernel_ref, hidden_ref, out_ref, wide_ref):
    n_ext, n_hidden, width = hidden_ref.shape
    n_rows = n_ext - 2
    n_cols = width - LANES
    for h in range(n_ext):
        hidden = hidden_ref[h].astype(F32)
        at = slice(h * n_cols, (h + 1) * n_cols)
        wide_ref[0:n_hidden, at] = pltpu.roll(hidden, 1, 1)[:, :n_cols].astype(BF16)
        wide_ref[n_hidden : 2 * n_hidden, at] = hidden_ref[h, :, 0:n_cols]
        wide_ref[2 * n_hidden :, at] = pltpu.roll(hidden, width - 1, 1)[:, :n_cols].astype(BF16)
    total = None
    for a in range(3):
        part = dot_nn(kernel_ref[a], wide_ref[:, a * n_cols : (a + n_rows) * n_cols])
        total = part if total is None else total + part
    for r in range(n_rows):
        out_ref[r] = total[:, r * n_cols : (r + 1) * n_cols].astype(BF16)


def encode(kernel, hidden):
    n_ext, n_hidden, width = hidden.shape
    own = kernel.shape[1]
    n_cols = width - LANES
    return call(
        encode_kernel,
        jax.ShapeDtypeStruct((n_ext - 2, own, n_cols), BF16),
        [vmem_spec()] * 2,
        [pltpu.VMEM((3 * n_hidden, n_ext * n_cols), BF16)],
        2 * n_ext * 9 * own * n_hidden * n_cols,
        hidden.size * 2,
        "encode",
    )(kernel, hidden)


def quarters_kernel(index_ref, keep_ref, got_ref, *outs):
    n = len(outs)
    rows = keep_ref.shape[0] // n
    for k in range(n):
        other = jnp.bitwise_xor(index_ref[0], k)
        at = pl.ds(pl.multiple_of(other * rows, rows), rows)
        outs[k][...] = (keep_ref[at, :] + got_ref[at, :].astype(F32)).astype(outs[k].dtype)


def quarters(index, keep, got, n):
    rows, lanes = keep.shape
    return call(
        quarters_kernel,
        [jax.ShapeDtypeStruct((rows // n, lanes), F32 if k == 0 else BF16) for k in range(n)],
        [smem_spec(), vmem_spec(), vmem_spec()],
        [],
        rows * lanes,
        rows * lanes * 8,
        "quarters",
    )(index, keep, got)


def finish_kernel(scale, own, chans, index_ref, mine_ref, other_ref, two_ref, one_ref, gain_ref, all_ref):
    n, rows, lanes = mine_ref.shape
    n_hidden = lanes // 3
    tile, sub = index_ref[0], index_ref[2]
    for k in range(n):
        at = jnp.bitwise_xor(tile, k) * rows
        here = pl.multiple_of(sub * (n * rows) + at, rows)
        there = pl.multiple_of((1 - sub) * (n * rows) + at, rows)
        all_ref[pl.ds(here, rows), :] = mine_ref[k].astype(F32) * scale
        all_ref[pl.ds(there, rows), :] = other_ref[k].astype(F32) * scale
    half_rows = 3 * chans // 2
    for a in range(3):
        for b in range(3):
            two_ref[a, b] = all_ref[a * own : (a + 1) * own, b * n_hidden : (b + 1) * n_hidden]
        lines = jnp.concatenate(
            [
                all_ref[3 * own : 3 * own + half_rows, s + a * own : s + (a + 1) * own]
                for s in (0, lanes // 2)
            ],
            axis=0,
        )
        for b in range(3):
            one_ref[a, b] = lines[b * chans : (b + 1) * chans]
    gain_ref[...] = all_ref[3 * own + half_rows : 3 * own + half_rows + 1, own : 2 * own]


def finish(index, mine, other, scale, own, chans):
    n, rows, lanes = mine.shape
    n_hidden = lanes // 3
    return call(
        functools.partial(finish_kernel, scale, own, chans),
        [
            jax.ShapeDtypeStruct((3, 3, own, n_hidden), F32),
            jax.ShapeDtypeStruct((3, 3, chans, own), F32),
            jax.ShapeDtypeStruct((1, own), F32),
        ],
        [smem_spec(), vmem_spec(), vmem_spec()],
        [pltpu.VMEM((2 * n * rows, lanes), F32)],
        n * rows * lanes,
        n * rows * lanes * 12,
        "finish",
    )(index, mine, other)


def offer_kernel(index_ref, two_ref, one_ref, gain_ref, out_ref):
    own = two_ref.shape[2]
    chans = one_ref.shape[2]
    at = pl.ds(pl.multiple_of((1 - index_ref[1]) * own, own), own)
    gain = gain_ref[...]
    high = gain.astype(BF16).astype(F32)
    middle = (gain - high).astype(BF16).astype(F32)
    line = iota((8, own), 0)
    terms = jnp.where(
        line == 0, high, jnp.where(line == 1, middle, jnp.where(line == 2, gain - high - middle, 0.0))
    ).astype(BF16)
    for a in range(3):
        for b in range(3):
            out_ref[a, b, 0:own] = two_ref[a, b, :, at]
            out_ref[a, b, own : own + chans] = one_ref[a, b]
            out_ref[a, b, own + chans :] = terms


def offer(index, two, one, gain):
    own, chans = two.shape[2], one.shape[2]
    return call(
        offer_kernel,
        jax.ShapeDtypeStruct((3, 3, own + chans + 8, own), BF16),
        [smem_spec()] + [vmem_spec()] * 3,
        [],
        9 * own * (own + chans),
        9 * own * (own + chans) * 4,
        "offer",
    )(index, two, one, gain[None])


def arrange_kernel(index_ref, two_ref, one_ref, gain_ref, theirs_ref, back_ref, code_ref, first_ref, column_ref):
    own = two_ref.shape[2]
    chans = one_ref.shape[2]
    chan = index_ref[1]
    mine = pl.ds(pl.multiple_of(chan * own, own), own)
    peer = pl.ds(pl.multiple_of((1 - chan) * own, own), own)

    def turned(block):
        return block.astype(F32).T.astype(BF16)

    for a in range(3):
        for b in range(3):
            left = b * 2 * own
            back_ref[a, :, left : left + own] = turned(two_ref[a, b, :, mine])
            back_ref[a, :, left + own : left + 2 * own] = turned(theirs_ref[a, b, 0:own])
            code_ref[a, :, left : left + 2 * own] = two_ref[a, b]
        first_ref[a, mine, :] = turned(jnp.concatenate([one_ref[a, b] for b in range(3)], axis=0))
        first_ref[a, peer, :] = turned(
            jnp.concatenate([theirs_ref[a, b, own : own + chans] for b in range(3)], axis=0)
        )
    terms = theirs_ref[0, 0, own + chans :].astype(F32)
    other = terms[0:1] + terms[1:2] + terms[2:3]
    column_ref[mine, :] = jnp.broadcast_to(gain_ref[...], (own, own)).T
    column_ref[peer, :] = jnp.broadcast_to(other, (own, own)).T


def arrange(index, two, one, gain, theirs):
    own, chans = two.shape[2], one.shape[2]
    return call(
        arrange_kernel,
        [
            jax.ShapeDtypeStruct((3, own, 6 * own), BF16),
            jax.ShapeDtypeStruct((3, own, 6 * own), BF16),
            jax.ShapeDtypeStruct((3, 2 * own, 3 * chans), BF16),
            jax.ShapeDtypeStruct((2 * own, LANES), F32),
        ],
        [smem_spec()] + [vmem_spec()] * 4,
        [],
        9 * own * (4 * own + 2 * chans),
        9 * own * (4 * own + 2 * chans) * 4,
        "arrange",
    )(index, two, one, gain[None], theirs)


def step_perm(count, by):
    return [(i, i + by) for i in range(count) if 0 <= i + by < count]


def swap_sub(x):
    return lax.ppermute(x, "sub", [(0, 1), (1, 0)])


def swap_chan(x):
    return lax.ppermute(x, "chan", [(0, 1), (1, 0)])


def swap_tile(x, n_tile, k):
    return lax.ppermute(x, "tile", [(i, i ^ k) for i in range(n_tile)])


def near(block, sub):
    n_cols = block.shape[-1]
    return jnp.where(sub == 0, block[..., n_cols - LANES :], block[..., :LANES])


def side_rows(parts, sub):
    columns = [
        jnp.concatenate([near(edge[: edge.shape[0] // 2], sub), near(mid, sub), near(edge[edge.shape[0] // 2 :], sub)], axis=0)
        for mid, edge in parts
    ]
    both = columns[0] if len(columns) == 1 else jnp.concatenate(columns, axis=1)
    return swap_sub(both)


def body(obs_values, obs_weight, obs_tile, obs_cell, conv_one, conv_two, density_gain, cotangent):
    own, n_rows, n_cols = cotangent.shape
    n_tile = lax.axis_size("tile")
    n_sub = lax.axis_size("sub")
    n_chan = lax.axis_size("chan")
    pair = n_chan == 2 and own == LANES
    n_tiles = n_tile * n_sub
    chans = obs_values.shape[1]
    n_hidden = own * n_chan
    cap = 2 * obs_values.shape[0] // n_tiles
    tile, chan, sub = lax.axis_index("tile"), lax.axis_index("chan"), lax.axis_index("sub")
    index = jnp.stack([tile, chan, sub, jnp.int32(n_tile), tile * n_sub + sub]).astype(jnp.int32)

    bottom, top = cotangent[:, -1], cotangent[:, 0]
    one_own = conv_one.transpose(0, 1, 3, 2)
    if pair:
        offered = offer(index, conv_two, one_own, density_gain)
        obs_tile, bottom, top, offered = lax.optimization_barrier((obs_tile, bottom, top, offered))
        theirs = swap_chan(offered)
    low = lax.ppermute(bottom, "tile", step_perm(n_tile, 1))
    high = lax.ppermute(top, "tile", step_perm(n_tile, -1))

    few = n_tiles == 8
    sent = route(index, obs_values, obs_weight, obs_tile, obs_cell, n_tiles, cap, few)
    if pair:
        sent, low, high, theirs = lax.optimization_barrier((sent, low, high, theirs))
    if few:
        far = [swap_tile(sent[k + 1], n_tile, k) for k in (1, 2, 3)]
        near_side = swap_sub(jnp.concatenate([sent[1], far[0][1:]], axis=0))
        steps = [
            [(sent[0], (0,)), (far[0], (0,)), (near_side, (0, 1))],
            [(far[1], (0,)), (far[2], (0,))],
            [(swap_sub(far[1][1:]), (0,)), (swap_sub(far[2][1:]), (0,))],
        ]
    else:
        got = lax.all_to_all(sent[0], ("tile", "sub"), split_axis=0, concat_axis=0, tiled=True)
        steps = [[(got, tuple(range(n_tiles)))]]

    if pair:
        cotangent, _ = lax.optimization_barrier((cotangent, sent[0]))
        cot = cotangent.transpose(1, 0, 2)
        cot_edge = jnp.stack([low, high])
        cot_peer = swap_chan(cotangent)
        pieces = [(cot, cot_edge), (cot_peer.transpose(1, 0, 2), swap_chan(cot_edge))]
    else:
        cot = cotangent.transpose(1, 0, 2)
        pieces = [
            (
                lax.all_gather(cot, "chan", axis=1, tiled=True),
                lax.all_gather(jnp.stack([low, high]), "chan", axis=1, tiled=True),
            )
        ]
    cot_side = side_rows(pieces, sub)

    if pair:
        back_weights, code_weights, one_weights, gain = arrange(
            index, conv_two, one_own, density_gain, theirs
        )
    else:
        columns = lax.all_to_all(conv_two, "chan", split_axis=3, concat_axis=2, tiled=True)
        one_full = lax.all_gather(one_own, "chan", axis=3, tiled=True)
        gain = lax.all_gather(density_gain, "chan", axis=0, tiled=True)
        gain = jnp.broadcast_to(gain[:, None], (n_hidden, LANES))
        code_weights = conv_two.transpose(0, 2, 1, 3).reshape(3, own, 3 * n_hidden)
        back_weights = columns.transpose(0, 3, 1, 2).reshape(3, own, 3 * n_hidden)
        one_weights = one_full.transpose(0, 3, 1, 2).reshape(3, n_hidden, 3 * chans)

    part = None
    for step in steps[:-1]:
        part = grid(step, part, False, n_rows, n_cols)[0]
    if few:
        part, back_weights, one_weights, code_weights, gain = lax.optimization_barrier(
            (part, back_weights, one_weights, code_weights, gain)
        )
    part, message, up, down = grid(steps[-1], part, True, n_rows, n_cols)
    data = n_rows * chans
    if not pair:
        part = lax.psum(part, "chan")
        density = part[data : data + n_rows]
        dense = density.astype(BF16)
        rest = (density - dense.astype(F32)).astype(BF16)
        message = jnp.concatenate([part[:data].astype(BF16), dense, rest], axis=0)
        blank = jnp.zeros((4, n_cols), BF16)
        up, down = [
            jnp.concatenate(
                [message[r * chans : (r + 2) * chans], dense[r : r + 2], rest[r : r + 2], blank], axis=0
            )
            for r in (n_rows - 2, 0)
        ]
    low = lax.ppermute(up, "tile", step_perm(n_tile, 1))
    high = lax.ppermute(down, "tile", step_perm(n_tile, -1))
    edge = jnp.concatenate([low, high], axis=0)
    back_out = back(index, back_weights, pieces, cot_side, n_cols)
    if pair:
        peer, peer_edge = swap_chan(message), swap_chan(edge)
        peer, peer_edge, back_out = lax.optimization_barrier((peer, peer_edge, back_out))
        side = [message, edge, peer, peer_edge]
    else:
        peer, peer_edge = None, None
        side = [message, edge]
    side = swap_sub(jnp.concatenate([near(x, sub) for x in side], axis=0))

    scale = 1.0 / math.sqrt(n_tiles * n_rows * n_cols)
    split = pair and n_tile == 4
    hidden, *partial = grads(
        split, index, one_weights, gain, part, edge, peer, peer_edge, side, cot, back_out
    )
    encoded = encode(code_weights, hidden).transpose(1, 0, 2)

    if split:
        keep, give = partial
        mine, *others = quarters(index, keep, swap_sub(give), n_tile)
        for k, other in enumerate(others, 1):
            mine = mine + swap_tile(other, n_tile, k).astype(F32)
        mine, encoded = lax.optimization_barrier((mine.astype(BF16), encoded))
        mine = jnp.stack([mine] + [swap_tile(mine, n_tile, k) for k in range(1, n_tile)])
        grad_two, grad_one, grad_gain = finish(index, mine, swap_sub(mine), scale, own, chans)
        return encoded, grad_one.transpose(0, 1, 3, 2), grad_two, grad_gain[0]

    total = lax.psum(partial[0], ("tile", "sub")) * scale
    three = 3 * own
    half_rows = 3 * chans // 2
    lanes = 3 * n_hidden
    grad_two = total[:three].reshape(3, own, 3, n_hidden).transpose(0, 2, 1, 3)
    lines = total[three : three + half_rows]
    lines = jnp.concatenate([lines[:, :three], lines[:, lanes // 2 : lanes // 2 + three]], axis=0)
    grad_one = lines.reshape(3, chans, 3, own).transpose(2, 0, 3, 1)
    grad_gain = total[three + half_rows, own : 2 * own]
    return encoded, grad_one, grad_two, grad_gain


def solution(mesh):
    placed = (
        P(("member", "tile", "chan", "sub"), None),
        P(("member", "tile", "chan", "sub")),
        P(("member", "tile", "chan", "sub")),
        P(("member", "tile", "chan", "sub")),
        P(None, None, "chan", None),
        P(None, None, "chan", None),
        P("chan"),
        P(("member", "chan"), "tile", "sub"),
    )
    return jax.shard_map(
        body,
        mesh=mesh,
        in_specs=placed,
        out_specs=(
            P(("member", "chan"), "tile", "sub"),
            P("member", None, "chan", None),
            P("member", None, "chan", None),
            P(("member", "chan")),
        ),
        check_vma=False,
    )
```
